256 devices in a mesh: gx: 32 (over z, y), gy: 8 (over x, core).
Axes of the slice: x: 4, y: 4, z: 8, core: 2. Of those that a mesh axis runs over, the one named last changes fastest.
Arguments:
- right_side: float32 [2, 128, 64, 384], P(None, 'gx', 'gy'), may hold values from -6 to 6
- velocity_table: float32 [16], replicated, may hold values from 2500 to 5000
- layer_index: int32 [128, 64, 384], P('gx', 'gy'), may hold values from 0 to 15
- absorb_level: int32 [128, 64, 384], P('gx', 'gy'), may hold values from 0 to 3
Outputs:
- solution_field: float32 [2, 128, 64, 384], P(None, 'gx', 'gy')
The draws below stay inside these ranges and needn't reach their ends.
All inputs are finite; a program needn't handle non-finite values.
Results may differ from the reference program's by a relative error of at most 0.0001.
Values sent between devices are 32-bit elements; how exact they have to be, the bound alone decides.
No kernel may reach another device: no remote copies, remote signals or barrier semaphores. Data moves between devices by JAX's collectives and lax.ppermute only.
A program may use at most 64 MiB of HBM per device.

```python
import math
import jax
import jax.numpy as jnp

LAYERS = 16
NU = 2
NC = 8
CYCLES = 2
NX = 128
NY = 64
NZ = 384


def place_ends(drawn, key, low, largest):
    shape = drawn.shape
    spot = [jax.random.randint(jax.random.fold_in(key, axis), (), 0, shape[axis]) for axis in range(len(shape))]
    drawn = drawn.at[tuple(spot)].set(low)
    longest = shape.index(max(shape))
    spot[longest] = (spot[longest] + 1) % shape[longest]
    return drawn.at[tuple(spot)].set(largest)


def block_levels(rng, extent, pieces, smallest, high):
    gain, own = 1.0, jax.random.fold_in(rng, 6)
    for axis_at, shards_of in pieces:
        heights = jnp.exp(jax.random.uniform(jax.random.fold_in(own, axis_at), (shards_of,), jnp.float32, smallest / len(pieces), high / len(pieces)))
        gain = gain * jnp.repeat(heights, extent[axis_at] // shards_of).reshape([-1 if axis == axis_at else 1 for axis in range(len(extent))])
    return gain


def scatter_about(own_key, shape, width, reach, shards=(), held_as=jnp.bfloat16):
    loudness = block_levels(own_key, shape, shards, -0.22, 0.18) if shards else 1.0
    entries = jax.random.normal(own_key, shape, jnp.float32) * width * loudness
    return jnp.minimum(jnp.maximum(entries, -reach), reach).astype(held_as)


def setup_inputs(seed: int = 0) -> dict:
    arg_keys = jax.random.split(jax.random.key(seed), 5)
    right_side = scatter_about(arg_keys[0], (2, NX, NY, NZ), 1.0, 6.0, ((1, 32), (2, 8)), jnp.float32)
    velocity_table = jnp.clip(jnp.exp(jax.random.uniform(arg_keys[1], (LAYERS,), jnp.float32, math.log(2500.0), math.log(5000.0))), 2500.0, 5000.0)
    layer_index = place_ends(jax.random.randint(arg_keys[2], (NX, NY, NZ), 0, LAYERS), jax.random.fold_in(arg_keys[2], 1), 0, LAYERS - 1).astype(jnp.int32)
    absorb_level = place_ends(jax.random.randint(arg_keys[3], (NX, NY, NZ), 0, 4), jax.random.fold_in(arg_keys[3], 1), 0, 3).astype(jnp.int32)
    return dict(right_side=right_side, velocity_table=velocity_table, layer_index=layer_index, absorb_level=absorb_level)


OMEGA = 0.6
BETA = 0.5
ABSORB = 0.25
KH_FACTOR = 2.0 * math.pi * 6.0 * 20.0


def complex_product(first, second):
    return jnp.stack([first[0] * second[0] - first[1] * second[1], first[0] * second[1] + first[1] * second[0]])


def neighbour_sum(padded):
    total = padded[:, 2:, 1:-1, 1:-1] + padded[:, :-2, 1:-1, 1:-1]
    total = total + padded[:, 1:-1, 2:, 1:-1] + padded[:, 1:-1, :-2, 1:-1]
    total = total + padded[:, 1:-1, 1:-1, 2:] + padded[:, 1:-1, 1:-1, :-2]
    return total


def apply_operator(field, shift_term, grid_level):
    padded = jnp.pad(field, ((0, 0), (1, 1), (1, 1), (1, 1)))
    return (6.0 * field - neighbour_sum(padded)) * (0.25 ** grid_level) - complex_product(shift_term, field)


def restrict(field):
    size_x, size_y, size_z = field.shape[1], field.shape[2], field.shape[3]
    return field.reshape(2, size_x // 2, 2, size_y // 2, 2, size_z // 2, 2).mean(axis=(2, 4, 6))


def prolong(field):
    return jnp.repeat(jnp.repeat(jnp.repeat(field, 2, 1), 2, 2), 2, 3)


def inverse_of(shift_term, grid_level):
    diag_real = 6.0 * (0.25 ** grid_level) - shift_term[0]
    diag_imag = -shift_term[1]
    denom = diag_real * diag_real + diag_imag * diag_imag
    return jnp.stack([diag_real / denom, -diag_imag / denom])


def smooth(update, source, shift_term, inverse_diag, grid_level, sweeps):
    for sweep in range(sweeps):
        update = update + OMEGA * complex_product(inverse_diag, source - apply_operator(update, shift_term, grid_level))
    return update


def vcycle(source, shifts, inverses, grid_level):
    if grid_level == 2:
        return smooth(jnp.zeros_like(source), source, shifts[2], inverses[2], 2, NC)
    update = smooth(jnp.zeros_like(source), source, shifts[grid_level], inverses[grid_level], grid_level, NU)
    residual = source - apply_operator(update, shifts[grid_level], grid_level)
    correction = vcycle(restrict(residual), shifts, inverses, grid_level + 1)
    update = update + prolong(correction)
    return smooth(update, source, shifts[grid_level], inverses[grid_level], grid_level, NU)


def reference(right_side, velocity_table, layer_index, absorb_level):
    velocity = velocity_table[layer_index]
    kh_square = (KH_FACTOR / velocity) ** 2
    damping = BETA + ABSORB * absorb_level.astype(jnp.float32)
    shift_zero = jnp.stack([kh_square, -kh_square * damping])
    shift_one = restrict(shift_zero)
    shift_two = restrict(shift_one)
    shifts = (shift_zero, shift_one, shift_two)
    inverses = (inverse_of(shift_zero, 0), inverse_of(shift_one, 1), inverse_of(shift_two, 2))
    first = vcycle(right_side, shifts, inverses, 0)
    residual = right_side - apply_operator(first, shift_zero, 0)
    for cycle_number in range(CYCLES - 1):
        first = first + vcycle(residual, shifts, inverses, 0)
        if cycle_number + 2 < CYCLES:
            residual = right_side - apply_operator(first, shift_zero, 0)
    return first
```

```python
import math

import jax
import jax.numpy as jnp
from jax import lax
from jax.experimental import pallas as pl
from jax.experimental.pallas import tpu as pltpu
from jax.sharding import PartitionSpec as P


NC = 8
OMEGA = 0.6
BETA = 0.5
ABSORB = 0.25
KH_FACTOR = 2.0 * math.pi * 6.0 * 20.0

F32 = jnp.float32
BF16 = jnp.bfloat16
VM = pl.BlockSpec(memory_space=pltpu.VMEM)
SM = pl.BlockSpec(memory_space=pltpu.SMEM)
PARAMS = pltpu.CompilerParams(vmem_limit_bytes=60 * 1024 * 1024)


def shape(*dims):
    return jax.ShapeDtypeStruct(dims, F32)


def scratch(*dims):
    return pltpu.VMEM(dims, F32)


def sort_matrix(rows, columns, flip):
    first = lax.broadcasted_iota(jnp.int32, (rows, columns), 0)
    second = lax.broadcasted_iota(jnp.int32, (rows, columns), 1)
    if flip:
        first, second = second, first
    lane = second % 128
    hit = (first == 4 * lane + second // 128) & (lane < 96)
    return jnp.where(hit, 1.0, 0.0).astype(BF16)


def exact_dot(values, matrix):
    high = values.astype(BF16)
    rest = values - high.astype(F32)
    middle = rest.astype(BF16)
    low = (rest - middle.astype(F32)).astype(BF16)
    dot = lambda part: jnp.dot(part, matrix, preferred_element_type=F32)
    return (dot(low) + dot(middle)) + dot(high)


def scaled_inverse(real, imag, scale):
    diag_real = 6.0 * scale - real
    diag_imag = -imag
    factor = OMEGA / (diag_real * diag_real + diag_imag * diag_imag)
    factor = jnp.where(real > 0.0, factor, 0.0)
    return diag_real * factor, -diag_imag * factor


def product(a, b):
    return a[0] * b[0] - a[1] * b[1], a[0] * b[1] + a[1] * b[0]


def pair_rows(value, temp):
    temp[8:32, :] = value
    row = lax.broadcasted_iota(jnp.int32, (24, 128), 0)
    return value + jnp.where(row % 2 == 0, temp[9:33, :], temp[7:31, :])


def neighbour(ref, x, c, r, count, step):
    center = lambda s: ref[x, c, s, 8:32, :]
    up = center(r + 1) if r < count - 1 else pltpu.roll(center(0), 127, 1)
    down = center(r - 1) if r > 0 else pltpu.roll(center(count - 1), 1, 1)
    total = ref[x - 1, c, r, 8:32, :] + ref[x + 1, c, r, 8:32, :]
    total = total + ref[x, c, r, 8 - step : 32 - step, :] + ref[x, c, r, 8 + step : 32 + step, :]
    return total + (up + down)


def sweep(old, new, weight, weight_at, source, source_at, low, high, count, step, scale):
    def body(x, _):
        for r in range(count):
            parts = []
            for c in range(2):
                total = neighbour(old, x, c, r, count, step)
                if scale != 1.0:
                    total = total * scale
                parts.append(source[x + source_at, c, r, 8:32, :] + total)
            w = [weight[x + weight_at, c, r, 8:32, :] for c in range(2)]
            moved = product(w, parts)
            for c in range(2):
                new[x, c, r, 8:32, :] = (1.0 - OMEGA) * old[x, c, r, 8:32, :] + moved[c]
        return 0

    lax.fori_loop(low, high, body, 0)


def clear(ref, count):
    def body(x, _):
        ref[x] = jnp.zeros(ref.shape[1:], F32)
        return 0

    lax.fori_loop(0, count, body, 0)


def pack_kernel(table, right_side, layer_index, absorb_level, packed, inverse_two, temp):
    matrix = sort_matrix(384, 512, False)
    field = exact_dot(right_side[...].reshape(64, 384), matrix)
    both = jnp.concatenate(
        [layer_index[...].reshape(32, 384), absorb_level[...].reshape(32, 384)], axis=0
    )
    codes = jnp.dot(both.astype(F32).astype(BF16), matrix, preferred_element_type=F32)
    inside = lax.broadcasted_iota(jnp.int32, (32, 128), 1) < 96
    total = [jnp.zeros((32, 128), F32), jnp.zeros((32, 128), F32)]
    for r in range(4):
        lanes = slice(r * 128, r * 128 + 128)
        layer = codes[0:32, lanes]
        velocity = jnp.full((32, 128), table[0], F32)
        for n in range(1, 16):
            velocity = jnp.where(layer == float(n), table[n], velocity)
        ratio = KH_FACTOR / velocity
        real = jnp.where(inside, ratio * ratio, 0.0)
        imag = -real * (BETA + ABSORB * codes[32:64, lanes])
        total = [total[0] + real, total[1] + imag]
        for x in range(4):
            rows = slice(x * 8, x * 8 + 8)
            packed[x, 0, r] = field[x * 8 : x * 8 + 8, lanes]
            packed[x, 1, r] = field[32 + x * 8 : 40 + x * 8, lanes]
            packed[x, 2, r] = real[rows]
            packed[x, 3, r] = imag[rows]
    means = []
    for c in range(2):
        t = total[c]
        t = (t[0:8] + t[8:16]) + (t[16:24] + t[24:32])
        temp[c] = t
        means.append(
            [
                ((temp[c, 4 * k : 4 * k + 1] + temp[c, 4 * k + 1 : 4 * k + 2])
                 + (temp[c, 4 * k + 2 : 4 * k + 3] + temp[c, 4 * k + 3 : 4 * k + 4])) * (1.0 / 64.0)
                for k in range(2)
            ]
        )
    for k in range(2):
        w = scaled_inverse(means[0][k], means[1][k], 0.0625)
        for c in range(2):
            inverse_two[0:1, (c * 2 + k) * 128 : (c * 2 + k) * 128 + 128] = w[c]


def pack(table, right_side, layer_index, absorb_level):
    return pl.pallas_call(
        pack_kernel,
        name="pack",
        out_shape=(shape(4, 4, 4, 8, 128), shape(1, 512)),
        in_specs=[SM, VM, VM, VM],
        out_specs=(VM, VM),
        scratch_shapes=[scratch(2, 8, 128)],
        compiler_params=PARAMS,
    )(table, right_side, layer_index, absorb_level)


def set_rows(target, x, c, r, low, mid, high):
    target[x, c, r, 8:16, :] = low
    target[x, c, r, 16:24, :] = mid
    target[x, c, r, 24:32, :] = high


def down_body(source, weight, diag, weight_one, diag_one, guess, out_guess, out_one, out_two, one, s1, t1, temp):
    def first(x, _):
        for r in range(4):
            f = [source[x, c, r, 8:32, :] for c in range(2)]
            w = [weight[x, c, r, 8:32, :] for c in range(2)]
            e = product(w, f)
            for c in range(2):
                guess[x, c, r, 8:32, :] = e[c]
        return 0

    lax.fori_loop(0, 16, first, 0)
    sweep(guess, out_guess, weight, 0, source, 0, 1, 15, 4, 1, 1.0)

    def residual(k, _):
        for s in range(2):
            sums = [None, None]
            for half in range(2):
                x = 2 + 2 * k + half
                for r in (2 * s, 2 * s + 1):
                    e = [out_guess[x, c, r, 8:32, :] for c in range(2)]
                    d = [diag[x, c, r, 8:32, :] for c in range(2)]
                    moved = product(d, e)
                    for c in range(2):
                        value = source[x, c, r, 8:32, :] + neighbour(out_guess, x, c, r, 4, 1) - moved[c]
                        sums[c] = value if sums[c] is None else sums[c] + value
            g = [pair_rows(sums[c], temp.at[c]) * 0.125 for c in range(2)]
            w = [weight_one[k, c, s, 8:32, :] for c in range(2)]
            e = product(w, g)
            for c in range(2):
                s1[k, c, s, 8:32, :] = g[c]
                one[k, c, s, 8:32, :] = e[c]
        return 0

    lax.fori_loop(0, 6, residual, 0)
    sweep(one, t1, weight_one, 0, s1, 0, 1, 5, 2, 2, 0.25)

    total = [None, None]
    for k in (2, 3):
        for s in range(2):
            e = [t1[k, c, s, 8:32, :] for c in range(2)]
            d = [diag_one[k, c, s, 8:32, :] for c in range(2)]
            moved = product(d, e)
            for c in range(2):
                value = s1[k, c, s, 8:32, :] + 0.25 * neighbour(t1, k, c, s, 2, 2) - moved[c]
                total[c] = value if total[c] is None else total[c] + value
    for c in range(2):
        temp[c, 8:32, :] = total[c]
        for k in range(2):
            row = 16 + 4 * k
            value = (temp[c, row : row + 1, :] + temp[c, row + 2 : row + 3, :]) * 0.125
            out_two[0:1, (c * 2 + k) * 128 : (c * 2 + k) * 128 + 128] = value

    def send(k, _):
        for s in range(2):
            for c in range(2):
                out_one[k, c, s * 4 : s * 4 + 4, :] = t1[k + 1, c, s, pl.ds(16, 4, 2), :]
                out_one[k, c + 2, s * 4 : s * 4 + 4, :] = s1[k + 1, c, s, pl.ds(16, 4, 2), :]
                if out_one.shape[1] > 4:
                    out_one[k, c + 4, s * 4 : s * 4 + 4, :] = weight_one[k + 1, c, s, pl.ds(16, 4, 2), :]
        return 0

    lax.fori_loop(0, 4, send, 0)


def down_first_kernel(mid, low, high, source, weight, diag, weight_one, diag_one, out_guess, out_one, out_two,
                      guess, one, s1, t1, temp):
    clear(guess, 16)
    clear(out_guess, 16)
    for ref in (one, s1, t1, weight_one, diag_one):
        clear(ref, 6)
    temp[...] = jnp.zeros(temp.shape, F32)
    zero = jnp.zeros((8, 128), F32)

    def fill(x, edge):
        for r in range(4):
            for c in range(4):
                parts = (zero, mid[x, c, r], zero) if edge else (low[x - 1, c, r], mid[x, c, r], high[x - 1, c, r])
                set_rows(source if c < 2 else diag, x, c % 2, r, *parts)
            real, imag = diag[x, 0, r, 8:32, :], diag[x, 1, r, 8:32, :]
            w = scaled_inverse(real, imag, 1.0)
            for c in range(2):
                weight[x, c, r, 8:32, :] = w[c]

    def filled(x, _):
        fill(x, False)
        return 0

    fill(0, True)
    lax.fori_loop(1, 15, filled, 0)
    fill(15, True)

    def coarse(k, _):
        for s in range(2):
            shift = []
            for c in range(2):
                total = None
                for half in range(2):
                    for r in (2 * s, 2 * s + 1):
                        value = diag[2 + 2 * k + half, c, r, 8:32, :]
                        total = value if total is None else total + value
                shift.append(pair_rows(total, temp.at[c]) * 0.125)
            w = scaled_inverse(shift[0], shift[1], 0.25)
            d = (1.5 - shift[0], -shift[1])
            for c in range(2):
                weight_one[k, c, s, 8:32, :] = w[c]
                diag_one[k, c, s, 8:32, :] = d[c]
        return 0

    lax.fori_loop(0, 6, coarse, 0)

    def turn(x, _):
        for r in range(4):
            diag[x, 0, r, 8:32, :] = 6.0 - diag[x, 0, r, 8:32, :]
            diag[x, 1, r, 8:32, :] = -diag[x, 1, r, 8:32, :]
        return 0

    lax.fori_loop(0, 16, turn, 0)
    down_body(source, weight, diag, weight_one, diag_one, guess, out_guess, out_one, out_two, one, s1, t1, temp)


FINE = (16, 2, 4, 40, 128)
COARSE = (6, 2, 2, 40, 128)
DOWN_SCRATCH = [scratch(*FINE), scratch(*COARSE), scratch(*COARSE), scratch(*COARSE), scratch(2, 40, 128)]


def down_first(mid, low, high):
    return pl.pallas_call(
        down_first_kernel,
        name="down_first",
        out_shape=(shape(*FINE), shape(*FINE), shape(*FINE), shape(*COARSE), shape(*COARSE), shape(*FINE),
                   shape(4, 6, 8, 128), shape(1, 512)),
        in_specs=[VM] * 3,
        out_specs=(VM,) * 8,
        scratch_shapes=DOWN_SCRATCH,
        compiler_params=PARAMS,
    )(mid, low, high)


def down_second_kernel(mid, low, high, weight, diag, weight_one, diag_one, out_source, out_guess, out_one, out_two,
                       guess, one, s1, t1, temp):
    clear(guess, 16)
    clear(out_guess, 16)
    for ref in (one, s1, t1):
        clear(ref, 6)
    temp[...] = jnp.zeros(temp.shape, F32)
    zero = jnp.zeros((8, 128), F32)

    def fill(x, edge):
        for r in range(4):
            for c in range(2):
                parts = (zero, mid[x, c, r], zero) if edge else (low[x - 1, c, r], mid[x, c, r], high[x - 1, c, r])
                set_rows(out_source, x, c, r, *parts)

    def filled(x, _):
        fill(x, False)
        return 0

    fill(0, True)
    lax.fori_loop(1, 15, filled, 0)
    fill(15, True)
    down_body(out_source, weight, diag, weight_one, diag_one, guess, out_guess, out_one, out_two, one, s1, t1, temp)


def down_second(mid, low, high, weight, diag, weight_one, diag_one):
    return pl.pallas_call(
        down_second_kernel,
        name="down_second",
        out_shape=(shape(*FINE), shape(*FINE), shape(4, 4, 8, 128), shape(1, 512)),
        in_specs=[VM] * 7,
        out_specs=(VM,) * 4,
        scratch_shapes=DOWN_SCRATCH,
        compiler_params=PARAMS,
    )(mid, low, high, weight, diag, weight_one, diag_one)


def solve_two(source, weight, ping, pong, planes, groups):
    clear(ping, planes + 8)
    clear(pong, planes + 8)
    rows = slice(8, 8 + groups)

    def start(x, _):
        for k in range(2):
            lanes = [slice((c * 2 + k) * 128, (c * 2 + k) * 128 + 128) for c in range(2)]
            e = product([weight[x, :, l] for l in lanes], [source[x, :, l] for l in lanes])
            for c in range(2):
                ping[x + 4, c * 2 + k, rows, :] = e[c]
        return 0

    lax.fori_loop(0, planes, start, 0)

    def step(old, new):
        def body(x, _):
            for k in range(2):
                parts, center = [], []
                for c in range(2):
                    here = old[x + 4, c * 2 + k, rows, :]
                    other = c * 2 + 1 - k
                    total = old[x + 3, c * 2 + k, rows, :] + old[x + 5, c * 2 + k, rows, :]
                    if k == 0:
                        total = total + old[x + 4, other, rows, :] + old[x + 4, other, 7 : 7 + groups, :]
                    else:
                        total = total + old[x + 4, other, rows, :] + old[x + 4, other, 9 : 9 + groups, :]
                    total = total + (pltpu.roll(here, 1, 1) + pltpu.roll(here, 127, 1))
                    lanes = slice((c * 2 + k) * 128, (c * 2 + k) * 128 + 128)
                    parts.append(source[x, :, lanes] + 0.0625 * total)
                    center.append(here)
                w = [weight[x, :, (c * 2 + k) * 128 : (c * 2 + k) * 128 + 128] for c in range(2)]
                moved = product(w, parts)
                for c in range(2):
                    new[x + 4, c * 2 + k, rows, :] = (1.0 - OMEGA) * center[c] + moved[c]
            return 0

        lax.fori_loop(0, planes, body, 0)

    pairs = (ping, pong)
    for number in range(NC - 1):
        step(pairs[number % 2], pairs[(number + 1) % 2])
    return pairs[(NC - 1) % 2]


def spread_rows(target, x, c, tile, block):
    for s in range(2):
        for twice in range(2):
            target[x, c, s, pl.ds(8 + 8 * tile + twice, 4, 2), :] = block[s * 4 : s * 4 + 4, :]


def add_two(answer, one, where, first, count):
    gx, gy = where[0], where[1]
    row = lax.broadcasted_iota(jnp.int32, (8, 128), 0)
    for j in range(count):
        x = gx + 4 + (first + j) // 2
        for c in range(2):
            for tile in range(3):
                spot = gy + 7 + tile
                low = jnp.broadcast_to(answer[x, c * 2, pl.ds(spot, 1), :], (8, 128))
                high = jnp.broadcast_to(answer[x, c * 2 + 1, pl.ds(spot, 1), :], (8, 128))
                value = jnp.where(row < 4, low, high)
                at = slice(8 + 8 * tile, 16 + 8 * tile)
                for s in range(2):
                    one[j, c, s, at, :] = one[j, c, s, at, :] + value


def up_first_kernel(planes, groups, where, source_two, weight_two, near_low, near_high, far_low, far_high, own,
                    source, weight, diag, guess, out_source, out_first, out_weight,
                    ping, pong, one, s1, t1, ea, eb):
    answer = solve_two(source_two, weight_two, ping, pong, planes, groups)
    for ref in (one, t1, s1):
        clear(ref, 12)
    clear(out_weight, 12)
    j = 0
    for ref, low, high in ((far_low, 0, 3), (near_low, 0, 2), (own, 0, 2), (near_high, 0, 2), (far_high, 0, 3)):
        for k in range(low, high):
            for c in range(2):
                for tile in range(3):
                    spread_rows(one, j, c, tile, ref[k, tile, c])
                    spread_rows(s1, j, c, tile, ref[k, tile, c + 2])
                    spread_rows(out_weight, j, c, tile, ref[k, tile, c + 4])
            j += 1
    add_two(answer, one, where, -5, 12)
    sweep(one, t1, out_weight, 0, s1, 0, 1, 11, 2, 2, 0.25)
    sweep(t1, one, out_weight, 0, s1, 0, 2, 10, 2, 2, 0.25)
    clear(ea, 16)
    clear(eb, 16)

    def correct(x1, _):
        for half in range(2):
            x = 2 * x1 - 4 + half
            for r in range(4):
                for c in range(2):
                    ea[x, c, r, 8:32, :] = guess[x, c, r, 8:32, :] + one[x1, c, r // 2, 8:32, :]
        return 0

    lax.fori_loop(2, 10, correct, 0)
    sweep(ea, eb, weight, 0, source, 0, 2, 14, 4, 1, 1.0)
    sweep(eb, ea, weight, 0, source, 0, 3, 13, 4, 1, 1.0)

    def rest(x, _):
        for r in range(4):
            e = [ea[x, c, r, 8:32, :] for c in range(2)]
            moved = product([diag[x, c, r, 8:32, :] for c in range(2)], e)
            for c in range(2):
                value = source[x, c, r, 8:32, :] + neighbour(ea, x, c, r, 4, 1) - moved[c]
                out_source[x - 4, c, r] = value[8:16]
        return 0

    lax.fori_loop(4, 12, rest, 0)
    for x in range(4):
        for c in range(2):
            for r in range(4):
                out_first[x, c, r] = ea[x + 6, c, r, 16:24, :]


def up_first(where, source_two, weight_two, near_low, near_high, far_low, far_high, own, source, weight, diag, guess):
    planes, groups = source_two.shape[0], source_two.shape[1]
    two = scratch(planes + 8, 4, 16 + groups, 128)
    level = scratch(12, 2, 2, 40, 128)
    return pl.pallas_call(
        lambda *refs: up_first_kernel(planes, groups, *refs),
        name="up_first",
        out_shape=(shape(8, 2, 4, 8, 128), shape(4, 2, 4, 8, 128), shape(12, 2, 2, 40, 128)),
        in_specs=[SM] + [VM] * 11,
        out_specs=(VM,) * 3,
        scratch_shapes=[two, two, level, level, level, scratch(*FINE), scratch(*FINE)],
        compiler_params=PARAMS,
    )(where, source_two, weight_two, near_low, near_high, far_low, far_high, own, source, weight, diag, guess)


def up_second_kernel(planes, groups, where, source_two, weight_two, near_low, near_high, own,
                     source, weight, guess, weight_one, first, result,
                     ping, pong, one, s1, t1, ea, eb):
    answer = solve_two(source_two, weight_two, ping, pong, planes, groups)
    for ref in (one, t1, s1):
        clear(ref, 8)
    j = 0
    for ref, low, high in ((near_low, 0, 3), (own, 0, 2), (near_high, 0, 3)):
        for k in range(low, high):
            for c in range(2):
                for tile in range(3):
                    spread_rows(one, j, c, tile, ref[k, tile, c])
                    spread_rows(s1, j, c, tile, ref[k, tile, c + 2])
            j += 1
    add_two(answer, one, where, -3, 8)
    sweep(one, t1, weight_one, 2, s1, 0, 1, 7, 2, 2, 0.25)
    sweep(t1, one, weight_one, 2, s1, 0, 2, 6, 2, 2, 0.25)
    clear(ea, 16)
    clear(eb, 16)

    def correct(x1, _):
        for half in range(2):
            x = 2 * x1 + half
            for r in range(4):
                for c in range(2):
                    ea[x, c, r, 8:32, :] = guess[x, c, r, 8:32, :] + one[x1, c, r // 2, 8:32, :]
        return 0

    lax.fori_loop(2, 6, correct, 0)
    sweep(ea, eb, weight, 0, source, 0, 5, 11, 4, 1, 1.0)
    sweep(eb, ea, weight, 0, source, 0, 6, 10, 4, 1, 1.0)
    blocks = []
    for c in range(2):
        for x in range(4):
            blocks.append(
                jnp.concatenate([first[x, c, r] + ea[x + 6, c, r, 16:24, :] for r in range(4)], axis=1)
            )
    values = jnp.concatenate(blocks, axis=0)
    result[...] = exact_dot(values, sort_matrix(512, 384, True)).reshape(2, 4, 8, 384)


def up_second(where, source_two, weight_two, near_low, near_high, own, source, weight, guess, weight_one, first):
    planes, groups = source_two.shape[0], source_two.shape[1]
    two = scratch(planes + 8, 4, 16 + groups, 128)
    level = scratch(8, 2, 2, 40, 128)
    return pl.pallas_call(
        lambda *refs: up_second_kernel(planes, groups, *refs),
        name="up_second",
        out_shape=shape(2, 4, 8, 384),
        in_specs=[SM] + [VM] * 10,
        out_specs=VM,
        scratch_shapes=[two, two, level, level, level, scratch(*FINE), scratch(*FINE)],
        compiler_params=PARAMS,
    )(where, source_two, weight_two, near_low, near_high, own, source, weight, guess, weight_one, first)


def shifted(block, axis, by):
    count = lax.axis_size(axis)
    pairs = [(i, i + by) for i in range(count) if 0 <= i + by < count]
    return lax.ppermute(block, axis, pairs)


def gather_two(row):
    count_y, count_x = lax.axis_size("gy"), lax.axis_size("gx")
    column = lax.all_to_all(jnp.broadcast_to(row[None], (count_y, 1, 512)), "gy", 0, 0)
    column = column.reshape(1, count_y, 512)
    return lax.all_to_all(jnp.broadcast_to(column, (count_x, count_y, 512)), "gx", 0, 0)


def y_sides(block):
    return shifted(block, "gy", 1), shifted(block, "gy", -1)


def y_tiles(block):
    low, high = y_sides(block)
    return jnp.stack([low, block, high], axis=1)


def local(right_side, velocity_table, layer_index, absorb_level):
    where = jnp.stack([lax.axis_index("gx"), lax.axis_index("gy")]).astype(jnp.int32)
    packed, inverse_two = pack(velocity_table, right_side, layer_index, absorb_level)
    weight_two = gather_two(inverse_two)
    mid = jnp.concatenate(
        [
            shifted(packed[2:], "gx", 2),
            shifted(packed, "gx", 1),
            packed,
            shifted(packed, "gx", -1),
            shifted(packed[:2], "gx", -2),
        ]
    )
    low, high = y_sides(mid[1:15])
    source, weight, diag, weight_one, diag_one, guess, one, two = down_first(mid, low, high)
    source_two = gather_two(two)
    tiles = y_tiles(one)
    near_low, near_high = shifted(tiles[1:3], "gx", 1), shifted(tiles[1:3], "gx", -1)
    far_low, far_high = shifted(tiles[0:3], "gx", 2), shifted(tiles[1:4], "gx", -2)
    rest, first, weight_one_wide = up_first(
        where, source_two, weight_two, near_low, near_high, far_low, far_high, tiles[1:3], source, weight, diag, guess
    )
    mid = jnp.concatenate([shifted(rest[0:6], "gx", 1), rest[2:6], shifted(rest[2:8], "gx", -1)])
    low, high = y_sides(mid[1:15])
    source, guess, one, two = down_second(mid, low, high, weight, diag, weight_one, diag_one)
    source_two = gather_two(two)
    tiles = y_tiles(one)
    near_low, near_high = shifted(tiles[0:3], "gx", 1), shifted(tiles[1:4], "gx", -1)
    return up_second(
        where, source_two, weight_two, near_low, near_high, tiles[1:3], source, weight, guess, weight_one_wide, first
    )


def solution(mesh):
    placed = (P(None, "gx", "gy", None), P(), P("gx", "gy", None), P("gx", "gy", None))
    return jax.shard_map(
        local, mesh=mesh, in_specs=placed, out_specs=P(None, "gx", "gy", None), check_vma=False
    )
```

```python
import math

import jax
import jax.numpy as jnp
from jax import lax
from jax.experimental import pallas as pl
from jax.experimental.pallas import tpu as pltpu
from jax.sharding import PartitionSpec as P


NC = 8
WINDOW = 21
OMEGA = 0.6
BETA = 0.5
ABSORB = 0.25
KH_FACTOR = 2.0 * math.pi * 6.0 * 20.0

F32 = jnp.float32
BF16 = jnp.bfloat16
VM = pl.BlockSpec(memory_space=pltpu.VMEM)
SM = pl.BlockSpec(memory_space=pltpu.SMEM)
PARAMS = pltpu.CompilerParams(vmem_limit_bytes=24 * 1024 * 1024)


def shape(*dims):
    return jax.ShapeDtypeStruct(dims, F32)


def scratch(*dims):
    return pltpu.VMEM(dims, F32)


def sort_matrix(rows, columns, flip):
    first = lax.broadcasted_iota(jnp.int32, (rows, columns), 0)
    second = lax.broadcasted_iota(jnp.int32, (rows, columns), 1)
    if flip:
        first, second = second, first
    lane = second % 128
    hit = (first == 4 * lane + second // 128) & (lane < 96)
    return jnp.where(hit, 1.0, 0.0).astype(BF16)


def exact_dot(values, matrix):
    high = values.astype(BF16)
    rest = values - high.astype(F32)
    middle = rest.astype(BF16)
    low = (rest - middle.astype(F32)).astype(BF16)
    dot = lambda part: jnp.dot(part, matrix, preferred_element_type=F32)
    return (dot(low) + dot(middle)) + dot(high)


def scaled_inverse(real, imag, scale):
    diag_real = 6.0 * scale - real
    diag_imag = -imag
    factor = OMEGA / (diag_real * diag_real + diag_imag * diag_imag)
    factor = jnp.where(real > 0.0, factor, 0.0)
    return diag_real * factor, -diag_imag * factor


def product(a, b):
    return a[0] * b[0] - a[1] * b[1], a[0] * b[1] + a[1] * b[0]


def pair_rows(value, temp):
    temp[8:32, :] = value
    row = lax.broadcasted_iota(jnp.int32, (24, 128), 0)
    return value + jnp.where(row % 2 == 0, temp[9:33, :], temp[7:31, :])


def neighbour(ref, x, c, r, count, step):
    center = lambda s: ref[x, c, s, 8:32, :]
    up = center(r + 1) if r < count - 1 else pltpu.roll(center(0), 127, 1)
    down = center(r - 1) if r > 0 else pltpu.roll(center(count - 1), 1, 1)
    total = ref[x - 1, c, r, 8:32, :] + ref[x + 1, c, r, 8:32, :]
    total = total + ref[x, c, r, 8 - step : 32 - step, :] + ref[x, c, r, 8 + step : 32 + step, :]
    return total + (up + down)


def sweep(old, new, weight, weight_at, source, source_at, low, high, count, step, scale):
    def body(x, _):
        for r in range(count):
            parts = []
            for c in range(2):
                total = neighbour(old, x, c, r, count, step)
                if scale != 1.0:
                    total = total * scale
                parts.append(source[x + source_at, c, r] + total)
            w = [weight[x + weight_at, c, r] for c in range(2)]
            moved = product(w, parts)
            for c in range(2):
                new[x, c, r, 8:32, :] = (1.0 - OMEGA) * old[x, c, r, 8:32, :] + moved[c]
        return 0

    lax.fori_loop(low, high, body, 0)


def clear(ref, count):
    def body(x, _):
        ref[x] = jnp.zeros(ref.shape[1:], F32)
        return 0

    lax.fori_loop(0, count, body, 0)


def clear_edges(ref, count):
    zero = jnp.zeros((8, 128), F32)

    def body(x, _):
        for c in range(2):
            for r in range(ref.shape[2]):
                ref[x, c, r, 0:8, :] = zero
                ref[x, c, r, 32:40, :] = zero
        return 0

    lax.fori_loop(0, count, body, 0)


def dense(target, pieces):
    lane = lax.broadcasted_iota(jnp.int32, (1, 128), 1)
    for n in range(3):
        tail = pltpu.roll(pieces[n + 1], 128 - 32 * (n + 1), 1)
        head = pieces[n] if n == 0 else pltpu.roll(pieces[n], 128 - 32 * n, 1)
        target[0:1, n * 128 : n * 128 + 128] = jnp.where(lane < 96 - 32 * n, head, tail)


def loose(block):
    lane = lax.broadcasted_iota(jnp.int32, (block.shape[0], 128), 1)
    parts = [block[:, n * 128 : n * 128 + 128] for n in range(3)]
    result = []
    for k in range(4):
        if k == 0:
            value = parts[0]
        elif k == 3:
            value = pltpu.roll(parts[2], 96, 1)
        else:
            value = jnp.where(lane < 32 * k, pltpu.roll(parts[k - 1], 32 * k, 1), pltpu.roll(parts[k], 32 * k, 1))
        result.append(jnp.where(lane < 96, value, 0.0))
    return result


def pack_kernel(table, right_side, layer_index, absorb_level, packed, inverse_two, temp):
    matrix = sort_matrix(384, 512, False)
    field = exact_dot(right_side[...].reshape(64, 384), matrix)
    both = jnp.concatenate(
        [layer_index[...].reshape(32, 384), absorb_level[...].reshape(32, 384)], axis=0
    )
    codes = jnp.dot(both.astype(F32).astype(BF16), matrix, preferred_element_type=F32)
    inside = lax.broadcasted_iota(jnp.int32, (32, 128), 1) < 96
    total = [jnp.zeros((32, 128), F32), jnp.zeros((32, 128), F32)]
    for r in range(4):
        lanes = slice(r * 128, r * 128 + 128)
        layer = codes[0:32, lanes]
        velocity = jnp.full((32, 128), table[0], F32)
        for n in range(1, 16):
            velocity = jnp.where(layer == float(n), table[n], velocity)
        ratio = KH_FACTOR / velocity
        real = jnp.where(inside, ratio * ratio, 0.0)
        imag = -real * (BETA + ABSORB * codes[32:64, lanes])
        total = [total[0] + real, total[1] + imag]
        for x in range(4):
            rows = slice(x * 8, x * 8 + 8)
            packed[x, 0, r] = field[x * 8 : x * 8 + 8, lanes]
            packed[x, 1, r] = field[32 + x * 8 : 40 + x * 8, lanes]
            packed[x, 2, r] = real[rows]
            packed[x, 3, r] = imag[rows]
    means = []
    for c in range(2):
        t = total[c]
        t = (t[0:8] + t[8:16]) + (t[16:24] + t[24:32])
        temp[c] = t
        means.append(
            [
                ((temp[c, 4 * k : 4 * k + 1] + temp[c, 4 * k + 1 : 4 * k + 2])
                 + (temp[c, 4 * k + 2 : 4 * k + 3] + temp[c, 4 * k + 3 : 4 * k + 4])) * (1.0 / 64.0)
                for k in range(2)
            ]
        )
    w = [scaled_inverse(means[0][k], means[1][k], 0.0625) for k in range(2)]
    dense(inverse_two, [w[k][c] for c in range(2) for k in range(2)])


def pack(table, right_side, layer_index, absorb_level):
    return pl.pallas_call(
        pack_kernel,
        name="pack",
        out_shape=(shape(4, 4, 4, 8, 128), shape(1, 384)),
        in_specs=[SM, VM, VM, VM],
        out_specs=(VM, VM),
        scratch_shapes=[scratch(2, 8, 128)],
        compiler_params=PARAMS,
    )(table, right_side, layer_index, absorb_level)


def set_rows(target, x, c, r, low, mid, high):
    target[x, c, r, 0:8, :] = low
    target[x, c, r, 8:16, :] = mid
    target[x, c, r, 16:24, :] = high


def down_body(source, weight, diag, weight_one, diag_one, guess, out_guess, out_one, out_two, one, s1, t1, temp):
    def first(x, _):
        for r in range(4):
            f = [source[x, c, r] for c in range(2)]
            w = [weight[x, c, r] for c in range(2)]
            e = product(w, f)
            for c in range(2):
                guess[x, c, r, 8:32, :] = e[c]
        return 0

    lax.fori_loop(0, 16, first, 0)
    sweep(guess, out_guess, weight, 0, source, 0, 1, 15, 4, 1, 1.0)

    def residual(k, _):
        for s in range(2):
            sums = [None, None]
            for half in range(2):
                x = 2 + 2 * k + half
                for r in (2 * s, 2 * s + 1):
                    e = [out_guess[x, c, r, 8:32, :] for c in range(2)]
                    d = [diag[x, c, r] for c in range(2)]
                    moved = product(d, e)
                    for c in range(2):
                        value = source[x, c, r] + neighbour(out_guess, x, c, r, 4, 1) - moved[c]
                        sums[c] = value if sums[c] is None else sums[c] + value
            g = [pair_rows(sums[c], temp.at[c]) * 0.125 for c in range(2)]
            w = [weight_one[k, c, s] for c in range(2)]
            e = product(w, g)
            for c in range(2):
                s1[k, c, s] = g[c]
                one[k, c, s, 8:32, :] = e[c]
        return 0

    lax.fori_loop(0, 6, residual, 0)
    sweep(one, t1, weight_one, 0, s1, 0, 1, 5, 2, 2, 0.25)

    total = [None, None]
    for k in (2, 3):
        for s in range(2):
            e = [t1[k, c, s, 8:32, :] for c in range(2)]
            d = [diag_one[k, c, s] for c in range(2)]
            moved = product(d, e)
            for c in range(2):
                value = s1[k, c, s] + 0.25 * neighbour(t1, k, c, s, 2, 2) - moved[c]
                total[c] = value if total[c] is None else total[c] + value
    pieces = []
    for c in range(2):
        temp[c, 8:32, :] = total[c]
        for k in range(2):
            row = 16 + 4 * k
            pieces.append((temp[c, row : row + 1, :] + temp[c, row + 2 : row + 3, :]) * 0.125)
    dense(out_two, pieces)

    def send(k, _):
        for s in range(2):
            for c in range(2):
                out_one[k, c, s * 4 : s * 4 + 4, :] = t1[k + 1, c, s, pl.ds(16, 4, 2), :]
                out_one[k, c + 2, s * 4 : s * 4 + 4, :] = s1[k + 1, c, s, pl.ds(8, 4, 2), :]
                if out_one.shape[1] > 4:
                    out_one[k, c + 4, s * 4 : s * 4 + 4, :] = weight_one[k + 1, c, s, pl.ds(8, 4, 2), :]
        return 0

    lax.fori_loop(0, 4, send, 0)


def down_first_kernel(before, mid, after, low, high, source, weight, diag, weight_one, diag_one, out_guess, out_one, out_two,
                      guess, one, s1, t1, temp):
    clear_edges(guess, 16)
    clear_edges(out_guess, 16)
    clear_edges(one, 6)
    clear_edges(t1, 6)
    zero = jnp.zeros((8, 128), F32)

    def fill(x, edge):
        for r in range(4):
            for c in range(4):
                if edge is None:
                    parts = (low[x - 1, c, r], mid[x - 1, c, r], high[x - 1, c, r])
                else:
                    parts = (zero, edge[c, r], zero)
                set_rows(source if c < 2 else diag, x, c % 2, r, *parts)
            real, imag = diag[x, 0, r], diag[x, 1, r]
            w = scaled_inverse(real, imag, 1.0)
            for c in range(2):
                weight[x, c, r] = w[c]

    def filled(x, _):
        fill(x, None)
        return 0

    fill(0, before.at[0])
    lax.fori_loop(1, 15, filled, 0)
    fill(15, after.at[after.shape[0] - 1])

    def coarse(k, _):
        for s in range(2):
            shift = []
            for c in range(2):
                total = None
                for half in range(2):
                    for r in (2 * s, 2 * s + 1):
                        value = diag[2 + 2 * k + half, c, r]
                        total = value if total is None else total + value
                shift.append(pair_rows(total, temp.at[c]) * 0.125)
            w = scaled_inverse(shift[0], shift[1], 0.25)
            d = (1.5 - shift[0], -shift[1])
            for c in range(2):
                weight_one[k, c, s] = w[c]
                diag_one[k, c, s] = d[c]
        return 0

    lax.fori_loop(0, 6, coarse, 0)

    def turn(x, _):
        for r in range(4):
            diag[x, 0, r] = 6.0 - diag[x, 0, r]
            diag[x, 1, r] = -diag[x, 1, r]
        return 0

    lax.fori_loop(0, 16, turn, 0)
    down_body(source, weight, diag, weight_one, diag_one, guess, out_guess, out_one, out_two, one, s1, t1, temp)


FINE = (16, 2, 4, 24, 128)
WIDE = (16, 2, 4, 40, 128)
COARSE = (6, 2, 2, 24, 128)
COARSE_WIDE = (6, 2, 2, 40, 128)
DOWN_SCRATCH = [scratch(*WIDE), scratch(*COARSE_WIDE), scratch(*COARSE), scratch(*COARSE_WIDE), scratch(2, 40, 128)]


def down_first(before, mid, after, low, high):
    return pl.pallas_call(
        down_first_kernel,
        name="down_first",
        out_shape=(shape(*FINE), shape(*FINE), shape(*FINE), shape(*COARSE), shape(*COARSE), shape(*WIDE),
                   shape(4, 6, 8, 128), shape(1, 384)),
        in_specs=[VM] * 5,
        out_specs=(VM,) * 8,
        scratch_shapes=DOWN_SCRATCH,
        compiler_params=PARAMS,
    )(before, mid, after, low, high)


def down_second_kernel(before, mid, after, low, high, weight, diag, weight_one, diag_one, out_source, out_guess, out_one, out_two,
                       guess, one, s1, t1, temp):
    clear_edges(guess, 16)
    clear_edges(out_guess, 16)
    clear_edges(one, 6)
    clear_edges(t1, 6)
    zero = jnp.zeros((8, 128), F32)

    def fill(x, edge):
        for r in range(4):
            for c in range(2):
                if edge is None:
                    parts = (low[x - 1, c, r], mid[x - 1, c, r], high[x - 1, c, r])
                else:
                    parts = (zero, edge[c, r], zero)
                set_rows(out_source, x, c, r, *parts)

    def filled(x, _):
        fill(x, None)
        return 0

    fill(0, before.at[0])
    lax.fori_loop(1, 15, filled, 0)
    fill(15, after.at[after.shape[0] - 1])
    down_body(out_source, weight, diag, weight_one, diag_one, guess, out_guess, out_one, out_two, one, s1, t1, temp)


def down_second(before, mid, after, low, high, weight, diag, weight_one, diag_one):
    return pl.pallas_call(
        down_second_kernel,
        name="down_second",
        out_shape=(shape(*FINE), shape(*WIDE), shape(4, 4, 8, 128), shape(1, 384)),
        in_specs=[VM] * 9,
        out_specs=(VM,) * 4,
        scratch_shapes=DOWN_SCRATCH,
        compiler_params=PARAMS,
    )(before, mid, after, low, high, weight, diag, weight_one, diag_one)


def unpack_two(packed, target, planes):
    def body(x, _):
        for k, part in enumerate(loose(packed[x])):
            target[x, k] = part
        return 0

    lax.fori_loop(0, planes, body, 0)


def solve_two(begin, source, weight, ping, pong, window, groups):
    clear(ping, window + 8)
    clear(pong, window + 8)
    rows = slice(8, 8 + groups)
    block = next(b for b in (7, 4, 1) if window % b == 0)

    def over(body):
        def several(number, _):
            for n in range(block):
                body(number * block + n)
            return 0

        lax.fori_loop(0, window // block, several, 0)

    def start(x):
        for k in range(2):
            e = product([weight[begin + x, k], weight[begin + x, 2 + k]], [source[begin + x, k], source[begin + x, 2 + k]])
            for c in range(2):
                ping[x + 4, c * 2 + k, rows, :] = e[c]

    over(start)

    def step(old, new):
        def body(x):
            here = [old[x + 4, n, rows, :] for n in range(4)]
            for k in range(2):
                parts = []
                for c in range(2):
                    n, other = c * 2 + k, c * 2 + 1 - k
                    side = old[x + 4, other, 7 : 7 + groups, :] if k == 0 else old[x + 4, other, 9 : 9 + groups, :]
                    total = (old[x + 3, n, rows, :] + old[x + 5, n, rows, :]) + (here[other] + side)
                    total = total + (pltpu.roll(here[n], 1, 1) + pltpu.roll(here[n], 127, 1))
                    parts.append(source[begin + x, n] + 0.0625 * total)
                moved = product([weight[begin + x, k], weight[begin + x, 2 + k]], parts)
                for c in range(2):
                    new[x + 4, c * 2 + k, rows, :] = (1.0 - OMEGA) * here[c * 2 + k] + moved[c]

        over(body)

    pairs = (ping, pong)
    for number in range(NC - 1):
        step(pairs[number % 2], pairs[(number + 1) % 2])
    return pairs[(NC - 1) % 2]


def spread_rows(target, at, x, c, tile, block):
    for s in range(2):
        for twice in range(2):
            target[x, c, s, pl.ds(at + 8 * tile + twice, 4, 2), :] = block[s * 4 : s * 4 + 4, :]


def add_two(answer, begin, one, where, first, count):
    gx, gy = where[0] - begin, where[1]
    row = lax.broadcasted_iota(jnp.int32, (8, 128), 0)
    for j in range(count):
        x = gx + 4 + (first + j) // 2
        for c in range(2):
            for tile in range(3):
                spot = gy + 7 + tile
                low = jnp.broadcast_to(answer[x, c * 2, pl.ds(spot, 1), :], (8, 128))
                high = jnp.broadcast_to(answer[x, c * 2 + 1, pl.ds(spot, 1), :], (8, 128))
                value = jnp.where(row < 4, low, high)
                at = slice(8 + 8 * tile, 16 + 8 * tile)
                for s in range(2):
                    one[j, c, s, at, :] = one[j, c, s, at, :] + value


def up_first_kernel(planes, groups, where, source_two, weight_two, near_low, near_high, far_low, far_high, own,
                    source, weight, diag, guess, out_source, out_first, out_weight,
                    out_low, out_high, out_two, packed_two, ping, pong, one, s1, t1, ea, eb):
    window = min(planes, WINDOW)
    begin = jnp.clip(where[0] - 10, 0, planes - window)
    unpack_two(weight_two, out_two, planes)
    unpack_two(source_two, packed_two, planes)
    answer = solve_two(begin, packed_two, out_two, ping, pong, window, groups)
    clear_edges(one, 12)
    clear_edges(t1, 12)
    j = 0
    for ref, low, high in ((far_low, 0, 3), (near_low, 0, 2), (own, 0, 2), (near_high, 0, 2), (far_high, 0, 3)):
        for k in range(low, high):
            for c in range(2):
                for tile in range(3):
                    spread_rows(one, 8, j, c, tile, ref[k, tile, c])
                    spread_rows(s1, 0, j, c, tile, ref[k, tile, c + 2])
                    spread_rows(out_weight, 0, j, c, tile, ref[k, tile, c + 4])
            j += 1
    add_two(answer, begin, one, where, -5, 12)
    sweep(one, t1, out_weight, 0, s1, 0, 1, 11, 2, 2, 0.25)
    sweep(t1, one, out_weight, 0, s1, 0, 2, 10, 2, 2, 0.25)
    clear_edges(ea, 16)
    clear_edges(eb, 16)

    def correct(x1, _):
        for half in range(2):
            x = 2 * x1 - 4 + half
            for r in range(4):
                for c in range(2):
                    ea[x, c, r, 8:32, :] = guess[x, c, r, 8:32, :] + one[x1, c, r // 2, 8:32, :]
        return 0

    lax.fori_loop(2, 10, correct, 0)
    sweep(ea, eb, weight, 0, source, 0, 2, 14, 4, 1, 1.0)
    sweep(eb, ea, weight, 0, source, 0, 3, 13, 4, 1, 1.0)

    def rest(targets):
        def body(x, _):
            for r in range(4):
                e = [ea[x, c, r, 8:32, :] for c in range(2)]
                moved = product([diag[x, c, r] for c in range(2)], e)
                for c in range(2):
                    value = source[x, c, r] + neighbour(ea, x, c, r, 4, 1) - moved[c]
                    for target, first in targets:
                        target[x - first, c, r] = value[8:16]
            return 0

        return body

    lax.fori_loop(4, 6, rest([(out_low, 4)]), 0)
    lax.fori_loop(6, 10, rest([(out_low, 4), (out_source, 6), (out_high, 6)]), 0)
    lax.fori_loop(10, 12, rest([(out_high, 6)]), 0)
    for x in range(4):
        for c in range(2):
            for r in range(4):
                out_first[x, c, r] = ea[x + 6, c, r, 16:24, :]


def up_first(where, source_two, weight_two, near_low, near_high, far_low, far_high, own, source, weight, diag, guess):
    planes, groups = source_two.shape[0], source_two.shape[1]
    two = scratch(min(planes, WINDOW) + 8, 4, 16 + groups, 128)
    level, wide = scratch(12, 2, 2, 24, 128), scratch(12, 2, 2, 40, 128)
    return pl.pallas_call(
        lambda *refs: up_first_kernel(planes, groups, *refs),
        name="up_first",
        out_shape=(shape(4, 2, 4, 8, 128), shape(4, 2, 4, 8, 128), shape(12, 2, 2, 24, 128),
                   shape(6, 2, 4, 8, 128), shape(6, 2, 4, 8, 128), shape(planes, 4, groups, 128)),
        in_specs=[SM] + [VM] * 11,
        out_specs=(VM,) * 6,
        scratch_shapes=[scratch(planes, 4, groups, 128), two, two, wide, level, wide, scratch(*WIDE), scratch(*WIDE)],
        compiler_params=PARAMS,
    )(where, source_two, weight_two, near_low, near_high, far_low, far_high, own, source, weight, diag, guess)


def up_second_kernel(planes, groups, where, source_two, weight_two, near_low, near_high, own,
                     source, weight, guess, weight_one, first, result,
                     packed_two, ping, pong, one, s1, t1, ea, eb):
    window = min(planes, WINDOW)
    begin = jnp.clip(where[0] - 10, 0, planes - window)
    unpack_two(source_two, packed_two, planes)
    answer = solve_two(begin, packed_two, weight_two, ping, pong, window, groups)
    clear_edges(one, 8)
    clear_edges(t1, 8)
    j = 0
    for ref, low, high in ((near_low, 0, 3), (own, 0, 2), (near_high, 0, 3)):
        for k in range(low, high):
            for c in range(2):
                for tile in range(3):
                    spread_rows(one, 8, j, c, tile, ref[k, tile, c])
                    spread_rows(s1, 0, j, c, tile, ref[k, tile, c + 2])
            j += 1
    add_two(answer, begin, one, where, -3, 8)
    sweep(one, t1, weight_one, 2, s1, 0, 1, 7, 2, 2, 0.25)
    sweep(t1, one, weight_one, 2, s1, 0, 2, 6, 2, 2, 0.25)
    clear_edges(ea, 16)
    clear_edges(eb, 16)

    def correct(x1, _):
        for half in range(2):
            x = 2 * x1 + half
            for r in range(4):
                for c in range(2):
                    ea[x, c, r, 8:32, :] = guess[x, c, r, 8:32, :] + one[x1, c, r // 2, 8:32, :]
        return 0

    lax.fori_loop(2, 6, correct, 0)
    sweep(ea, eb, weight, 0, source, 0, 5, 11, 4, 1, 1.0)
    sweep(eb, ea, weight, 0, source, 0, 6, 10, 4, 1, 1.0)
    blocks = []
    for c in range(2):
        for x in range(4):
            blocks.append(
                jnp.concatenate([first[x, c, r] + ea[x + 6, c, r, 16:24, :] for r in range(4)], axis=1)
            )
    values = jnp.concatenate(blocks, axis=0)
    result[...] = exact_dot(values, sort_matrix(512, 384, True)).reshape(2, 4, 8, 384)


def up_second(where, source_two, weight_two, near_low, near_high, own, source, weight, guess, weight_one, first):
    planes, groups = source_two.shape[0], source_two.shape[1]
    two = scratch(min(planes, WINDOW) + 8, 4, 16 + groups, 128)
    level, wide = scratch(8, 2, 2, 24, 128), scratch(8, 2, 2, 40, 128)
    return pl.pallas_call(
        lambda *refs: up_second_kernel(planes, groups, *refs),
        name="up_second",
        out_shape=shape(2, 4, 8, 384),
        in_specs=[SM] + [VM] * 10,
        out_specs=VM,
        scratch_shapes=[scratch(planes, 4, groups, 128), two, two, wide, level, wide, scratch(*WIDE), scratch(*WIDE)],
        compiler_params=PARAMS,
    )(where, source_two, weight_two, near_low, near_high, own, source, weight, guess, weight_one, first)


def shifted(block, axis, by):
    count = lax.axis_size(axis)
    pairs = [(i, i + by) for i in range(count) if 0 <= i + by < count]
    return lax.ppermute(block, axis, pairs)


def gather_two(row):
    count_y, count_x = lax.axis_size("gy"), lax.axis_size("gx")
    width = row.shape[0]
    sent = jnp.broadcast_to(row[None], (count_x * count_y, width, 384))
    got = lax.all_to_all(sent, ("gx", "gy"), 0, 0)
    return [got[:, n].reshape(count_x, count_y, 384) for n in range(width)]


def y_sides(block):
    return shifted(block, "gy", 1), shifted(block, "gy", -1)


def y_tiles(block):
    low, high = y_sides(block)
    return jnp.stack([low, block, high], axis=1)


def local(right_side, velocity_table, layer_index, absorb_level):
    where = jnp.stack([lax.axis_index("gx"), lax.axis_index("gy")]).astype(jnp.int32)
    packed, inverse_two = pack(velocity_table, right_side, layer_index, absorb_level)
    before, after = shifted(packed[2:], "gx", 2), shifted(packed[:2], "gx", -2)
    mid = jnp.concatenate(
        [before[1:], shifted(packed, "gx", 1), packed, shifted(packed, "gx", -1), after[:1]]
    )
    low, high = y_sides(mid)
    source, weight, diag, weight_one, diag_one, guess, one, two = down_first(before, mid, after, low, high)
    source_two, weight_two = gather_two(jnp.concatenate([two, inverse_two]))
    tiles = y_tiles(one)
    near_low, near_high = shifted(tiles[1:3], "gx", 1), shifted(tiles[1:3], "gx", -1)
    far_low, far_high = shifted(tiles[0:3], "gx", 2), shifted(tiles[1:4], "gx", -2)
    rest, first, weight_one_wide, rest_low, rest_high, weight_two = up_first(
        where, source_two, weight_two, near_low, near_high, far_low, far_high, tiles[1:3], source, weight, diag, guess
    )
    before, after = shifted(rest_low, "gx", 1), shifted(rest_high, "gx", -1)
    mid = jnp.concatenate([before[1:], rest, after[:5]])
    low, high = y_sides(mid)
    source, guess, one, two = down_second(before, mid, after, low, high, weight, diag, weight_one, diag_one)
    (source_two,) = gather_two(two)
    tiles = y_tiles(one)
    near_low, near_high = shifted(tiles[0:3], "gx", 1), shifted(tiles[1:4], "gx", -1)
    return up_second(
        where, source_two, weight_two, near_low, near_high, tiles[1:3], source, weight, guess, weight_one_wide, first
    )


def solution(mesh):
    placed = (P(None, "gx", "gy", None), P(), P("gx", "gy", None), P("gx", "gy", None))
    return jax.shard_map(
        local, mesh=mesh, in_specs=placed, out_specs=P(None, "gx", "gy", None), check_vma=False
    )
```

```python
import math
from types import SimpleNamespace

import jax
import jax.numpy as jnp
from jax import lax
from jax.experimental import pallas as pl
from jax.experimental.pallas import tpu as pltpu
from jax.sharding import PartitionSpec as P


NC = 8
WINDOW = 21
OMEGA = 0.6
BETA = 0.5
ABSORB = 0.25
KH_FACTOR = 2.0 * math.pi * 6.0 * 20.0

F32 = jnp.float32
BF16 = jnp.bfloat16
VM = pltpu.VMEM
SM = pltpu.SMEM
HB = pltpu.HBM
PARAMS = pltpu.CompilerParams(vmem_limit_bytes=32 * 1024 * 1024)


def run(name, kernel, inputs, outputs, scratch, copies):
    names = list(inputs) + list(outputs) + list(scratch) + ["sem"]
    result = pl.pallas_call(
        lambda *refs: kernel(SimpleNamespace(**dict(zip(names, refs)))),
        name=name,
        out_shape=tuple(jax.ShapeDtypeStruct(dims, F32) for dims, _ in outputs.values()),
        in_specs=[pl.BlockSpec(memory_space=space) for _, space in inputs.values()],
        out_specs=tuple(pl.BlockSpec(memory_space=space) for _, space in outputs.values()),
        scratch_shapes=[pltpu.VMEM(dims, F32) if isinstance(dims, tuple) else dims for dims in scratch.values()]
        + [pltpu.SemaphoreType.DMA((copies,))],
        compiler_params=PARAMS,
    )(*[array for array, _ in inputs.values()])
    return SimpleNamespace(**dict(zip(outputs, result)))


def sort_matrix(rows, columns, flip):
    first = lax.broadcasted_iota(jnp.int32, (rows, columns), 0)
    second = lax.broadcasted_iota(jnp.int32, (rows, columns), 1)
    if flip:
        first, second = second, first
    lane = second % 128
    hit = (first == 4 * lane + second // 128) & (lane < 96)
    return jnp.where(hit, 1.0, 0.0).astype(BF16)


def exact_dot(values, matrix):
    high = values.astype(BF16)
    rest = values - high.astype(F32)
    middle = rest.astype(BF16)
    low = (rest - middle.astype(F32)).astype(BF16)
    dot = lambda part: jnp.dot(part, matrix, preferred_element_type=F32)
    return (dot(low) + dot(middle)) + dot(high)


def scaled_inverse(real, imag, scale):
    diag_real = 6.0 * scale - real
    diag_imag = -imag
    factor = OMEGA / (diag_real * diag_real + diag_imag * diag_imag)
    factor = jnp.where(real > 0.0, factor, 0.0)
    return diag_real * factor, -diag_imag * factor


def product(a, b):
    return a[0] * b[0] - a[1] * b[1], a[0] * b[1] + a[1] * b[0]


def pair_rows(value, temp):
    temp[8:32, :] = value
    row = lax.broadcasted_iota(jnp.int32, (24, 128), 0)
    return value + jnp.where(row % 2 == 0, temp[9:33, :], temp[7:31, :])


def neighbour(ref, x, c, r, count, step):
    center = lambda s: ref[x, c, s, 8:32, :]
    up = center(r + 1) if r < count - 1 else pltpu.roll(center(0), 127, 1)
    down = center(r - 1) if r > 0 else pltpu.roll(center(count - 1), 1, 1)
    total = ref[x - 1, c, r, 8:32, :] + ref[x + 1, c, r, 8:32, :]
    total = total + ref[x, c, r, 8 - step : 32 - step, :] + ref[x, c, r, 8 + step : 32 + step, :]
    return total + (up + down)


def sweep(old, new, weight, weight_at, source, source_at, low, high, count, step, scale):
    def body(x, _):
        for r in range(count):
            parts = []
            for c in range(2):
                total = neighbour(old, x, c, r, count, step)
                if scale != 1.0:
                    total = total * scale
                parts.append(source[x + source_at, c, r] + total)
            w = [weight[x + weight_at, c, r] for c in range(2)]
            moved = product(w, parts)
            for c in range(2):
                new[x, c, r, 8:32, :] = (1.0 - OMEGA) * old[x, c, r, 8:32, :] + moved[c]
        return 0

    lax.fori_loop(low, high, body, 0)


def clear(ref, count):
    def body(x, _):
        ref[x] = jnp.zeros(ref.shape[1:], F32)
        return 0

    lax.fori_loop(0, count, body, 0)


def clear_edges(ref, count):
    zero = jnp.zeros((8, 128), F32)

    def body(x, _):
        for c in range(2):
            for r in range(ref.shape[2]):
                ref[x, c, r, 0:8, :] = zero
                ref[x, c, r, 32:40, :] = zero
        return 0

    lax.fori_loop(0, count, body, 0)


def dense(target, at, pieces):
    lane = lax.broadcasted_iota(jnp.int32, (1, 128), 1)
    for n in range(3):
        tail = pltpu.roll(pieces[n + 1], 128 - 32 * (n + 1), 1)
        head = pieces[n] if n == 0 else pltpu.roll(pieces[n], 128 - 32 * n, 1)
        target[0:1, at + n * 128 : at + n * 128 + 128] = jnp.where(lane < 96 - 32 * n, head, tail)


def loose(block):
    lane = lax.broadcasted_iota(jnp.int32, (block.shape[0], 128), 1)
    parts = [block[:, n * 128 : n * 128 + 128] for n in range(3)]
    result = []
    for k in range(4):
        if k == 0:
            value = parts[0]
        elif k == 3:
            value = pltpu.roll(parts[2], 96, 1)
        else:
            value = jnp.where(lane < 32 * k, pltpu.roll(parts[k - 1], 32 * k, 1), pltpu.roll(parts[k], 32 * k, 1))
        result.append(jnp.where(lane < 96, value, 0.0))
    return result


def pack_kernel(v):
    loads = [
        pltpu.make_async_copy(v.right_side, v.field, v.sem.at[0]),
        pltpu.make_async_copy(v.layer_index, v.layers, v.sem.at[1]),
        pltpu.make_async_copy(v.absorb_level, v.levels, v.sem.at[2]),
    ]
    for load in loads:
        load.start()
    matrix = sort_matrix(384, 512, False)
    for load in loads:
        load.wait()
    field = exact_dot(v.field[...].reshape(64, 384), matrix)
    both = jnp.concatenate([v.layers[...].reshape(32, 384), v.levels[...].reshape(32, 384)], axis=0)
    codes = jnp.dot(both.astype(F32).astype(BF16), matrix, preferred_element_type=F32)
    inside = lax.broadcasted_iota(jnp.int32, (32, 128), 1) < 96
    total = [jnp.zeros((32, 128), F32), jnp.zeros((32, 128), F32)]
    for r in range(4):
        lanes = slice(r * 128, r * 128 + 128)
        layer = codes[0:32, lanes]
        velocity = jnp.full((32, 128), v.table[0], F32)
        for n in range(1, v.table.shape[0]):
            velocity = jnp.where(layer == float(n), v.table[n], velocity)
        ratio = KH_FACTOR / velocity
        real = jnp.where(inside, ratio * ratio, 0.0)
        imag = -real * (BETA + ABSORB * codes[32:64, lanes])
        total = [total[0] + real, total[1] + imag]
        for x in range(4):
            rows = slice(x * 8, x * 8 + 8)
            values = (field[x * 8 : x * 8 + 8, lanes], field[32 + x * 8 : 40 + x * 8, lanes], real[rows], imag[rows])
            for c in range(4):
                v.packed[x, c, r] = values[c]
                if x < 2:
                    v.front[x, c, r] = values[c]
                else:
                    v.back[x - 2, c, r] = values[c]
    means = []
    for c in range(2):
        t = total[c]
        v.temp[c] = (t[0:8] + t[8:16]) + (t[16:24] + t[24:32])
        row = [v.temp[c, n : n + 1] for n in range(8)]
        means.append([((row[4 * k] + row[4 * k + 1]) + (row[4 * k + 2] + row[4 * k + 3])) * (1.0 / 64.0) for k in range(2)])
    w = [scaled_inverse(means[0][k], means[1][k], 0.0625) for k in range(2)]
    dense(v.inverse_two, 0, [w[k][c] for c in range(2) for k in range(2)])


def pack(table, right_side, layer_index, absorb_level):
    return run(
        "pack",
        pack_kernel,
        dict(table=(table, SM), right_side=(right_side, HB), layer_index=(layer_index, HB), absorb_level=(absorb_level, HB)),
        dict(packed=((4, 4, 4, 8, 128), VM), front=((2, 4, 4, 8, 128), VM), back=((2, 4, 4, 8, 128), VM),
             inverse_two=((1, 384), VM)),
        dict(field=right_side.shape, layers=pltpu.VMEM(layer_index.shape, jnp.int32),
             levels=pltpu.VMEM(absorb_level.shape, jnp.int32), temp=(2, 8, 128)),
        3,
    )


FINE = (16, 2, 4, 24, 128)
WIDE = (16, 2, 4, 40, 128)
COARSE = (6, 2, 2, 24, 128)
COARSE_WIDE = (6, 2, 2, 40, 128)


def keep(v, number, source, target):
    copy = pltpu.make_async_copy(source, target, v.sem.at[number])
    copy.start()
    return copy


def squeeze_rows(target, n, source, k, c, tile, top):
    for s in range(2):
        target[n, s * 4 : s * 4 + 4, :] = source[k, c, s, pl.ds(top + 8 * tile, 4, 2), :]


def down_body(v, source, weight, diag, weight_one, diag_one, first_copy, sends_weight):
    def first(x, _):
        for r in range(4):
            e = product([weight[x, c, r] for c in range(2)], [source[x, c, r] for c in range(2)])
            for c in range(2):
                v.start[x, c, r, 8:32, :] = e[c]
        return 0

    lax.fori_loop(0, 16, first, 0)
    sweep(v.start, v.guess, weight, 0, source, 0, 1, 15, 4, 1, 1.0)
    copies = [keep(v, first_copy, v.guess, v.out_guess)]

    def residual(k, _):
        for s in range(2):
            sums = [None, None]
            for half in range(2):
                x = 2 + 2 * k + half
                for r in (2 * s, 2 * s + 1):
                    e = [v.guess[x, c, r, 8:32, :] for c in range(2)]
                    moved = product([diag[x, c, r] for c in range(2)], e)
                    for c in range(2):
                        value = source[x, c, r] + neighbour(v.guess, x, c, r, 4, 1) - moved[c]
                        sums[c] = value if sums[c] is None else sums[c] + value
            g = [pair_rows(sums[c], v.temp.at[c]) * 0.125 for c in range(2)]
            e = product([weight_one[k, c, s] for c in range(2)], g)
            for c in range(2):
                v.source_one[k, c, s] = g[c]
                v.start_one[k, c, s, 8:32, :] = e[c]
        return 0

    lax.fori_loop(0, 6, residual, 0)
    copies.append(keep(v, first_copy + 1, v.source_one, v.out_source_one))
    sweep(v.start_one, v.guess_one, weight_one, 0, v.source_one, 0, 1, 5, 2, 2, 0.25)
    copies.append(keep(v, first_copy + 2, v.guess_one, v.out_guess_one))

    total = [None, None]
    for k in (2, 3):
        for s in range(2):
            e = [v.guess_one[k, c, s, 8:32, :] for c in range(2)]
            moved = product([diag_one[k, c, s] for c in range(2)], e)
            for c in range(2):
                value = v.source_one[k, c, s] + 0.25 * neighbour(v.guess_one, k, c, s, 2, 2) - moved[c]
                total[c] = value if total[c] is None else total[c] + value
    pieces = []
    for c in range(2):
        v.temp[c, 8:32, :] = total[c]
        for k in range(2):
            row = 16 + 4 * k
            pieces.append((v.temp[c, row : row + 1, :] + v.temp[c, row + 2 : row + 3, :]) * 0.125)
    dense(v.two, 0, pieces)

    for c in range(2):
        for k in range(4):
            squeeze_rows(v.send_y, k * 2 + c, v.guess_one, k + 1, c, 1, 8)
        for tile in range(3):
            for k in range(2):
                n = (k * 3 + tile) * 2 + c
                squeeze_rows(v.send_up, n, v.guess_one, k + 1, c, tile, 8)
                squeeze_rows(v.send_down, n, v.guess_one, k + 3, c, tile, 8)
        if sends_weight:
            for target, k in ((v.send_up, 1), (v.send_down, 4)):
                squeeze_rows(target, 12 + c, v.source_one, k, c, 1, 0)
                squeeze_rows(target, 14 + c, weight_one, k, c, 1, 0)
            squeeze_rows(v.send_far_up, c, v.guess_one, 2, c, 1, 8)
            squeeze_rows(v.send_far_down, c, v.guess_one, 3, c, 1, 8)
    return copies


def fill(v, target, at, count, x):
    for r in range(4):
        for c in range(count):
            target[x, c, r, 0:8, :] = v.low[x, at + c, r]
            target[x, c, r, 8:16, :] = v.mid[x, at + c, r]
            target[x, c, r, 16:24, :] = v.high[x, at + c, r]


def clear_down(v):
    clear_edges(v.start, 16)
    clear_edges(v.guess, 16)
    clear_edges(v.start_one, 6)
    clear_edges(v.guess_one, 6)


def down_first_kernel(v):
    clear_down(v)

    def filled(x, _):
        fill(v, v.source, 0, 2, x)
        fill(v, v.diag, 2, 2, x)
        for r in range(4):
            w = scaled_inverse(v.diag[x, 0, r], v.diag[x, 1, r], 1.0)
            for c in range(2):
                v.weight[x, c, r] = w[c]
        return 0

    lax.fori_loop(0, 16, filled, 0)
    copies = [keep(v, 0, v.source, v.out_source), keep(v, 1, v.weight, v.out_weight)]

    def coarse(k, _):
        for s in range(2):
            shift = []
            for c in range(2):
                total = None
                for half in range(2):
                    for r in (2 * s, 2 * s + 1):
                        value = v.diag[2 + 2 * k + half, c, r]
                        total = value if total is None else total + value
                shift.append(pair_rows(total, v.temp.at[c]) * 0.125)
            w = scaled_inverse(shift[0], shift[1], 0.25)
            d = (1.5 - shift[0], -shift[1])
            for c in range(2):
                v.weight_one[k, c, s] = w[c]
                v.diag_one[k, c, s] = d[c]
        return 0

    lax.fori_loop(0, 6, coarse, 0)

    def turn(x, _):
        for r in range(4):
            v.diag[x, 0, r] = 6.0 - v.diag[x, 0, r]
            v.diag[x, 1, r] = -v.diag[x, 1, r]
        return 0

    lax.fori_loop(0, 16, turn, 0)
    copies += [keep(v, 2, v.diag, v.out_diag), keep(v, 3, v.weight_one, v.out_weight_one),
               keep(v, 4, v.diag_one, v.out_diag_one)]
    copies += down_body(v, v.source, v.weight, v.diag, v.weight_one, v.diag_one, 5, True)
    v.two[0:1, 384:768] = v.inverse_two[...]
    for copy in copies:
        copy.wait()


def down_first(mid, low, high, inverse_two):
    return run(
        "down_first",
        down_first_kernel,
        dict(mid=(mid, VM), low=(low, VM), high=(high, VM), inverse_two=(inverse_two, VM)),
        dict(out_source=(FINE, HB), out_weight=(FINE, HB), out_diag=(FINE, HB), out_weight_one=(COARSE, HB),
             out_diag_one=(COARSE, HB), out_guess=(WIDE, HB), out_source_one=(COARSE, HB), out_guess_one=(COARSE_WIDE, HB),
             two=((1, 768), VM), send_y=((8, 8, 128), VM), send_up=((16, 8, 128), VM), send_down=((16, 8, 128), VM),
             send_far_up=((2, 8, 128), VM), send_far_down=((2, 8, 128), VM)),
        dict(source=FINE, weight=FINE, diag=FINE, weight_one=COARSE, diag_one=COARSE, start=WIDE, guess=WIDE,
             start_one=COARSE_WIDE, source_one=COARSE, guess_one=COARSE_WIDE, temp=(2, 40, 128)),
        8,
    )


def down_second_kernel(v):
    loads = [keep(v, 0, v.in_weight, v.weight), keep(v, 1, v.in_diag, v.diag),
             keep(v, 2, v.in_weight_one, v.weight_one), keep(v, 3, v.in_diag_one, v.diag_one)]
    clear_down(v)

    def filled(x, _):
        fill(v, v.source, 0, 2, x)
        return 0

    lax.fori_loop(0, 16, filled, 0)
    copies = [keep(v, 4, v.source, v.out_source)]
    for load in loads:
        load.wait()
    copies += down_body(v, v.source, v.weight, v.diag, v.weight_one, v.diag_one, 5, False)
    for copy in copies:
        copy.wait()


def down_second(mid, low, high, old):
    return run(
        "down_second",
        down_second_kernel,
        dict(mid=(mid, VM), low=(low, VM), high=(high, VM), in_weight=(old.out_weight, HB), in_diag=(old.out_diag, HB),
             in_weight_one=(old.out_weight_one, HB), in_diag_one=(old.out_diag_one, HB)),
        dict(out_source=(FINE, HB), out_guess=(WIDE, HB), out_source_one=(COARSE, HB), out_guess_one=(COARSE_WIDE, HB),
             two=((1, 384), VM), send_y=((8, 8, 128), VM), send_up=((12, 8, 128), VM), send_down=((12, 8, 128), VM)),
        dict(source=FINE, weight=FINE, diag=FINE, weight_one=COARSE, diag_one=COARSE, start=WIDE, guess=WIDE,
             start_one=COARSE_WIDE, source_one=COARSE, guess_one=COARSE_WIDE, temp=(2, 40, 128)),
        8,
    )


def unpack_two(packed, first, target, planes):
    def body(x, _):
        for k, part in enumerate(loose(packed[x, :, first : first + 384])):
            target[x, k] = part
        return 0

    lax.fori_loop(0, planes, body, 0)


def solve_two(begin, source, weight, ping, pong, window, groups):
    clear(ping, window + 8)
    clear(pong, window + 8)
    rows = slice(8, 8 + groups)
    block = next(b for b in (7, 4, 1) if window % b == 0)

    def over(body):
        def several(number, _):
            for n in range(block):
                body(number * block + n)
            return 0

        lax.fori_loop(0, window // block, several, 0)

    def start(x):
        for k in range(2):
            e = product([weight[begin + x, k], weight[begin + x, 2 + k]], [source[begin + x, k], source[begin + x, 2 + k]])
            for c in range(2):
                ping[x + 4, c * 2 + k, rows, :] = e[c]

    over(start)

    def step(old, new):
        def body(x):
            here = [old[x + 4, n, rows, :] for n in range(4)]
            for k in range(2):
                parts = []
                for c in range(2):
                    n, other = c * 2 + k, c * 2 + 1 - k
                    side = old[x + 4, other, 7 : 7 + groups, :] if k == 0 else old[x + 4, other, 9 : 9 + groups, :]
                    total = (old[x + 3, n, rows, :] + old[x + 5, n, rows, :]) + (here[other] + side)
                    total = total + (pltpu.roll(here[n], 1, 1) + pltpu.roll(here[n], 127, 1))
                    parts.append(source[begin + x, n] + 0.0625 * total)
                moved = product([weight[begin + x, k], weight[begin + x, 2 + k]], parts)
                for c in range(2):
                    new[x + 4, c * 2 + k, rows, :] = (1.0 - OMEGA) * here[c * 2 + k] + moved[c]

        over(body)

    pairs = (ping, pong)
    for number in range(NC - 1):
        step(pairs[number % 2], pairs[(number + 1) % 2])
    return pairs[(NC - 1) % 2]


def spread_rows(target, top, x, c, tile, block):
    for s in range(2):
        for twice in range(2):
            target[x, c, s, pl.ds(top + 8 * tile + twice, 4, 2), :] = block[s * 4 : s * 4 + 4, :]


def add_two(answer, gx, gy, one, first, count):
    row = lax.broadcasted_iota(jnp.int32, (8, 128), 0)
    for j in range(count):
        x = gx + 4 + (first + j) // 2
        for c in range(2):
            for tile in range(3):
                spot = gy + 7 + tile
                low = jnp.broadcast_to(answer[x, c * 2, pl.ds(spot, 1), :], (8, 128))
                high = jnp.broadcast_to(answer[x, c * 2 + 1, pl.ds(spot, 1), :], (8, 128))
                value = jnp.where(row < 4, low, high)
                at = slice(8 + 8 * tile, 16 + 8 * tile)
                for s in range(2):
                    one[j, c, s, at, :] = one[j, c, s, at, :] + value


def up_kernel(v, planes, groups, far):
    count = 8 + 2 * far
    loads = [keep(v, 0, v.in_source, v.source), keep(v, 1, v.in_weight, v.weight), keep(v, 2, v.in_guess, v.guess),
             keep(v, 3, v.in_guess_one, v.guess_one),
             keep(v, 4, v.in_source_one, v.source_one.at[2 * far : 6 + 2 * far]),
             keep(v, 5, v.in_weight_one, v.weight_one.at[2 * far : 6 + 2 * far])]
    if far:
        loads.append(keep(v, 6, v.in_diag, v.diag))
    else:
        loads.append(keep(v, 6, v.in_weight_two, v.weight_two))
        loads.append(keep(v, 7, v.in_first, v.first))
    window = min(planes, WINDOW)
    begin = jnp.clip(v.where[0] - 10, 0, planes - window)
    unpack_two(v.gathered, 0, v.source_two, planes)
    copies = []
    if far:
        unpack_two(v.gathered, 384, v.weight_two, planes)
        copies.append(keep(v, 7, v.weight_two, v.out_weight_two))
    else:
        loads[6].wait()
    answer = solve_two(begin, v.source_two, v.weight_two, v.ping, v.pong, window, groups)
    clear_edges(v.one, count)
    clear_edges(v.one_next, count)
    clear_edges(v.ea, 16)
    clear_edges(v.eb, 16)
    for load in loads[0:6]:
        load.wait()

    for k in range(4):
        for c in range(2):
            for s in range(2):
                v.one[k + 2 + far, c, s, 16:24, :] = v.guess_one[k + 1, c, s, 16:24, :]
            spread_rows(v.one, 8, k + 2 + far, c, 0, v.from_y_low[k * 2 + c])
            spread_rows(v.one, 8, k + 2 + far, c, 2, v.from_y_high[k * 2 + c])
    for c in range(2):
        for tile in range(3):
            for k in range(2):
                n = (k * 3 + tile) * 2 + c
                spread_rows(v.one, 8, far + k, c, tile, v.from_low[n])
                spread_rows(v.one, 8, 6 + far + k, c, tile, v.from_high[n])
    if far:
        zero = jnp.zeros((24, 128), F32)
        for c in range(2):
            for ref, edge, plane in ((v.from_low, v.from_far_low, 0), (v.from_high, v.from_far_high, 9)):
                inner = 1 if plane == 0 else 8
                for s in range(2):
                    v.one[plane, c, s, 8:32, :] = zero
                    v.source_one[inner, c, s] = zero
                    v.weight_one[inner, c, s] = zero
                spread_rows(v.one, 8, plane, c, 1, edge[c])
                spread_rows(v.source_one, 0, inner, c, 1, ref[12 + c])
                spread_rows(v.weight_one, 0, inner, c, 1, ref[14 + c])
    add_two(answer, v.where[0] - begin, v.where[1], v.one, -3 - far, count)
    shift = 0 if far else -1
    sweep(v.one, v.one_next, v.weight_one, shift, v.source_one, shift, 1, count - 1, 2, 2, 0.25)
    sweep(v.one_next, v.one, v.weight_one, shift, v.source_one, shift, 2, count - 2, 2, 2, 0.25)

    def correct(j, _):
        for half in range(2):
            x = 2 * (j - far) + half
            for r in range(4):
                for c in range(2):
                    v.ea[x, c, r, 8:32, :] = v.guess[x, c, r, 8:32, :] + v.one[j, c, r // 2, 8:32, :]
        return 0

    lax.fori_loop(2, count - 2, correct, 0)
    sweep(v.ea, v.eb, v.weight, 0, v.source, 0, 5 - far, 11 + far, 4, 1, 1.0)
    sweep(v.eb, v.ea, v.weight, 0, v.source, 0, 6 - far, 10 + far, 4, 1, 1.0)
    loads[6].wait() if far else loads[7].wait()
    return copies


def up_first_kernel(v, planes, groups):
    copies = up_kernel(v, planes, groups, 1)
    for x in range(4):
        for r in range(4):
            e = [v.ea[x + 6, c, r, 8:32, :] for c in range(2)]
            moved = product([v.diag[x + 6, c, r] for c in range(2)], e)
            for c in range(2):
                value = v.source[x + 6, c, r] + neighbour(v.ea, x + 6, c, r, 4, 1) - moved[c]
                v.packed[x, c, r] = value[8:16]
                if x < 2:
                    v.front[x, c, r] = value[8:16]
                else:
                    v.back[x - 2, c, r] = value[8:16]
                v.first[x, c, r] = e[c][8:16]
    copies.append(keep(v, 8, v.first, v.out_first))
    for copy in copies:
        copy.wait()


def up_second_kernel(v, planes, groups):
    up_kernel(v, planes, groups, 0)
    blocks = []
    for c in range(2):
        for x in range(4):
            blocks.append(
                jnp.concatenate([v.first[x, c, r] + v.ea[x + 6, c, r, 16:24, :] for r in range(4)], axis=1)
            )
    values = jnp.concatenate(blocks, axis=0)
    v.result[...] = exact_dot(values, sort_matrix(512, 384, True)).reshape(2, 4, 8, 384)


def up_scratch(planes, groups, far):
    level = (8 + 2 * far, 2, 2, 40, 128)
    source = (6 + 4 * far, 2, 2, 24, 128)
    two = (min(planes, WINDOW) + 8, 4, 16 + groups, 128)
    return dict(source=FINE, weight=FINE, guess=WIDE, guess_one=COARSE_WIDE, source_one=source, weight_one=source,
                source_two=(planes, 4, groups, 128), weight_two=(planes, 4, groups, 128), ping=two, pong=two,
                one=level, one_next=level, ea=WIDE, eb=WIDE, first=(4, 2, 4, 8, 128))


def up_inputs(where, gathered, messages, down, first_down):
    return dict(where=(where, SM), gathered=(gathered, VM), **{name: (array, VM) for name, array in messages.items()},
                in_source=(down.out_source, HB), in_weight=(first_down.out_weight, HB), in_guess=(down.out_guess, HB),
                in_guess_one=(down.out_guess_one, HB), in_source_one=(down.out_source_one, HB),
                in_weight_one=(first_down.out_weight_one, HB))


def up_first(where, gathered, messages, down):
    planes, groups = gathered.shape[0], gathered.shape[1]
    return run(
        "up_first",
        lambda v: up_first_kernel(v, planes, groups),
        dict(**up_inputs(where, gathered, messages, down, down), in_diag=(down.out_diag, HB)),
        dict(packed=((4, 2, 4, 8, 128), VM), front=((2, 2, 4, 8, 128), VM), back=((2, 2, 4, 8, 128), VM),
             out_first=((4, 2, 4, 8, 128), HB), out_weight_two=((planes, 4, groups, 128), HB)),
        dict(**up_scratch(planes, groups, 1), diag=FINE),
        9,
    )


def up_second(where, gathered, messages, down, first_down, first_up):
    planes, groups = gathered.shape[0], gathered.shape[1]
    return run(
        "up_second",
        lambda v: up_second_kernel(v, planes, groups),
        dict(**up_inputs(where, gathered, messages, down, first_down), in_weight_two=(first_up.out_weight_two, HB),
             in_first=(first_up.out_first, HB)),
        dict(result=((2, 4, 8, 384), VM)),
        up_scratch(planes, groups, 0),
        8,
    ).result


def shifted(block, axis, by):
    count = lax.axis_size(axis)
    pairs = [(i, i + by) for i in range(count) if 0 <= i + by < count]
    return lax.ppermute(block, axis, pairs)


def gather_two(row):
    count_y, count_x = lax.axis_size("gy"), lax.axis_size("gx")
    width = row.shape[1]
    sent = jnp.broadcast_to(row[None], (count_x * count_y, 1, width))
    return lax.all_to_all(sent, ("gx", "gy"), 0, 0).reshape(count_x, count_y, width)


def surround(own):
    mid = jnp.concatenate(
        [
            shifted(own.back, "gx", 2),
            shifted(own.packed, "gx", 1),
            own.packed,
            shifted(own.packed, "gx", -1),
            shifted(own.front, "gx", -2),
        ]
    )
    return mid, shifted(mid, "gy", 1), shifted(mid, "gy", -1)


def exchange_one(down):
    messages = dict(
        from_y_low=shifted(down.send_y, "gy", 1),
        from_y_high=shifted(down.send_y, "gy", -1),
        from_low=shifted(down.send_up, "gx", 1),
        from_high=shifted(down.send_down, "gx", -1),
    )
    if hasattr(down, "send_far_up"):
        messages["from_far_low"] = shifted(down.send_far_up, "gx", 2)
        messages["from_far_high"] = shifted(down.send_far_down, "gx", -2)
    return messages


def local(right_side, velocity_table, layer_index, absorb_level):
    where = jnp.stack([lax.axis_index("gx"), lax.axis_index("gy")]).astype(jnp.int32)
    packed = pack(velocity_table, right_side, layer_index, absorb_level)
    down = down_first(*surround(packed), packed.inverse_two)
    middle = up_first(where, gather_two(down.two), exchange_one(down), down)
    again = down_second(*surround(middle), down)
    return up_second(where, gather_two(again.two), exchange_one(again), again, down, middle)


def solution(mesh):
    placed = (P(None, "gx", "gy", None), P(), P("gx", "gy", None), P("gx", "gy", None))
    return jax.shard_map(
        local, mesh=mesh, in_specs=placed, out_specs=P(None, "gx", "gy", None), check_vma=False
    )
```

```python
import math
from types import SimpleNamespace

import jax
import jax.numpy as jnp
from jax import lax
from jax.experimental import pallas as pl
from jax.experimental.pallas import tpu as pltpu
from jax.sharding import PartitionSpec as P


NC = 8
WINDOW = 21
OMEGA = 0.6
BETA = 0.5
ABSORB = 0.25
KH_FACTOR = 2.0 * math.pi * 6.0 * 20.0

F32 = jnp.float32
BF16 = jnp.bfloat16
VM = pltpu.VMEM
SM = pltpu.SMEM
HB = pltpu.HBM
PARAMS = pltpu.CompilerParams(vmem_limit_bytes=32 * 1024 * 1024)


def run(name, kernel, inputs, outputs, scratch, copies):
    names = list(inputs) + list(outputs) + list(scratch) + ["sem"]
    result = pl.pallas_call(
        lambda *refs: kernel(SimpleNamespace(**dict(zip(names, refs)))),
        name=name,
        out_shape=tuple(HB(dims, F32) if space is HB else jax.ShapeDtypeStruct(dims, F32) for dims, space in outputs.values()),
        in_specs=[pl.BlockSpec(memory_space=space) for _, space in inputs.values()],
        out_specs=tuple(pl.BlockSpec(memory_space=space) for _, space in outputs.values()),
        scratch_shapes=[pltpu.VMEM(dims, F32) if isinstance(dims, tuple) else dims for dims in scratch.values()]
        + [pltpu.SemaphoreType.DMA((copies,))],
        compiler_params=PARAMS,
    )(*[pltpu.with_memory_space_constraint(array, HB) if space is HB else array for array, space in inputs.values()])
    return SimpleNamespace(**dict(zip(outputs, result)))


def sort_matrix(rows, columns, flip):
    first = lax.broadcasted_iota(jnp.int32, (rows, columns), 0)
    second = lax.broadcasted_iota(jnp.int32, (rows, columns), 1)
    if flip:
        first, second = second, first
    lane = second % 128
    hit = (first == 4 * lane + second // 128) & (lane < 96)
    return jnp.where(hit, 1.0, 0.0).astype(BF16)


def exact_dot(values, matrix):
    high = values.astype(BF16)
    rest = values - high.astype(F32)
    middle = rest.astype(BF16)
    low = (rest - middle.astype(F32)).astype(BF16)
    dot = lambda part: jnp.dot(part, matrix, preferred_element_type=F32)
    return (dot(low) + dot(middle)) + dot(high)


def scaled_inverse(real, imag, scale):
    diag_real = 6.0 * scale - real
    diag_imag = -imag
    factor = OMEGA / (diag_real * diag_real + diag_imag * diag_imag)
    factor = jnp.where(real > 0.0, factor, 0.0)
    return diag_real * factor, -diag_imag * factor


def product(a, b):
    return a[0] * b[0] - a[1] * b[1], a[0] * b[1] + a[1] * b[0]


def pair_rows(value, temp):
    temp[8:32, :] = value
    row = lax.broadcasted_iota(jnp.int32, (24, 128), 0)
    return value + jnp.where(row % 2 == 0, temp[9:33, :], temp[7:31, :])


def neighbour(ref, x, c, r, count, step, low=8, high=32):
    center = lambda s: ref[x, c, s, low:high, :]
    up = center(r + 1) if r < count - 1 else pltpu.roll(center(0), 127, 1)
    down = center(r - 1) if r > 0 else pltpu.roll(center(count - 1), 1, 1)
    total = ref[x - 1, c, r, low:high, :] + ref[x + 1, c, r, low:high, :]
    total = total + ref[x, c, r, low - step : high - step, :] + ref[x, c, r, low + step : high + step, :]
    return total + (up + down)


def sweep(old, new, weight, weight_at, source, source_at, low, high, count, step, scale):
    def body(x, _):
        for r in range(count):
            parts = []
            for c in range(2):
                total = neighbour(old, x, c, r, count, step)
                if scale != 1.0:
                    total = total * scale
                parts.append(source[x + source_at, c, r] + total)
            w = [weight[x + weight_at, c, r] for c in range(2)]
            moved = product(w, parts)
            for c in range(2):
                new[x, c, r, 8:32, :] = (1.0 - OMEGA) * old[x, c, r, 8:32, :] + moved[c]
        return 0

    lax.fori_loop(low, high, body, 0)


def clear(ref, count):
    def body(x, _):
        ref[x] = jnp.zeros(ref.shape[1:], F32)
        return 0

    lax.fori_loop(0, count, body, 0)


def clear_edges(ref, count):
    zero = jnp.zeros((8, 128), F32)

    def body(x, _):
        for c in range(2):
            for r in range(ref.shape[2]):
                ref[x, c, r, 0:8, :] = zero
                ref[x, c, r, 32:40, :] = zero
        return 0

    lax.fori_loop(0, count, body, 0)


def dense(parts):
    lane = lax.broadcasted_iota(jnp.int32, parts[0].shape, 1)
    result = []
    for n in range(3):
        head = parts[0] if n == 0 else pltpu.roll(parts[n], 128 - 32 * n, 1)
        result.append(jnp.where(lane < 96 - 32 * n, head, pltpu.roll(parts[n + 1], 96 - 32 * n, 1)))
    return result


def loose(parts, clean):
    lane = lax.broadcasted_iota(jnp.int32, parts[0].shape, 1)
    result = [parts[0]]
    for k in (1, 2):
        result.append(jnp.where(lane < 32 * k, pltpu.roll(parts[k - 1], 32 * k, 1), pltpu.roll(parts[k], 32 * k, 1)))
    result.append(pltpu.roll(parts[2], 96, 1))
    return [jnp.where(lane < 96, value, 0.0) for value in result] if clean else result


def put_dense(v, x, c, parts):
    for n, tile in enumerate(dense(parts)):
        v.packed[x, c, n] = tile
        if x < 2:
            v.front[x, c, n] = tile
        else:
            v.back[x - 2, c, n] = tile


def pack_kernel(v):
    loads = [
        pltpu.make_async_copy(v.right_side, v.field, v.sem.at[0]),
        pltpu.make_async_copy(v.layer_index, v.layers, v.sem.at[1]),
        pltpu.make_async_copy(v.absorb_level, v.levels, v.sem.at[2]),
        pltpu.make_async_copy(v.speeds, v.table, v.sem.at[3]),
    ]
    for load in loads:
        load.start()
    matrix = sort_matrix(384, 512, False)
    for load in loads:
        load.wait()
    field = exact_dot(v.field[...].reshape(64, 384), matrix)
    both = jnp.concatenate([v.layers[...].reshape(32, 384), v.levels[...].reshape(32, 384)], axis=0)
    codes = jnp.dot(both.astype(F32).astype(BF16), matrix, preferred_element_type=F32)
    inside = lax.broadcasted_iota(jnp.int32, (32, 128), 1) < 96
    total = [jnp.zeros((32, 128), F32), jnp.zeros((32, 128), F32)]
    reals, imags = [], []
    for r in range(4):
        lanes = slice(r * 128, r * 128 + 128)
        layer = codes[0:32, lanes]
        velocity = jnp.full((32, 128), v.table[0], F32)
        for n in range(1, v.table.shape[0]):
            velocity = jnp.where(layer == float(n), v.table[n], velocity)
        ratio = KH_FACTOR / velocity
        real = jnp.where(inside, ratio * ratio, 0.0)
        imag = -real * (BETA + ABSORB * codes[32:64, lanes])
        total = [total[0] + real, total[1] + imag]
        reals.append(real)
        imags.append(imag)
    for x in range(4):
        rows = slice(x * 8, x * 8 + 8)
        for c in range(2):
            at = 32 * c + x * 8
            put_dense(v, x, c, [field[at : at + 8, r * 128 : r * 128 + 128] for r in range(4)])
        put_dense(v, x, 2, [reals[r][rows] for r in range(4)])
        put_dense(v, x, 3, [imags[r][rows] for r in range(4)])
    means = []
    for c in range(2):
        t = total[c]
        v.temp[c] = (t[0:8] + t[8:16]) + (t[16:24] + t[24:32])
        row = [v.temp[c, n : n + 1] for n in range(8)]
        means.append([((row[4 * k] + row[4 * k + 1]) + (row[4 * k + 2] + row[4 * k + 3])) * (1.0 / 64.0) for k in range(2)])
    w = [scaled_inverse(means[0][k], means[1][k], 0.0625) for k in range(2)]
    v.inverse_two[...] = jnp.concatenate(dense([w[k][c] for c in range(2) for k in range(2)]), axis=1)


def pack(table, right_side, layer_index, absorb_level):
    return run(
        "pack",
        pack_kernel,
        dict(speeds=(table, HB), right_side=(right_side, HB), layer_index=(layer_index, HB), absorb_level=(absorb_level, HB)),
        dict(packed=((4, 4, 3, 8, 128), VM), front=((2, 4, 3, 8, 128), VM), back=((2, 4, 3, 8, 128), VM),
             inverse_two=((1, 384), VM)),
        dict(field=right_side.shape, layers=pltpu.VMEM(layer_index.shape, jnp.int32),
             levels=pltpu.VMEM(absorb_level.shape, jnp.int32), table=pltpu.SMEM(table.shape, F32), temp=(2, 8, 128)),
        4,
    )


FINE = (16, 2, 4, 24, 128)
WIDE = (16, 2, 4, 40, 128)
PART = (8, 2, 4, 24, 128)
INNER = (12, 2, 4, 24, 128)
COARSE = (6, 2, 2, 24, 128)
COARSE_WIDE = (6, 2, 2, 40, 128)


def keep(v, number, source, target):
    copy = pltpu.make_async_copy(source, target, v.sem.at[number])
    copy.start()
    return copy


def squeeze_rows(target, n, source, k, c, tile, top):
    for s in range(2):
        target[n, s * 4 : s * 4 + 4, :] = source[k, c, s, pl.ds(top + 8 * tile, 4, 2), :]


def down_body(v, source, weight, diag, weight_one, diag_one, first_copy, sends_weight):
    def first(x, _):
        for r in range(4):
            e = product([weight[x, c, r] for c in range(2)], [source[x, c, r] for c in range(2)])
            for c in range(2):
                v.start[x, c, r, 8:32, :] = e[c]
        return 0

    lax.fori_loop(0, 16, first, 0)
    sweep(v.start, v.guess, weight, 0, source, 0, 1, 15, 4, 1, 1.0)
    copies = [keep(v, first_copy, v.guess.at[2:14, :, :, 8:32, :], v.out_guess)]

    def residual(k, _):
        for s in range(2):
            sums = [None, None]
            for half in range(2):
                x = 2 + 2 * k + half
                for r in (2 * s, 2 * s + 1):
                    e = [v.guess[x, c, r, 8:32, :] for c in range(2)]
                    moved = product([diag[x, c, r] for c in range(2)], e)
                    for c in range(2):
                        value = source[x, c, r] + neighbour(v.guess, x, c, r, 4, 1) - moved[c]
                        sums[c] = value if sums[c] is None else sums[c] + value
            g = [pair_rows(sums[c], v.temp.at[c]) * 0.125 for c in range(2)]
            e = product([weight_one[k, c, s] for c in range(2)], g)
            for c in range(2):
                v.source_one[k, c, s] = g[c]
                v.start_one[k, c, s, 8:32, :] = e[c]
        return 0

    lax.fori_loop(0, 6, residual, 0)
    copies.append(keep(v, first_copy + 1, v.source_one, v.out_source_one))
    sweep(v.start_one, v.guess_one, weight_one, 0, v.source_one, 0, 1, 5, 2, 2, 0.25)
    copies.append(keep(v, first_copy + 2, v.guess_one, v.out_guess_one))

    total = [None, None]
    for k in (2, 3):
        for s in range(2):
            e = [v.guess_one[k, c, s, 8:32, :] for c in range(2)]
            moved = product([diag_one[k, c, s] for c in range(2)], e)
            for c in range(2):
                value = v.source_one[k, c, s] + 0.25 * neighbour(v.guess_one, k, c, s, 2, 2) - moved[c]
                total[c] = value if total[c] is None else total[c] + value
    pieces = []
    for c in range(2):
        v.temp[c, 8:32, :] = total[c]
        for k in range(2):
            row = 16 + 4 * k
            pieces.append((v.temp[c, row : row + 1, :] + v.temp[c, row + 2 : row + 3, :]) * 0.125)
    for n, tile in enumerate(dense(pieces)):
        v.two[0:1, n * 128 : n * 128 + 128] = tile

    for c in range(2):
        for k in range(4):
            squeeze_rows(v.send_y, k * 2 + c, v.guess_one, k + 1, c, 1, 8)
        for tile in range(3):
            for k in range(2):
                n = (k * 3 + tile) * 2 + c
                squeeze_rows(v.send_up, n, v.guess_one, k + 1, c, tile, 8)
                squeeze_rows(v.send_down, n, v.guess_one, k + 3, c, tile, 8)
        if sends_weight:
            for target, k in ((v.send_up, 1), (v.send_down, 4)):
                squeeze_rows(target, 12 + c, v.source_one, k, c, 1, 0)
                squeeze_rows(target, 14 + c, weight_one, k, c, 1, 0)
            squeeze_rows(v.send_far_up, c, v.guess_one, 2, c, 1, 8)
            squeeze_rows(v.send_far_down, c, v.guess_one, 3, c, 1, 8)
    return copies


def fill(v, target, at, count, x):
    for c in range(count):
        for tile, ref in enumerate((v.low, v.mid, v.high)):
            parts = loose([ref[x, at + c, n] for n in range(3)], at + c == 2)
            for r in range(4):
                target[x, c, r, 8 * tile : 8 * tile + 8, :] = parts[r]


def clear_down(v):
    clear_edges(v.start, 16)
    clear_edges(v.guess, 16)
    clear_edges(v.start_one, 6)
    clear_edges(v.guess_one, 6)


def down_first_kernel(v):
    clear_down(v)

    def filled(x, _):
        fill(v, v.source, 0, 2, x)
        fill(v, v.diag, 2, 2, x)
        for r in range(4):
            w = scaled_inverse(v.diag[x, 0, r], v.diag[x, 1, r], 1.0)
            for c in range(2):
                v.weight[x, c, r] = w[c]
        return 0

    lax.fori_loop(0, 16, filled, 0)
    copies = [keep(v, 0, v.source.at[4:12], v.out_source), keep(v, 1, v.weight, v.out_weight)]

    def coarse(k, _):
        for s in range(2):
            shift = []
            for c in range(2):
                total = None
                for half in range(2):
                    for r in (2 * s, 2 * s + 1):
                        value = v.diag[2 + 2 * k + half, c, r]
                        total = value if total is None else total + value
                shift.append(pair_rows(total, v.temp.at[c]) * 0.125)
            w = scaled_inverse(shift[0], shift[1], 0.25)
            d = (1.5 - shift[0], -shift[1])
            for c in range(2):
                v.weight_one[k, c, s] = w[c]
                v.diag_one[k, c, s] = d[c]
        return 0

    lax.fori_loop(0, 6, coarse, 0)

    def turn(x, _):
        for r in range(4):
            v.diag[x, 0, r] = 6.0 - v.diag[x, 0, r]
            v.diag[x, 1, r] = -v.diag[x, 1, r]
        return 0

    lax.fori_loop(0, 16, turn, 0)
    copies += [keep(v, 2, v.diag.at[2:14], v.out_diag), keep(v, 3, v.weight_one, v.out_weight_one),
               keep(v, 4, v.diag_one, v.out_diag_one)]
    copies += down_body(v, v.source, v.weight, v.diag, v.weight_one, v.diag_one, 5, True)
    v.two[0:1, 384:768] = v.inverse_two[...]
    for copy in copies:
        copy.wait()


def down_first(mid, low, high, inverse_two):
    return run(
        "down_first",
        down_first_kernel,
        dict(mid=(mid, VM), low=(low, VM), high=(high, VM), inverse_two=(inverse_two, VM)),
        dict(out_source=(PART, HB), out_weight=(FINE, HB), out_diag=(INNER, HB), out_weight_one=(COARSE, HB),
             out_diag_one=(COARSE, HB), out_guess=(INNER, HB), out_source_one=(COARSE, HB), out_guess_one=(COARSE_WIDE, HB),
             two=((1, 768), VM), send_y=((8, 8, 128), VM), send_up=((16, 8, 128), VM), send_down=((16, 8, 128), VM),
             send_far_up=((2, 8, 128), VM), send_far_down=((2, 8, 128), VM)),
        dict(source=FINE, weight=FINE, diag=FINE, weight_one=COARSE, diag_one=COARSE, start=WIDE, guess=WIDE,
             start_one=COARSE_WIDE, source_one=COARSE, guess_one=COARSE_WIDE, temp=(2, 40, 128)),
        8,
    )


def down_second_kernel(v):
    loads = [keep(v, 0, v.in_weight, v.weight), keep(v, 1, v.in_diag, v.diag.at[2:14]),
             keep(v, 2, v.in_weight_one, v.weight_one), keep(v, 3, v.in_diag_one, v.diag_one)]
    clear_down(v)

    def filled(x, _):
        fill(v, v.source, 0, 2, x)
        return 0

    lax.fori_loop(0, 16, filled, 0)
    copies = [keep(v, 4, v.source.at[4:12], v.out_source)]
    for load in loads:
        load.wait()
    copies += down_body(v, v.source, v.weight, v.diag, v.weight_one, v.diag_one, 5, False)
    for copy in copies:
        copy.wait()


def down_second(mid, low, high, old):
    return run(
        "down_second",
        down_second_kernel,
        dict(mid=(mid, VM), low=(low, VM), high=(high, VM), in_weight=(old.out_weight, HB), in_diag=(old.out_diag, HB),
             in_weight_one=(old.out_weight_one, HB), in_diag_one=(old.out_diag_one, HB)),
        dict(out_source=(PART, HB), out_guess=(INNER, HB), out_source_one=(COARSE, HB), out_guess_one=(COARSE_WIDE, HB),
             two=((1, 384), VM), send_y=((8, 8, 128), VM), send_up=((12, 8, 128), VM), send_down=((12, 8, 128), VM)),
        dict(source=FINE, weight=FINE, diag=FINE, weight_one=COARSE, diag_one=COARSE, start=WIDE, guess=WIDE,
             start_one=COARSE_WIDE, source_one=COARSE, guess_one=COARSE_WIDE, temp=(2, 40, 128)),
        8,
    )


def over(low, count, block, body):
    def several(number, _):
        for n in range(block):
            body(low + number * block + n)
        return 0

    lax.fori_loop(0, count // block, several, 0)
    for n in range(count - count % block, count):
        body(low + n)


def unpack_two(packed, first, begin, target, window, clean):
    def body(x):
        parts = [packed[begin + x, :, first + n * 128 : first + n * 128 + 128] for n in range(3)]
        for k, part in enumerate(loose(parts, clean)):
            target[x, k] = part

    over(0, window, 7, body)


def solve_two(own, source, weight, ping, pong, window, planes, groups):
    clear(ping, window + 8)
    clear(pong, window + 8)
    rows = slice(8, 8 + groups)

    def start(x):
        for k in range(2):
            e = product([weight[x, k], weight[x, 2 + k]], [source[x, k], source[x, 2 + k]])
            for c in range(2):
                ping[x + 4, c * 2 + k, rows, :] = e[c]

    over(0, window, 7, start)

    def step(old, new, left):
        def body(x):
            here = [old[x + 4, n, rows, :] for n in range(4)]
            for k in range(2):
                parts = []
                for c in range(2):
                    n, other = c * 2 + k, c * 2 + 1 - k
                    side = old[x + 4, other, 7 : 7 + groups, :] if k == 0 else old[x + 4, other, 9 : 9 + groups, :]
                    total = (old[x + 3, n, rows, :] + old[x + 5, n, rows, :]) + (here[other] + side)
                    total = total + (pltpu.roll(here[n], 1, 1) + pltpu.roll(here[n], 127, 1))
                    parts.append(source[x, n] + 0.0625 * total)
                moved = product([weight[x, k], weight[x, 2 + k]], parts)
                for c in range(2):
                    new[x + 4, c * 2 + k, rows, :] = (1.0 - OMEGA) * here[c * 2 + k] + moved[c]

        count = min(window, 2 * (3 + left) + 1)
        over(jnp.clip(own - 3 - left, 0, window - count), count, 4, body)

    pairs = (ping, pong)
    for number in range(NC - 1):
        step(pairs[number % 2], pairs[(number + 1) % 2], NC - 2 - number)
    return pairs[(NC - 1) % 2]


def spread_rows(target, top, x, c, tile, block):
    for s in range(2):
        for twice in range(2):
            target[x, c, s, pl.ds(top + 8 * tile + twice, 4, 2), :] = block[s * 4 : s * 4 + 4, :]


def add_two(answer, gx, gy, one, first, count):
    row = lax.broadcasted_iota(jnp.int32, (8, 128), 0)
    for j in range(count):
        x = gx + 4 + (first + j) // 2
        for c in range(2):
            for tile in range(3):
                spot = gy + 7 + tile
                low = jnp.broadcast_to(answer[x, c * 2, pl.ds(spot, 1), :], (8, 128))
                high = jnp.broadcast_to(answer[x, c * 2 + 1, pl.ds(spot, 1), :], (8, 128))
                value = jnp.where(row < 4, low, high)
                at = slice(8 + 8 * tile, 16 + 8 * tile)
                for s in range(2):
                    one[j, c, s, at, :] = one[j, c, s, at, :] + value


def up_kernel(v, planes, groups, far):
    count = 8 + 2 * far
    loads = []
    if not far:
        loads.append(keep(v, 7, v.in_weight_two, v.weight_two))
    loads += [keep(v, 0, v.in_source, v.source.at[4:12]), keep(v, 1, v.in_weight.at[4:12], v.weight.at[4:12]),
              keep(v, 2, v.in_guess, v.guess.at[2:14]), keep(v, 3, v.in_guess_one, v.guess_one),
              keep(v, 4, v.in_source_one, v.source_one.at[2 * far : 6 + 2 * far]),
              keep(v, 5, v.in_weight_one, v.weight_one.at[2 * far : 6 + 2 * far])]
    if far:
        loads.append(keep(v, 6, v.in_diag.at[4:8], v.diag.at[6:10]))
    else:
        loads.append(keep(v, 6, v.in_first, v.first))
        v.matrix[...] = sort_matrix(512, 384, True)
    window = min(planes, WINDOW)
    begin = jnp.clip(v.where[0] - 10, 0, planes - window)
    unpack_two(v.gathered, 0, begin, v.source_two, window, False)
    copies = []
    if far:
        unpack_two(v.gathered, 384, begin, v.weight_two, window, True)
        copies.append(keep(v, 7, v.weight_two, v.out_weight_two))
    else:
        loads.pop(0).wait()
    answer = solve_two(v.where[0] - begin, v.source_two, v.weight_two, v.ping, v.pong, window, planes, groups)
    clear_edges(v.one, count)
    clear_edges(v.one_next, count)
    clear_edges(v.ea, 16)
    clear_edges(v.eb, 16)
    for load in loads:
        load.wait()

    for k in range(4):
        for c in range(2):
            for s in range(2):
                v.one[k + 2 + far, c, s, 16:24, :] = v.guess_one[k + 1, c, s, 16:24, :]
            spread_rows(v.one, 8, k + 2 + far, c, 0, v.from_y_low[k * 2 + c])
            spread_rows(v.one, 8, k + 2 + far, c, 2, v.from_y_high[k * 2 + c])
    for c in range(2):
        for tile in range(3):
            for k in range(2):
                n = (k * 3 + tile) * 2 + c
                spread_rows(v.one, 8, far + k, c, tile, v.from_low[n])
                spread_rows(v.one, 8, 6 + far + k, c, tile, v.from_high[n])
    if far:
        zero = jnp.zeros((24, 128), F32)
        for c in range(2):
            for ref, edge, plane in ((v.from_low, v.from_far_low, 0), (v.from_high, v.from_far_high, 9)):
                inner = 1 if plane == 0 else 8
                for s in range(2):
                    v.one[plane, c, s, 8:32, :] = zero
                    v.source_one[inner, c, s] = zero
                    v.weight_one[inner, c, s] = zero
                spread_rows(v.one, 8, plane, c, 1, edge[c])
                spread_rows(v.source_one, 0, inner, c, 1, ref[12 + c])
                spread_rows(v.weight_one, 0, inner, c, 1, ref[14 + c])
    add_two(answer, v.where[0] - begin, v.where[1], v.one, -3 - far, count)
    shift = 0 if far else -1
    sweep(v.one, v.one_next, v.weight_one, shift, v.source_one, shift, 1, count - 1, 2, 2, 0.25)
    sweep(v.one_next, v.one, v.weight_one, shift, v.source_one, shift, 2, count - 2, 2, 2, 0.25)

    def correct(j, _):
        for half in range(2):
            x = 2 * (j - far) + half
            for r in range(4):
                for c in range(2):
                    v.ea[x, c, r, 8:32, :] = v.guess[x, c, r] + v.one[j, c, r // 2, 8:32, :]
        return 0

    lax.fori_loop(2, count - 2, correct, 0)
    sweep(v.ea, v.eb, v.weight, 0, v.source, 0, 5 - far, 11 + far, 4, 1, 1.0)
    sweep(v.eb, v.ea, v.weight, 0, v.source, 0, 6 - far, 10 + far, 4, 1, 1.0)
    return copies


def up_first_kernel(v, planes, groups):
    copies = up_kernel(v, planes, groups, 1)
    for x in range(4):
        values = [[], []]
        for r in range(4):
            e = [v.ea[x + 6, c, r, 16:24, :] for c in range(2)]
            moved = product([v.diag[x + 6, c, r, 8:16, :] for c in range(2)], e)
            for c in range(2):
                total = neighbour(v.ea, x + 6, c, r, 4, 1, 16, 24)
                values[c].append(v.source[x + 6, c, r, 8:16, :] + total - moved[c])
                v.first[x, c, r] = e[c]
        for c in range(2):
            put_dense(v, x, c, values[c])
    copies.append(keep(v, 8, v.first, v.out_first))
    for copy in copies:
        copy.wait()


def up_second_kernel(v, planes, groups):
    up_kernel(v, planes, groups, 0)
    blocks = []
    for c in range(2):
        for x in range(4):
            blocks.append(
                jnp.concatenate([v.first[x, c, r] + v.ea[x + 6, c, r, 16:24, :] for r in range(4)], axis=1)
            )
    values = jnp.concatenate(blocks, axis=0)
    v.result[...] = exact_dot(values, v.matrix[...]).reshape(2, 4, 8, 384)


def up_scratch(planes, groups, far):
    level = (8 + 2 * far, 2, 2, 40, 128)
    source = (6 + 4 * far, 2, 2, 24, 128)
    two = (min(planes, WINDOW) + 8, 4, 16 + groups, 128)
    return dict(source=FINE, weight=FINE, guess=FINE, guess_one=COARSE_WIDE, source_one=source, weight_one=source,
                source_two=(min(planes, WINDOW), 4, groups, 128),
                weight_two=(min(planes, WINDOW), 4, groups, 128), ping=two, pong=two,
                one=level, one_next=level, ea=WIDE, eb=WIDE, first=(4, 2, 4, 8, 128))


def up_inputs(where, gathered, messages, down, first_down):
    return dict(where=(where, SM), gathered=(gathered, VM), **{name: (array, VM) for name, array in messages.items()},
                in_source=(down.out_source, HB), in_weight=(first_down.out_weight, HB), in_guess=(down.out_guess, HB),
                in_guess_one=(down.out_guess_one, HB), in_source_one=(down.out_source_one, HB),
                in_weight_one=(first_down.out_weight_one, HB))


def up_first(where, gathered, messages, down):
    planes, groups = gathered.shape[0], gathered.shape[1]
    return run(
        "up_first",
        lambda v: up_first_kernel(v, planes, groups),
        dict(**up_inputs(where, gathered, messages, down, down), in_diag=(down.out_diag, HB)),
        dict(packed=((4, 2, 3, 8, 128), VM), front=((2, 2, 3, 8, 128), VM), back=((2, 2, 3, 8, 128), VM),
             out_first=((4, 2, 4, 8, 128), HB), out_weight_two=((min(planes, WINDOW), 4, groups, 128), HB)),
        dict(**up_scratch(planes, groups, 1), diag=FINE),
        9,
    )


def up_second(where, gathered, messages, down, first_down, first_up):
    planes, groups = gathered.shape[0], gathered.shape[1]
    return run(
        "up_second",
        lambda v: up_second_kernel(v, planes, groups),
        dict(**up_inputs(where, gathered, messages, down, first_down), in_weight_two=(first_up.out_weight_two, HB),
             in_first=(first_up.out_first, HB)),
        dict(result=((2, 4, 8, 384), VM)),
        dict(**up_scratch(planes, groups, 0), matrix=pltpu.VMEM((512, 384), BF16)),
        8,
    ).result


def shifted(block, axis, by):
    count = lax.axis_size(axis)
    pairs = [(i, i + by) for i in range(count) if 0 <= i + by < count]
    return lax.ppermute(block, axis, pairs)


def gather_two(row):
    count_y, count_x = lax.axis_size("gy"), lax.axis_size("gx")
    width = row.shape[1]
    sent = jnp.broadcast_to(row[None], (count_x * count_y, 1, width))
    return lax.all_to_all(sent, ("gx", "gy"), 0, 0).reshape(count_x, count_y, width)


def surround(own):
    mid = jnp.concatenate(
        [
            shifted(own.back, "gx", 2),
            shifted(own.packed, "gx", 1),
            own.packed,
            shifted(own.packed, "gx", -1),
            shifted(own.front, "gx", -2),
        ]
    )
    return mid, shifted(mid, "gy", 1), shifted(mid, "gy", -1)


def exchange_one(down):
    messages = dict(
        from_y_low=shifted(down.send_y, "gy", 1),
        from_y_high=shifted(down.send_y, "gy", -1),
        from_low=shifted(down.send_up, "gx", 1),
        from_high=shifted(down.send_down, "gx", -1),
    )
    if hasattr(down, "send_far_up"):
        messages["from_far_low"] = shifted(down.send_far_up, "gx", 2)
        messages["from_far_high"] = shifted(down.send_far_down, "gx", -2)
    return messages


def local(right_side, velocity_table, layer_index, absorb_level):
    where = jnp.stack([lax.axis_index("gx"), lax.axis_index("gy")]).astype(jnp.int32)
    packed = pack(velocity_table, right_side, layer_index, absorb_level)
    down = down_first(*surround(packed), packed.inverse_two)
    middle = up_first(where, gather_two(down.two), exchange_one(down), down)
    again = down_second(*surround(middle), down)
    return up_second(where, gather_two(again.two), exchange_one(again), again, down, middle)


def solution(mesh):
    placed = (P(None, "gx", "gy", None), P(), P("gx", "gy", None), P("gx", "gy", None))
    return jax.shard_map(
        local, mesh=mesh, in_specs=placed, out_specs=P(None, "gx", "gy", None), check_vma=False
    )
```

```python
import math
from types import SimpleNamespace

import jax
import jax.numpy as jnp
from jax import lax
from jax.experimental import pallas as pl
from jax.experimental.pallas import tpu as pltpu
from jax.sharding import PartitionSpec as P


NC = 8
WINDOW = 21
OMEGA = 0.6
BETA = 0.5
ABSORB = 0.25
KH_FACTOR = 2.0 * math.pi * 6.0 * 20.0

F32 = jnp.float32
BF16 = jnp.bfloat16
VM = pltpu.VMEM
SM = pltpu.SMEM
HB = pltpu.HBM
PARAMS = pltpu.CompilerParams(vmem_limit_bytes=32 * 1024 * 1024)


def run(name, kernel, inputs, outputs, scratch, copies):
    names = list(inputs) + list(outputs) + list(scratch) + ["sem"]
    result = pl.pallas_call(
        lambda *refs: kernel(SimpleNamespace(**dict(zip(names, refs)))),
        name=name,
        out_shape=tuple(HB(dims, F32) if space is HB else jax.ShapeDtypeStruct(dims, F32) for dims, space in outputs.values()),
        in_specs=[pl.BlockSpec(memory_space=space) for _, space in inputs.values()],
        out_specs=tuple(pl.BlockSpec(memory_space=space) for _, space in outputs.values()),
        scratch_shapes=[pltpu.VMEM(dims, F32) if isinstance(dims, tuple) else dims for dims in scratch.values()]
        + [pltpu.SemaphoreType.DMA((copies,))],
        compiler_params=PARAMS,
    )(*[pltpu.with_memory_space_constraint(array, HB) if space is HB else array for array, space in inputs.values()])
    return SimpleNamespace(**dict(zip(outputs, result)))


def sort_matrix(rows, columns, flip):
    first = lax.broadcasted_iota(jnp.int32, (rows, columns), 0)
    second = lax.broadcasted_iota(jnp.int32, (rows, columns), 1)
    if flip:
        first, second = second, first
    lane = second % 128
    hit = (first == 4 * lane + second // 128) & (lane < 96)
    return jnp.where(hit, 1.0, 0.0).astype(BF16)


def exact_dot(values, matrix):
    high = values.astype(BF16)
    rest = values - high.astype(F32)
    middle = rest.astype(BF16)
    low = (rest - middle.astype(F32)).astype(BF16)
    dot = lambda part: jnp.dot(part, matrix, preferred_element_type=F32)
    return (dot(low) + dot(middle)) + dot(high)


def scaled_inverse(real, imag, scale):
    diag_real = 6.0 * scale - real
    diag_imag = -imag
    factor = OMEGA / (diag_real * diag_real + diag_imag * diag_imag)
    factor = jnp.where(real > 0.0, factor, 0.0)
    return diag_real * factor, -diag_imag * factor


def product(a, b):
    return a[0] * b[0] - a[1] * b[1], a[0] * b[1] + a[1] * b[0]


def pair_rows(value, temp):
    temp[8:32, :] = value
    row = lax.broadcasted_iota(jnp.int32, (24, 128), 0)
    return value + jnp.where(row % 2 == 0, temp[9:33, :], temp[7:31, :])


def neighbour(ref, x, c, r, count, step, low=8, high=32):
    center = lambda s: ref[x, c, s, low:high, :]
    up = center(r + 1) if r < count - 1 else pltpu.roll(center(0), 127, 1)
    down = center(r - 1) if r > 0 else pltpu.roll(center(count - 1), 1, 1)
    total = ref[x - 1, c, r, low:high, :] + ref[x + 1, c, r, low:high, :]
    total = total + ref[x, c, r, low - step : high - step, :] + ref[x, c, r, low + step : high + step, :]
    return total + (up + down)


def sweep(old, new, weight, weight_at, source, source_at, low, high, count, step, scale):
    def body(x, _):
        for r in range(count):
            parts = []
            for c in range(2):
                total = neighbour(old, x, c, r, count, step)
                if scale != 1.0:
                    total = total * scale
                parts.append(source[x + source_at, c, r] + total)
            w = [weight[x + weight_at, c, r] for c in range(2)]
            moved = product(w, parts)
            for c in range(2):
                new[x, c, r, 8:32, :] = (1.0 - OMEGA) * old[x, c, r, 8:32, :] + moved[c]
        return 0

    lax.fori_loop(low, high, body, 0)


def clear(ref, count):
    def body(x, _):
        ref[x] = jnp.zeros(ref.shape[1:], F32)
        return 0

    lax.fori_loop(0, count, body, 0)


def clear_edges(ref, count):
    zero = jnp.zeros((8, 128), F32)

    def body(x, _):
        for c in range(2):
            for r in range(ref.shape[2]):
                ref[x, c, r, 0:8, :] = zero
                ref[x, c, r, 32:40, :] = zero
        return 0

    lax.fori_loop(0, count, body, 0)


def dense(parts):
    lane = lax.broadcasted_iota(jnp.int32, parts[0].shape, 1)
    result = []
    for n in range(3):
        head = parts[0] if n == 0 else pltpu.roll(parts[n], 128 - 32 * n, 1)
        result.append(jnp.where(lane < 96 - 32 * n, head, pltpu.roll(parts[n + 1], 96 - 32 * n, 1)))
    return result


def loose(parts, clean):
    lane = lax.broadcasted_iota(jnp.int32, parts[0].shape, 1)
    result = [parts[0]]
    for k in (1, 2):
        result.append(jnp.where(lane < 32 * k, pltpu.roll(parts[k - 1], 32 * k, 1), pltpu.roll(parts[k], 32 * k, 1)))
    result.append(pltpu.roll(parts[2], 96, 1))
    return [jnp.where(lane < 96, value, 0.0) for value in result] if clean else result


def put_dense(v, x, c, parts):
    for n, tile in enumerate(dense(parts)):
        v.packed[x, c, n] = tile
        depth = v.front.shape[0]
        if x < depth:
            v.front[x, c, n] = tile
        if x >= 4 - depth:
            v.back[x - 4 + depth, c, n] = tile


def pack_kernel(v):
    loads = [
        pltpu.make_async_copy(v.right_side, v.field, v.sem.at[0]),
        pltpu.make_async_copy(v.layer_index, v.layers, v.sem.at[1]),
        pltpu.make_async_copy(v.absorb_level, v.levels, v.sem.at[2]),
        pltpu.make_async_copy(v.speeds, v.table, v.sem.at[3]),
    ]
    for load in loads:
        load.start()
    matrix = sort_matrix(384, 512, False)
    for load in loads:
        load.wait()
    field = exact_dot(v.field[...].reshape(64, 384), matrix)
    both = jnp.concatenate([v.layers[...].reshape(32, 384), v.levels[...].reshape(32, 384)], axis=0)
    codes = jnp.dot(both.astype(F32).astype(BF16), matrix, preferred_element_type=F32)
    inside = lax.broadcasted_iota(jnp.int32, (32, 128), 1) < 96
    total = [jnp.zeros((32, 128), F32), jnp.zeros((32, 128), F32)]
    reals, imags = [], []
    for r in range(4):
        lanes = slice(r * 128, r * 128 + 128)
        layer = codes[0:32, lanes]
        velocity = jnp.full((32, 128), v.table[0], F32)
        for n in range(1, v.table.shape[0]):
            velocity = jnp.where(layer == float(n), v.table[n], velocity)
        ratio = KH_FACTOR / velocity
        real = jnp.where(inside, ratio * ratio, 0.0)
        imag = -real * (BETA + ABSORB * codes[32:64, lanes])
        total = [total[0] + real, total[1] + imag]
        reals.append(real)
        imags.append(imag)
    for x in range(4):
        rows = slice(x * 8, x * 8 + 8)
        for c in range(2):
            at = 32 * c + x * 8
            put_dense(v, x, c, [field[at : at + 8, r * 128 : r * 128 + 128] for r in range(4)])
        put_dense(v, x, 2, [reals[r][rows] for r in range(4)])
        put_dense(v, x, 3, [imags[r][rows] for r in range(4)])
    means = []
    for c in range(2):
        t = total[c]
        v.temp[c] = (t[0:8] + t[8:16]) + (t[16:24] + t[24:32])
        row = [v.temp[c, n : n + 1] for n in range(8)]
        means.append([((row[4 * k] + row[4 * k + 1]) + (row[4 * k + 2] + row[4 * k + 3])) * (1.0 / 64.0) for k in range(2)])
    w = [scaled_inverse(means[0][k], means[1][k], 0.0625) for k in range(2)]
    v.inverse_two[...] = jnp.concatenate(dense([w[k][c] for c in range(2) for k in range(2)]), axis=1)


def pack(table, right_side, layer_index, absorb_level):
    return run(
        "pack",
        pack_kernel,
        dict(speeds=(table, HB), right_side=(right_side, HB), layer_index=(layer_index, HB), absorb_level=(absorb_level, HB)),
        dict(packed=((4, 4, 3, 8, 128), VM), front=((2, 4, 3, 8, 128), VM), back=((2, 4, 3, 8, 128), VM),
             inverse_two=((1, 384), VM)),
        dict(field=right_side.shape, layers=pltpu.VMEM(layer_index.shape, jnp.int32),
             levels=pltpu.VMEM(absorb_level.shape, jnp.int32), table=pltpu.SMEM(table.shape, F32), temp=(2, 8, 128)),
        4,
    )


FINE = (16, 2, 4, 24, 128)
WIDE = (16, 2, 4, 40, 128)
PART = (8, 2, 4, 24, 128)
INNER = (12, 2, 4, 24, 128)
COARSE = (6, 2, 2, 24, 128)
COARSE_WIDE = (6, 2, 2, 40, 128)


def keep(v, number, source, target):
    copy = pltpu.make_async_copy(source, target, v.sem.at[number])
    copy.start()
    return copy


def squeeze_rows(target, n, source, k, c, tile, top):
    for s in range(2):
        target[n, s * 4 : s * 4 + 4, :] = source[k, c, s, pl.ds(top + 8 * tile, 4, 2), :]


def down_body(v, source, weight, diag, weight_one, diag_one, first_copy):
    def first(x, _):
        for r in range(4):
            e = product([weight[x, c, r] for c in range(2)], [source[x, c, r] for c in range(2)])
            for c in range(2):
                v.start[x, c, r, 8:32, :] = e[c]
        return 0

    lax.fori_loop(0, 16, first, 0)
    sweep(v.start, v.guess, weight, 0, source, 0, 1, 15, 4, 1, 1.0)
    copies = [keep(v, first_copy, v.guess.at[2:14, :, :, 8:32, :], v.out_guess)]

    def residual(k, _):
        for s in range(2):
            sums = [None, None]
            for half in range(2):
                x = 2 + 2 * k + half
                for r in (2 * s, 2 * s + 1):
                    e = [v.guess[x, c, r, 8:32, :] for c in range(2)]
                    moved = product([diag[x, c, r] for c in range(2)], e)
                    for c in range(2):
                        value = source[x, c, r] + neighbour(v.guess, x, c, r, 4, 1) - moved[c]
                        sums[c] = value if sums[c] is None else sums[c] + value
            g = [pair_rows(sums[c], v.temp.at[c]) * 0.125 for c in range(2)]
            e = product([weight_one[k, c, s] for c in range(2)], g)
            for c in range(2):
                v.source_one[k, c, s] = g[c]
                v.start_one[k, c, s, 8:32, :] = e[c]
        return 0

    lax.fori_loop(0, 6, residual, 0)
    copies.append(keep(v, first_copy + 1, v.source_one, v.out_source_one))
    sweep(v.start_one, v.guess_one, weight_one, 0, v.source_one, 0, 1, 5, 2, 2, 0.25)
    copies.append(keep(v, first_copy + 2, v.guess_one, v.out_guess_one))

    total = [None, None]
    for k in (2, 3):
        for s in range(2):
            e = [v.guess_one[k, c, s, 8:32, :] for c in range(2)]
            moved = product([diag_one[k, c, s] for c in range(2)], e)
            for c in range(2):
                value = v.source_one[k, c, s] + 0.25 * neighbour(v.guess_one, k, c, s, 2, 2) - moved[c]
                total[c] = value if total[c] is None else total[c] + value
    pieces = []
    for c in range(2):
        v.temp[c, 8:32, :] = total[c]
        for k in range(2):
            row = 16 + 4 * k
            pieces.append((v.temp[c, row : row + 1, :] + v.temp[c, row + 2 : row + 3, :]) * 0.125)
    for n, tile in enumerate(dense(pieces)):
        v.two[0:1, n * 128 : n * 128 + 128] = tile

    for c in range(2):
        for k in range(4):
            squeeze_rows(v.send_y, k * 2 + c, v.guess_one, k + 1, c, 1, 8)
        for tile in range(3):
            for k in range(2):
                n = (k * 3 + tile) * 2 + c
                squeeze_rows(v.send_up, n, v.guess_one, k + 1, c, tile, 8)
                squeeze_rows(v.send_down, n, v.guess_one, k + 3, c, tile, 8)
    return copies


def fill(v, target, at, count, x):
    for c in range(count):
        for tile, ref in enumerate((v.low, v.mid, v.high)):
            parts = loose([ref[x, at + c, n] for n in range(3)], at + c == 2)
            for r in range(4):
                target[x, c, r, 8 * tile : 8 * tile + 8, :] = parts[r]


def clear_down(v):
    clear_edges(v.start, 16)
    clear_edges(v.guess, 16)
    clear_edges(v.start_one, 6)
    clear_edges(v.guess_one, 6)


def down_first_kernel(v):
    clear_down(v)

    def filled(x, _):
        fill(v, v.source, 0, 2, x)
        fill(v, v.diag, 2, 2, x)
        for r in range(4):
            w = scaled_inverse(v.diag[x, 0, r], v.diag[x, 1, r], 1.0)
            for c in range(2):
                v.weight[x, c, r] = w[c]
        return 0

    lax.fori_loop(0, 16, filled, 0)
    copies = [keep(v, 0, v.source, v.out_source), keep(v, 1, v.weight, v.out_weight)]

    def coarse(k, _):
        for s in range(2):
            shift = []
            for c in range(2):
                total = None
                for half in range(2):
                    for r in (2 * s, 2 * s + 1):
                        value = v.diag[2 + 2 * k + half, c, r]
                        total = value if total is None else total + value
                shift.append(pair_rows(total, v.temp.at[c]) * 0.125)
            w = scaled_inverse(shift[0], shift[1], 0.25)
            d = (1.5 - shift[0], -shift[1])
            for c in range(2):
                v.weight_one[k, c, s] = w[c]
                v.diag_one[k, c, s] = d[c]
        return 0

    lax.fori_loop(0, 6, coarse, 0)

    def turn(x, _):
        for r in range(4):
            v.diag[x, 0, r] = 6.0 - v.diag[x, 0, r]
            v.diag[x, 1, r] = -v.diag[x, 1, r]
        return 0

    lax.fori_loop(0, 16, turn, 0)
    copies += [keep(v, 2, v.diag, v.out_diag), keep(v, 3, v.weight_one, v.out_weight_one),
               keep(v, 4, v.diag_one, v.out_diag_one)]
    copies += down_body(v, v.source, v.weight, v.diag, v.weight_one, v.diag_one, 5)
    v.two[0:1, 384:768] = v.inverse_two[...]
    for copy in copies:
        copy.wait()


def down_first(mid, low, high, inverse_two):
    return run(
        "down_first",
        down_first_kernel,
        dict(mid=(mid, VM), low=(low, VM), high=(high, VM), inverse_two=(inverse_two, VM)),
        dict(out_source=(FINE, HB), out_weight=(FINE, HB), out_diag=(FINE, HB), out_weight_one=(COARSE, HB),
             out_diag_one=(COARSE, HB), out_guess=(INNER, HB), out_source_one=(COARSE, HB), out_guess_one=(COARSE_WIDE, HB),
             two=((1, 768), VM), send_y=((8, 8, 128), VM), send_up=((12, 8, 128), VM), send_down=((12, 8, 128), VM)),
        dict(source=FINE, weight=FINE, diag=FINE, weight_one=COARSE, diag_one=COARSE, start=WIDE, guess=WIDE,
             start_one=COARSE_WIDE, source_one=COARSE, guess_one=COARSE_WIDE, temp=(2, 40, 128)),
        8,
    )


EDGE = 18 * 2 * 3


def down_second_kernel(v):
    loads = [keep(v, 0, v.in_right, v.right), keep(v, 1, v.in_diag, v.diag), keep(v, 2, v.in_weight, v.weight),
             keep(v, 3, v.in_weight_one, v.weight_one), keep(v, 4, v.in_diag_one, v.diag_one)]
    clear_down(v)
    clear_edges(v.first, 18)

    def filled(x, _):
        for c in range(2):
            for tile, ref in enumerate((v.low, v.mid, v.high)):
                parts = loose([ref[(x * 2 + c) * 3 + n] for n in range(3)], True)
                for r in range(4):
                    v.first[x, c, r, 8 + 8 * tile : 16 + 8 * tile, :] = parts[r]
        return 0

    lax.fori_loop(0, 18, filled, 0)
    for x in range(4):
        for c in range(2):
            for r in range(4):
                row = slice(c * 4 + r, c * 4 + r + 1)
                v.first[x + 7, c, r, 7:8, :] = v.low[EDGE + x, row]
                v.first[x + 7, c, r, 32:33, :] = v.high[EDGE + 4 + x, row]
    for load in loads:
        load.wait()

    def residual(x, _):
        for r in range(4):
            moved = product([v.diag[x, c, r] for c in range(2)], [v.first[x + 1, c, r, 8:32, :] for c in range(2)])
            for c in range(2):
                v.source[x, c, r] = v.right[x, c, r] + neighbour(v.first, x + 1, c, r, 4, 1) - moved[c]
        return 0

    lax.fori_loop(0, 16, residual, 0)
    copies = [keep(v, 8, v.source.at[4:12], v.out_source)]
    copies += down_body(v, v.source, v.weight, v.diag, v.weight_one, v.diag_one, 5)
    for copy in copies:
        copy.wait()


def down_second(mid, low, high, old):
    return run(
        "down_second",
        down_second_kernel,
        dict(mid=(mid, VM), low=(low, VM), high=(high, VM), in_right=(old.out_source, HB), in_weight=(old.out_weight, HB),
             in_diag=(old.out_diag, HB), in_weight_one=(old.out_weight_one, HB), in_diag_one=(old.out_diag_one, HB)),
        dict(out_source=(PART, HB), out_guess=(INNER, HB), out_source_one=(COARSE, HB), out_guess_one=(COARSE_WIDE, HB),
             two=((1, 384), VM), send_y=((8, 8, 128), VM), send_up=((12, 8, 128), VM), send_down=((12, 8, 128), VM)),
        dict(source=FINE, weight=FINE, diag=FINE, weight_one=COARSE, diag_one=COARSE, start=WIDE, guess=WIDE,
             start_one=COARSE_WIDE, source_one=COARSE, guess_one=COARSE_WIDE, temp=(2, 40, 128),
             right=FINE, first=(18, 2, 4, 40, 128)),
        9,
    )


def over(low, count, block, body):
    def several(number, _):
        for n in range(block):
            body(low + number * block + n)
        return 0

    lax.fori_loop(0, count // block, several, 0)
    for n in range(count - count % block, count):
        body(low + n)


def unpack_two(packed, first, begin, target, window, clean):
    def body(x):
        parts = [packed[begin + x, :, first + n * 128 : first + n * 128 + 128] for n in range(3)]
        for k, part in enumerate(loose(parts, clean)):
            target[x, k] = part

    over(0, window, 7, body)


def solve_two(own, source, weight, ping, pong, window, planes, groups):
    clear(ping, window + 8)
    clear(pong, window + 8)
    rows = slice(8, 8 + groups)

    def start(x):
        for k in range(2):
            e = product([weight[x, k], weight[x, 2 + k]], [source[x, k], source[x, 2 + k]])
            for c in range(2):
                ping[x + 4, c * 2 + k, rows, :] = e[c]

    over(0, window, 7, start)

    def step(old, new, left):
        def body(x):
            here = [old[x + 4, n, rows, :] for n in range(4)]
            for k in range(2):
                parts = []
                for c in range(2):
                    n, other = c * 2 + k, c * 2 + 1 - k
                    side = old[x + 4, other, 7 : 7 + groups, :] if k == 0 else old[x + 4, other, 9 : 9 + groups, :]
                    total = (old[x + 3, n, rows, :] + old[x + 5, n, rows, :]) + (here[other] + side)
                    total = total + (pltpu.roll(here[n], 1, 1) + pltpu.roll(here[n], 127, 1))
                    parts.append(source[x, n] + 0.0625 * total)
                moved = product([weight[x, k], weight[x, 2 + k]], parts)
                for c in range(2):
                    new[x + 4, c * 2 + k, rows, :] = (1.0 - OMEGA) * here[c * 2 + k] + moved[c]

        count = min(window, 2 * (3 + left) + 1)
        over(jnp.clip(own - 3 - left, 0, window - count), count, 4, body)

    pairs = (ping, pong)
    for number in range(NC - 1):
        step(pairs[number % 2], pairs[(number + 1) % 2], NC - 2 - number)
    return pairs[(NC - 1) % 2]


def spread_rows(target, top, x, c, tile, block):
    for s in range(2):
        for twice in range(2):
            target[x, c, s, pl.ds(top + 8 * tile + twice, 4, 2), :] = block[s * 4 : s * 4 + 4, :]


def add_two(answer, gx, gy, one, first, count):
    row = lax.broadcasted_iota(jnp.int32, (8, 128), 0)
    for j in range(count):
        x = gx + 4 + (first + j) // 2
        for c in range(2):
            for tile in range(3):
                spot = gy + 7 + tile
                low = jnp.broadcast_to(answer[x, c * 2, pl.ds(spot, 1), :], (8, 128))
                high = jnp.broadcast_to(answer[x, c * 2 + 1, pl.ds(spot, 1), :], (8, 128))
                value = jnp.where(row < 4, low, high)
                at = slice(8 + 8 * tile, 16 + 8 * tile)
                for s in range(2):
                    one[j, c, s, at, :] = one[j, c, s, at, :] + value


def up_kernel(v, planes, groups, second):
    count = 8
    loads = []
    if second:
        loads.append(keep(v, 7, v.in_weight_two, v.weight_two))
    own = v.in_source if second else v.in_source.at[4:12]
    loads += [keep(v, 0, own, v.source.at[4:12]), keep(v, 1, v.in_weight.at[4:12], v.weight.at[4:12]),
              keep(v, 2, v.in_guess, v.guess.at[2:14]), keep(v, 3, v.in_guess_one, v.guess_one),
              keep(v, 4, v.in_source_one, v.source_one), keep(v, 5, v.in_weight_one, v.weight_one)]
    if second:
        loads.append(keep(v, 6, v.in_first, v.first))
        v.matrix[...] = sort_matrix(512, 384, True)
    window = min(planes, WINDOW)
    begin = jnp.clip(v.where[0] - 10, 0, planes - window)
    unpack_two(v.gathered, 0, begin, v.source_two, window, False)
    copies = []
    if second:
        loads.pop(0).wait()
    else:
        unpack_two(v.gathered, 384, begin, v.weight_two, window, True)
        copies.append(keep(v, 7, v.weight_two, v.out_weight_two))
    answer = solve_two(v.where[0] - begin, v.source_two, v.weight_two, v.ping, v.pong, window, planes, groups)
    clear_edges(v.one, count)
    clear_edges(v.one_next, count)
    clear_edges(v.ea, 16)
    clear_edges(v.eb, 16)
    for load in loads:
        load.wait()

    for k in range(4):
        for c in range(2):
            for s in range(2):
                v.one[k + 2, c, s, 16:24, :] = v.guess_one[k + 1, c, s, 16:24, :]
            spread_rows(v.one, 8, k + 2, c, 0, v.from_y_low[k * 2 + c])
            spread_rows(v.one, 8, k + 2, c, 2, v.from_y_high[k * 2 + c])
    for c in range(2):
        for tile in range(3):
            for k in range(2):
                n = (k * 3 + tile) * 2 + c
                spread_rows(v.one, 8, k, c, tile, v.from_low[n])
                spread_rows(v.one, 8, 6 + k, c, tile, v.from_high[n])
    add_two(answer, v.where[0] - begin, v.where[1], v.one, -3, count)
    sweep(v.one, v.one_next, v.weight_one, -1, v.source_one, -1, 1, 7, 2, 2, 0.25)
    sweep(v.one_next, v.one, v.weight_one, -1, v.source_one, -1, 2, 6, 2, 2, 0.25)

    def correct(j, _):
        for half in range(2):
            x = 2 * j + half
            for r in range(4):
                for c in range(2):
                    v.ea[x, c, r, 8:32, :] = v.guess[x, c, r] + v.one[j, c, r // 2, 8:32, :]
        return 0

    lax.fori_loop(2, 6, correct, 0)
    sweep(v.ea, v.eb, v.weight, 0, v.source, 0, 5, 11, 4, 1, 1.0)
    sweep(v.eb, v.ea, v.weight, 0, v.source, 0, 6, 10, 4, 1, 1.0)
    return copies


def up_first_kernel(v, planes, groups):
    copies = up_kernel(v, planes, groups, False)
    for x in range(4):
        for c in range(2):
            for r in range(4):
                v.first[x, c, r] = v.ea[x + 6, c, r, 16:24, :]
                row = slice(c * 4 + r, c * 4 + r + 1)
                v.edges[x, row] = v.ea[x + 6, c, r, 15:16, :]
                v.edges[x + 4, row] = v.ea[x + 6, c, r, 24:25, :]
            put_dense(v, x, c, [v.ea[x + 6, c, r, 16:24, :] for r in range(4)])
    copies.append(keep(v, 8, v.first, v.out_first))
    for copy in copies:
        copy.wait()


def up_second_kernel(v, planes, groups):
    up_kernel(v, planes, groups, True)
    blocks = []
    for c in range(2):
        for x in range(4):
            blocks.append(
                jnp.concatenate([v.first[x, c, r] + v.ea[x + 6, c, r, 16:24, :] for r in range(4)], axis=1)
            )
    values = jnp.concatenate(blocks, axis=0)
    v.result[...] = exact_dot(values, v.matrix[...]).reshape(2, 4, 8, 384)


def up_scratch(planes, groups):
    level = (8, 2, 2, 40, 128)
    two = (min(planes, WINDOW) + 8, 4, 16 + groups, 128)
    source = (min(planes, WINDOW), 4, groups, 128)
    return dict(source=FINE, weight=FINE, guess=FINE, guess_one=COARSE_WIDE, source_one=COARSE, weight_one=COARSE,
                source_two=source, weight_two=source, ping=two, pong=two,
                one=level, one_next=level, ea=WIDE, eb=WIDE, first=(4, 2, 4, 8, 128))


def up_inputs(where, gathered, messages, down, first_down):
    return dict(where=(where, SM), gathered=(gathered, VM), **{name: (array, VM) for name, array in messages.items()},
                in_source=(down.out_source, HB), in_weight=(first_down.out_weight, HB), in_guess=(down.out_guess, HB),
                in_guess_one=(down.out_guess_one, HB), in_source_one=(down.out_source_one, HB),
                in_weight_one=(first_down.out_weight_one, HB))


def up_first(where, gathered, messages, down):
    planes, groups = gathered.shape[0], gathered.shape[1]
    return run(
        "up_first",
        lambda v: up_first_kernel(v, planes, groups),
        up_inputs(where, gathered, messages, down, down),
        dict(packed=((4, 2, 3, 8, 128), VM), front=((3, 2, 3, 8, 128), VM), back=((3, 2, 3, 8, 128), VM),
             edges=((8, 8, 128), VM), out_first=((4, 2, 4, 8, 128), HB), out_weight_two=((min(planes, WINDOW), 4, groups, 128), HB)),
        up_scratch(planes, groups),
        9,
    )


def up_second(where, gathered, messages, down, first_down, first_up):
    planes, groups = gathered.shape[0], gathered.shape[1]
    return run(
        "up_second",
        lambda v: up_second_kernel(v, planes, groups),
        dict(**up_inputs(where, gathered, messages, down, first_down), in_weight_two=(first_up.out_weight_two, HB),
             in_first=(first_up.out_first, HB)),
        dict(result=((2, 4, 8, 384), VM)),
        dict(**up_scratch(planes, groups), matrix=pltpu.VMEM((512, 384), BF16)),
        8,
    ).result


def shifted(block, axis, by):
    count = lax.axis_size(axis)
    pairs = [(i, i + by) for i in range(count) if 0 <= i + by < count]
    return lax.ppermute(block, axis, pairs)


def gather_two(row):
    count_y, count_x = lax.axis_size("gy"), lax.axis_size("gx")
    width = row.shape[1]
    sent = jnp.broadcast_to(row[None], (count_x * count_y, 1, width))
    return lax.all_to_all(sent, ("gx", "gy"), 0, 0).reshape(count_x, count_y, width)


def beside(own):
    return jnp.concatenate(
        [
            shifted(own.back, "gx", 2),
            shifted(own.packed, "gx", 1),
            own.packed,
            shifted(own.packed, "gx", -1),
            shifted(own.front, "gx", -2),
        ]
    )


def surround(mid):
    return mid, shifted(mid, "gy", 1), shifted(mid, "gy", -1)


def exchange_one(down):
    return dict(
        from_y_low=shifted(down.send_y, "gy", 1),
        from_y_high=shifted(down.send_y, "gy", -1),
        from_low=shifted(down.send_up, "gx", 1),
        from_high=shifted(down.send_down, "gx", -1),
    )


def local(right_side, velocity_table, layer_index, absorb_level):
    where = jnp.stack([lax.axis_index("gx"), lax.axis_index("gy")]).astype(jnp.int32)
    packed = pack(velocity_table, right_side, layer_index, absorb_level)
    down = down_first(*surround(beside(packed)), packed.inverse_two)
    middle = up_first(where, gather_two(down.two), exchange_one(down), down)
    rows = jnp.concatenate([beside(middle).reshape(EDGE, 8, 128), middle.edges])
    again = down_second(*surround(rows), down)
    return up_second(where, gather_two(again.two), exchange_one(again), again, down, middle)


def solution(mesh):
    placed = (P(None, "gx", "gy", None), P(), P("gx", "gy", None), P("gx", "gy", None))
    return jax.shard_map(
        local, mesh=mesh, in_specs=placed, out_specs=P(None, "gx", "gy", None), check_vma=False
    )
```

```python
import math
from types import SimpleNamespace

import jax
import jax.numpy as jnp
from jax import lax
from jax.experimental import pallas as pl
from jax.experimental.pallas import tpu as pltpu
from jax.sharding import PartitionSpec as P


NC = 8
WINDOW = 21
OMEGA = 0.6
BETA = 0.5
ABSORB = 0.25
KH_FACTOR = 2.0 * math.pi * 6.0 * 20.0

F32 = jnp.float32
BF16 = jnp.bfloat16
VM = pltpu.VMEM
SM = pltpu.SMEM
HB = pltpu.HBM
PARAMS = pltpu.CompilerParams(vmem_limit_bytes=32 * 1024 * 1024)


def run(name, kernel, inputs, outputs, scratch, copies):
    names = list(inputs) + list(outputs) + list(scratch) + ["sem"]
    result = pl.pallas_call(
        lambda *refs: kernel(SimpleNamespace(**dict(zip(names, refs)))),
        name=name,
        out_shape=tuple(HB(dims, F32) if space is HB else jax.ShapeDtypeStruct(dims, F32) for dims, space in outputs.values()),
        in_specs=[pl.BlockSpec(memory_space=space) for _, space in inputs.values()],
        out_specs=tuple(pl.BlockSpec(memory_space=space) for _, space in outputs.values()),
        scratch_shapes=[pltpu.VMEM(dims, F32) if isinstance(dims, tuple) else dims for dims in scratch.values()]
        + [pltpu.SemaphoreType.DMA((copies,))],
        compiler_params=PARAMS,
    )(*[pltpu.with_memory_space_constraint(array, HB) if space is HB else array for array, space in inputs.values()])
    return SimpleNamespace(**dict(zip(outputs, result)))


def sort_matrix(rows, columns, flip):
    first = lax.broadcasted_iota(jnp.int32, (rows, columns), 0)
    second = lax.broadcasted_iota(jnp.int32, (rows, columns), 1)
    if flip:
        first, second = second, first
    lane = second % 128
    hit = (first == 4 * lane + second // 128) & (lane < 96)
    return jnp.where(hit, 1.0, 0.0).astype(BF16)


def exact_dot(values, matrix):
    high = values.astype(BF16)
    rest = values - high.astype(F32)
    middle = rest.astype(BF16)
    low = (rest - middle.astype(F32)).astype(BF16)
    dot = lambda part: jnp.dot(part, matrix, preferred_element_type=F32)
    return (dot(low) + dot(middle)) + dot(high)


def scaled_inverse(real, imag, scale):
    diag_real = 6.0 * scale - real
    diag_imag = -imag
    factor = OMEGA / (diag_real * diag_real + diag_imag * diag_imag)
    factor = jnp.where(real > 0.0, factor, 0.0)
    return diag_real * factor, -diag_imag * factor


def product(a, b):
    return a[0] * b[0] - a[1] * b[1], a[0] * b[1] + a[1] * b[0]


def pair_rows(value, temp):
    temp[8:32, :] = value
    row = lax.broadcasted_iota(jnp.int32, (24, 128), 0)
    return value + jnp.where(row % 2 == 0, temp[9:33, :], temp[7:31, :])


def neighbour(ref, x, c, r, count, step, low=8, high=32):
    center = lambda s: ref[x, c, s, low:high, :]
    up = center(r + 1) if r < count - 1 else pltpu.roll(center(0), 127, 1)
    down = center(r - 1) if r > 0 else pltpu.roll(center(count - 1), 1, 1)
    total = ref[x - 1, c, r, low:high, :] + ref[x + 1, c, r, low:high, :]
    total = total + ref[x, c, r, low - step : high - step, :] + ref[x, c, r, low + step : high + step, :]
    return total + (up + down)


def sweep(old, new, weight, weight_at, source, source_at, low, high, count, step, scale):
    def body(x, _):
        for r in range(count):
            parts = []
            for c in range(2):
                total = neighbour(old, x, c, r, count, step)
                if scale != 1.0:
                    total = total * scale
                parts.append(source[x + source_at, c, r] + total)
            w = [weight[x + weight_at, c, r] for c in range(2)]
            moved = product(w, parts)
            for c in range(2):
                new[x, c, r, 8:32, :] = (1.0 - OMEGA) * old[x, c, r, 8:32, :] + moved[c]
        return 0

    lax.fori_loop(low, high, body, 0)


def clear(ref, count):
    def body(x, _):
        ref[x] = jnp.zeros(ref.shape[1:], F32)
        return 0

    lax.fori_loop(0, count, body, 0)


def clear_edges(ref, count, begin=0):
    zero = jnp.zeros((8, 128), F32)

    def body(x, _):
        for c in range(2):
            for r in range(ref.shape[2]):
                ref[x, c, r, 0:8, :] = zero
                ref[x, c, r, 32:40, :] = zero
        return 0

    lax.fori_loop(begin, count, body, 0)


def dense(parts):
    lane = lax.broadcasted_iota(jnp.int32, parts[0].shape, 1)
    result = []
    for n in range(3):
        head = parts[0] if n == 0 else pltpu.roll(parts[n], 128 - 32 * n, 1)
        result.append(jnp.where(lane < 96 - 32 * n, head, pltpu.roll(parts[n + 1], 96 - 32 * n, 1)))
    return result


def loose(parts, clean):
    lane = lax.broadcasted_iota(jnp.int32, parts[0].shape, 1)
    result = [parts[0]]
    for k in (1, 2):
        result.append(jnp.where(lane < 32 * k, pltpu.roll(parts[k - 1], 32 * k, 1), pltpu.roll(parts[k], 32 * k, 1)))
    result.append(pltpu.roll(parts[2], 96, 1))
    return [jnp.where(lane < 96, value, 0.0) for value in result] if clean else result


def put_dense(v, x, c, parts):
    for n, tile in enumerate(dense(parts)):
        v.packed[x, c, n] = tile
        depth = v.front.shape[0]
        if x < depth:
            v.front[x, c, n] = tile
        if x >= 4 - depth:
            v.back[x - 4 + depth, c, n] = tile


def pack_kernel(v):
    loads = [
        pltpu.make_async_copy(v.right_side, v.field, v.sem.at[0]),
        pltpu.make_async_copy(v.layer_index, v.layers, v.sem.at[1]),
        pltpu.make_async_copy(v.absorb_level, v.levels, v.sem.at[2]),
        pltpu.make_async_copy(v.speeds, v.table, v.sem.at[3]),
    ]
    for load in loads:
        load.start()
    matrix = sort_matrix(384, 512, False)
    for load in loads:
        load.wait()
    field = exact_dot(v.field[...].reshape(64, 384), matrix)
    both = jnp.concatenate([v.layers[...].reshape(32, 384), v.levels[...].reshape(32, 384)], axis=0)
    codes = jnp.dot(both.astype(F32).astype(BF16), matrix, preferred_element_type=F32)
    inside = lax.broadcasted_iota(jnp.int32, (32, 128), 1) < 96
    total = [jnp.zeros((32, 128), F32), jnp.zeros((32, 128), F32)]
    reals, imags = [], []
    for r in range(4):
        lanes = slice(r * 128, r * 128 + 128)
        layer = codes[0:32, lanes]
        velocity = jnp.full((32, 128), v.table[0], F32)
        for n in range(1, v.table.shape[0]):
            velocity = jnp.where(layer == float(n), v.table[n], velocity)
        ratio = KH_FACTOR / velocity
        real = jnp.where(inside, ratio * ratio, 0.0)
        imag = -real * (BETA + ABSORB * codes[32:64, lanes])
        total = [total[0] + real, total[1] + imag]
        reals.append(real)
        imags.append(imag)
    for x in range(4):
        rows = slice(x * 8, x * 8 + 8)
        for c in range(2):
            at = 32 * c + x * 8
            put_dense(v, x, c, [field[at : at + 8, r * 128 : r * 128 + 128] for r in range(4)])
        put_dense(v, x, 2, [reals[r][rows] for r in range(4)])
        put_dense(v, x, 3, [imags[r][rows] for r in range(4)])
    means = []
    for c in range(2):
        t = total[c]
        v.temp[c] = (t[0:8] + t[8:16]) + (t[16:24] + t[24:32])
        row = [v.temp[c, n : n + 1] for n in range(8)]
        means.append([((row[4 * k] + row[4 * k + 1]) + (row[4 * k + 2] + row[4 * k + 3])) * (1.0 / 64.0) for k in range(2)])
    w = [scaled_inverse(means[0][k], means[1][k], 0.0625) for k in range(2)]
    v.inverse_two[...] = jnp.concatenate(dense([w[k][c] for c in range(2) for k in range(2)]), axis=1)


def pack(table, right_side, layer_index, absorb_level):
    return run(
        "pack",
        pack_kernel,
        dict(speeds=(table, HB), right_side=(right_side, HB), layer_index=(layer_index, HB), absorb_level=(absorb_level, HB)),
        dict(packed=((4, 4, 3, 8, 128), VM), front=((2, 4, 3, 8, 128), VM), back=((2, 4, 3, 8, 128), VM),
             inverse_two=((1, 384), VM)),
        dict(field=right_side.shape, layers=pltpu.VMEM(layer_index.shape, jnp.int32),
             levels=pltpu.VMEM(absorb_level.shape, jnp.int32), table=pltpu.SMEM(table.shape, F32), temp=(2, 8, 128)),
        4,
    )


FINE = (16, 2, 4, 24, 128)
WIDE = (16, 2, 4, 40, 128)
PART = (8, 2, 4, 24, 128)
INNER = (12, 2, 4, 24, 128)
COARSE = (6, 2, 2, 24, 128)
COARSE_WIDE = (6, 2, 2, 40, 128)


def keep(v, number, source, target):
    copy = pltpu.make_async_copy(source, target, v.sem.at[number])
    copy.start()
    return copy


def squeeze_rows(target, n, source, k, c, tile, top):
    for s in range(2):
        target[n, s * 4 : s * 4 + 4, :] = source[k, c, s, pl.ds(top + 8 * tile, 4, 2), :]


def down_body(v, source, weight, diag, weight_one, diag_one, first_copy):
    def first(x, _):
        for r in range(4):
            e = product([weight[x, c, r] for c in range(2)], [source[x, c, r] for c in range(2)])
            for c in range(2):
                v.start[x, c, r, 8:32, :] = e[c]
        return 0

    lax.fori_loop(0, 16, first, 0)
    sweep(v.start, v.guess, weight, 0, source, 0, 1, 15, 4, 1, 1.0)
    copies = [keep(v, first_copy, v.guess.at[2:14, :, :, 8:32, :], v.out_guess)]

    def residual(k, _):
        for s in range(2):
            sums = [None, None]
            for half in range(2):
                x = 2 + 2 * k + half
                for r in (2 * s, 2 * s + 1):
                    e = [v.guess[x, c, r, 8:32, :] for c in range(2)]
                    moved = product([diag[x, c, r] for c in range(2)], e)
                    for c in range(2):
                        value = source[x, c, r] + neighbour(v.guess, x, c, r, 4, 1) - moved[c]
                        sums[c] = value if sums[c] is None else sums[c] + value
            g = [pair_rows(sums[c], v.temp.at[c]) * 0.125 for c in range(2)]
            e = product([weight_one[k, c, s] for c in range(2)], g)
            for c in range(2):
                v.source_one[k, c, s] = g[c]
                v.start_one[k, c, s, 8:32, :] = e[c]
        return 0

    lax.fori_loop(0, 6, residual, 0)
    copies.append(keep(v, first_copy + 1, v.source_one, v.out_source_one))
    sweep(v.start_one, v.guess_one, weight_one, 0, v.source_one, 0, 1, 5, 2, 2, 0.25)
    copies.append(keep(v, first_copy + 2, v.guess_one, v.out_guess_one))

    total = [None, None]
    for k in (2, 3):
        for s in range(2):
            e = [v.guess_one[k, c, s, 8:32, :] for c in range(2)]
            moved = product([diag_one[k, c, s] for c in range(2)], e)
            for c in range(2):
                value = v.source_one[k, c, s] + 0.25 * neighbour(v.guess_one, k, c, s, 2, 2) - moved[c]
                total[c] = value if total[c] is None else total[c] + value
    pieces = []
    for c in range(2):
        v.temp[c, 8:32, :] = total[c]
        for k in range(2):
            row = 16 + 4 * k
            pieces.append((v.temp[c, row : row + 1, :] + v.temp[c, row + 2 : row + 3, :]) * 0.125)
    for n, tile in enumerate(dense(pieces)):
        v.two[0:1, n * 128 : n * 128 + 128] = tile

    for c in range(2):
        for k in range(4):
            squeeze_rows(v.send_y, k * 2 + c, v.guess_one, k + 1, c, 1, 8)
        for tile in range(3):
            for k in range(2):
                n = (k * 3 + tile) * 2 + c
                squeeze_rows(v.send_up, n, v.guess_one, k + 1, c, tile, 8)
                squeeze_rows(v.send_down, n, v.guess_one, k + 3, c, tile, 8)
    return copies


def fill(v, target, at, count, x):
    for c in range(count):
        for tile, ref in enumerate((v.low, v.mid, v.high)):
            parts = loose([ref[x, at + c, n] for n in range(3)], at + c == 2)
            for r in range(4):
                target[x, c, r, 8 * tile : 8 * tile + 8, :] = parts[r]


def clear_down(v):
    clear_edges(v.start, 16)
    clear_edges(v.guess, 16)
    clear_edges(v.start_one, 6)
    clear_edges(v.guess_one, 6)


def down_first_kernel(v):
    clear_down(v)

    def filled(x, _):
        fill(v, v.source, 0, 2, x)
        fill(v, v.diag, 2, 2, x)
        for r in range(4):
            w = scaled_inverse(v.diag[x, 0, r], v.diag[x, 1, r], 1.0)
            for c in range(2):
                v.weight[x, c, r] = w[c]
        return 0

    lax.fori_loop(0, 16, filled, 0)
    copies = [keep(v, 0, v.source, v.out_source), keep(v, 1, v.weight, v.out_weight)]

    def coarse(k, _):
        for s in range(2):
            shift = []
            for c in range(2):
                total = None
                for half in range(2):
                    for r in (2 * s, 2 * s + 1):
                        value = v.diag[2 + 2 * k + half, c, r]
                        total = value if total is None else total + value
                shift.append(pair_rows(total, v.temp.at[c]) * 0.125)
            w = scaled_inverse(shift[0], shift[1], 0.25)
            d = (1.5 - shift[0], -shift[1])
            for c in range(2):
                v.weight_one[k, c, s] = w[c]
                v.diag_one[k, c, s] = d[c]
        return 0

    lax.fori_loop(0, 6, coarse, 0)

    def turn(x, _):
        for r in range(4):
            v.diag[x, 0, r] = 6.0 - v.diag[x, 0, r]
            v.diag[x, 1, r] = -v.diag[x, 1, r]
        return 0

    lax.fori_loop(0, 16, turn, 0)
    copies += [keep(v, 2, v.diag, v.out_diag), keep(v, 3, v.weight_one, v.out_weight_one),
               keep(v, 4, v.diag_one, v.out_diag_one)]
    copies += down_body(v, v.source, v.weight, v.diag, v.weight_one, v.diag_one, 5)
    for copy in copies:
        copy.wait()


def down_first(mid, low, high):
    return run(
        "down_first",
        down_first_kernel,
        dict(mid=(mid, VM), low=(low, VM), high=(high, VM)),
        dict(out_source=(FINE, HB), out_weight=(FINE, HB), out_diag=(FINE, HB), out_weight_one=(COARSE, HB),
             out_diag_one=(COARSE, HB), out_guess=(INNER, HB), out_source_one=(COARSE, HB), out_guess_one=(COARSE_WIDE, HB),
             two=((1, 384), VM), send_y=((8, 8, 128), VM), send_up=((12, 8, 128), VM), send_down=((12, 8, 128), VM)),
        dict(source=FINE, weight=FINE, diag=FINE, weight_one=COARSE, diag_one=COARSE, start=WIDE, guess=WIDE,
             start_one=COARSE_WIDE, source_one=COARSE, guess_one=COARSE_WIDE, temp=(2, 40, 128)),
        8,
    )


EDGE = 18 * 2 * 3


def down_second_kernel(v):
    loads = [keep(v, 0, v.in_right, v.right), keep(v, 1, v.in_diag, v.diag), keep(v, 2, v.in_weight, v.weight),
             keep(v, 3, v.in_weight_one, v.weight_one), keep(v, 4, v.in_diag_one, v.diag_one)]
    clear_down(v)
    clear_edges(v.first, 18)

    def filled(x, _):
        for c in range(2):
            for tile, ref in enumerate((v.low, v.mid, v.high)):
                parts = loose([ref[(x * 2 + c) * 3 + n] for n in range(3)], True)
                for r in range(4):
                    v.first[x, c, r, 8 + 8 * tile : 16 + 8 * tile, :] = parts[r]
        return 0

    lax.fori_loop(0, 18, filled, 0)
    for x in range(4):
        for c in range(2):
            for r in range(4):
                row = slice(c * 4 + r, c * 4 + r + 1)
                v.first[x + 7, c, r, 7:8, :] = v.low[EDGE + x, row]
                v.first[x + 7, c, r, 32:33, :] = v.high[EDGE + 4 + x, row]
    for load in loads[0:2]:
        load.wait()

    def residual(x, _):
        for r in range(4):
            moved = product([v.diag[x, c, r] for c in range(2)], [v.first[x + 1, c, r, 8:32, :] for c in range(2)])
            for c in range(2):
                v.source[x, c, r] = v.right[x, c, r] + neighbour(v.first, x + 1, c, r, 4, 1) - moved[c]
        return 0

    lax.fori_loop(0, 16, residual, 0)
    for load in loads[2:5]:
        load.wait()
    copies = [keep(v, 8, v.source.at[4:12], v.out_source)]
    copies += down_body(v, v.source, v.weight, v.diag, v.weight_one, v.diag_one, 5)
    for copy in copies:
        copy.wait()


def down_second(mid, low, high, old):
    return run(
        "down_second",
        down_second_kernel,
        dict(mid=(mid, VM), low=(low, VM), high=(high, VM), in_right=(old.out_source, HB), in_weight=(old.out_weight, HB),
             in_diag=(old.out_diag, HB), in_weight_one=(old.out_weight_one, HB), in_diag_one=(old.out_diag_one, HB)),
        dict(out_source=(PART, HB), out_guess=(INNER, HB), out_source_one=(COARSE, HB), out_guess_one=(COARSE_WIDE, HB),
             two=((1, 384), VM), send_y=((8, 8, 128), VM), send_up=((12, 8, 128), VM), send_down=((12, 8, 128), VM)),
        dict(source=FINE, weight=FINE, diag=FINE, weight_one=COARSE, diag_one=COARSE, start=WIDE, guess=WIDE,
             start_one=COARSE_WIDE, source_one=COARSE, guess_one=COARSE_WIDE, temp=(2, 40, 128),
             right=FINE, first=(18, 2, 4, 40, 128)),
        9,
    )


def over(low, count, block, body):
    def several(number, _):
        for n in range(block):
            body(low + number * block + n)
        return 0

    lax.fori_loop(0, count // block, several, 0)
    for n in range(count - count % block, count):
        body(low + n)


def unpack_two(packed, begin, target, window, clean):
    def body(x):
        parts = [packed[begin + x, :, n * 128 : n * 128 + 128] for n in range(3)]
        for k, part in enumerate(loose(parts, clean)):
            target[x, k] = part

    over(0, window, 7, body)


def solve_two(own, source, weight, ping, pong, window, planes, groups):
    clear(ping, window + 8)
    clear(pong, window + 8)
    rows = slice(8, 8 + groups)

    def start(x):
        for k in range(2):
            e = product([weight[x, k], weight[x, 2 + k]], [source[x, k], source[x, 2 + k]])
            for c in range(2):
                ping[x + 4, c * 2 + k, rows, :] = e[c]

    over(0, window, 7, start)

    def step(old, new, left):
        def body(x):
            here = [old[x + 4, n, rows, :] for n in range(4)]
            for k in range(2):
                parts = []
                for c in range(2):
                    n, other = c * 2 + k, c * 2 + 1 - k
                    side = old[x + 4, other, 7 : 7 + groups, :] if k == 0 else old[x + 4, other, 9 : 9 + groups, :]
                    total = (old[x + 3, n, rows, :] + old[x + 5, n, rows, :]) + (here[other] + side)
                    total = total + (pltpu.roll(here[n], 1, 1) + pltpu.roll(here[n], 127, 1))
                    parts.append(source[x, n] + 0.0625 * total)
                moved = product([weight[x, k], weight[x, 2 + k]], parts)
                for c in range(2):
                    new[x + 4, c * 2 + k, rows, :] = (1.0 - OMEGA) * here[c * 2 + k] + moved[c]

        count = min(window, 2 * (3 + left) + 1)
        over(jnp.clip(own - 3 - left, 0, window - count), count, 4, body)

    pairs = (ping, pong)
    for number in range(NC - 1):
        step(pairs[number % 2], pairs[(number + 1) % 2], NC - 2 - number)
    return pairs[(NC - 1) % 2]


def spread_rows(target, top, x, c, tile, block):
    for s in range(2):
        for twice in range(2):
            target[x, c, s, pl.ds(top + 8 * tile + twice, 4, 2), :] = block[s * 4 : s * 4 + 4, :]


def add_two(answer, gx, gy, one, first, count):
    row = lax.broadcasted_iota(jnp.int32, (8, 128), 0)
    for j in range(count):
        x = gx + 4 + (first + j) // 2
        for c in range(2):
            for tile in range(3):
                spot = gy + 7 + tile
                low = jnp.broadcast_to(answer[x, c * 2, pl.ds(spot, 1), :], (8, 128))
                high = jnp.broadcast_to(answer[x, c * 2 + 1, pl.ds(spot, 1), :], (8, 128))
                value = jnp.where(row < 4, low, high)
                at = slice(8 + 8 * tile, 16 + 8 * tile)
                for s in range(2):
                    one[j, c, s, at, :] = one[j, c, s, at, :] + value


def up_kernel(v, planes, groups, second):
    count = 8
    loads = []
    if second:
        loads.append(keep(v, 7, v.in_weight_two, v.weight_two))
    own = v.in_source if second else v.in_source.at[4:12]
    loads += [keep(v, 0, own, v.source.at[4:12]), keep(v, 1, v.in_weight.at[4:12], v.weight.at[4:12]),
              keep(v, 2, v.in_guess, v.guess.at[2:14]), keep(v, 3, v.in_guess_one, v.guess_one),
              keep(v, 4, v.in_source_one, v.source_one), keep(v, 5, v.in_weight_one, v.weight_one)]
    if second:
        loads.append(keep(v, 6, v.in_first, v.first))
        v.matrix[...] = sort_matrix(512, 384, True)
    window = min(planes, WINDOW)
    begin = jnp.clip(v.where[0] - 10, 0, planes - window)
    unpack_two(v.gathered, begin, v.source_two, window, False)
    copies = []
    if second:
        loads.pop(0).wait()
    else:
        unpack_two(v.gathered_weight, begin, v.weight_two, window, True)
        copies.append(keep(v, 7, v.weight_two, v.out_weight_two))
    answer = solve_two(v.where[0] - begin, v.source_two, v.weight_two, v.ping, v.pong, window, planes, groups)
    clear_edges(v.one, count)
    clear_edges(v.one_next, count)
    clear_edges(v.ea, 12, 4)
    clear_edges(v.eb, 11, 5)
    for load in loads:
        load.wait()

    for k in range(4):
        for c in range(2):
            for s in range(2):
                v.one[k + 2, c, s, 16:24, :] = v.guess_one[k + 1, c, s, 16:24, :]
            spread_rows(v.one, 8, k + 2, c, 0, v.from_y_low[k * 2 + c])
            spread_rows(v.one, 8, k + 2, c, 2, v.from_y_high[k * 2 + c])
    for c in range(2):
        for tile in range(3):
            for k in range(2):
                n = (k * 3 + tile) * 2 + c
                spread_rows(v.one, 8, k, c, tile, v.from_low[n])
                spread_rows(v.one, 8, 6 + k, c, tile, v.from_high[n])
    add_two(answer, v.where[0] - begin, v.where[1], v.one, -3, count)
    sweep(v.one, v.one_next, v.weight_one, -1, v.source_one, -1, 1, 7, 2, 2, 0.25)
    sweep(v.one_next, v.one, v.weight_one, -1, v.source_one, -1, 2, 6, 2, 2, 0.25)

    def correct(j, _):
        for half in range(2):
            x = 2 * j + half
            for r in range(4):
                for c in range(2):
                    v.ea[x, c, r, 8:32, :] = v.guess[x, c, r] + v.one[j, c, r // 2, 8:32, :]
        return 0

    lax.fori_loop(2, 6, correct, 0)
    sweep(v.ea, v.eb, v.weight, 0, v.source, 0, 5, 11, 4, 1, 1.0)
    sweep(v.eb, v.ea, v.weight, 0, v.source, 0, 6, 10, 4, 1, 1.0)
    return copies


def up_first_kernel(v, planes, groups):
    copies = up_kernel(v, planes, groups, False)
    for x in range(4):
        for c in range(2):
            for r in range(4):
                v.first[x, c, r] = v.ea[x + 6, c, r, 16:24, :]
                row = slice(c * 4 + r, c * 4 + r + 1)
                v.edges[x, row] = v.ea[x + 6, c, r, 15:16, :]
                v.edges[x + 4, row] = v.ea[x + 6, c, r, 24:25, :]
            put_dense(v, x, c, [v.ea[x + 6, c, r, 16:24, :] for r in range(4)])
    copies.append(keep(v, 8, v.first, v.out_first))
    for copy in copies:
        copy.wait()


def up_second_kernel(v, planes, groups):
    up_kernel(v, planes, groups, True)
    blocks = []
    for c in range(2):
        for x in range(4):
            blocks.append(
                jnp.concatenate([v.first[x, c, r] + v.ea[x + 6, c, r, 16:24, :] for r in range(4)], axis=1)
            )
    values = jnp.concatenate(blocks, axis=0)
    v.result[...] = exact_dot(values, v.matrix[...]).reshape(2, 4, 8, 384)


def up_scratch(planes, groups):
    level = (8, 2, 2, 40, 128)
    two = (min(planes, WINDOW) + 8, 4, 16 + groups, 128)
    source = (min(planes, WINDOW), 4, groups, 128)
    return dict(source=FINE, weight=FINE, guess=FINE, guess_one=COARSE_WIDE, source_one=COARSE, weight_one=COARSE,
                source_two=source, weight_two=source, ping=two, pong=two,
                one=level, one_next=level, ea=WIDE, eb=WIDE, first=(4, 2, 4, 8, 128))


def up_inputs(where, gathered, messages, down, first_down):
    return dict(where=(where, SM), gathered=(gathered, VM), **{name: (array, VM) for name, array in messages.items()},
                in_source=(down.out_source, HB), in_weight=(first_down.out_weight, HB), in_guess=(down.out_guess, HB),
                in_guess_one=(down.out_guess_one, HB), in_source_one=(down.out_source_one, HB),
                in_weight_one=(first_down.out_weight_one, HB))


def up_first(where, gathered, gathered_weight, messages, down):
    planes, groups = gathered.shape[0], gathered.shape[1]
    return run(
        "up_first",
        lambda v: up_first_kernel(v, planes, groups),
        dict(**up_inputs(where, gathered, messages, down, down), gathered_weight=(gathered_weight, VM)),
        dict(packed=((4, 2, 3, 8, 128), VM), front=((3, 2, 3, 8, 128), VM), back=((3, 2, 3, 8, 128), VM),
             edges=((8, 8, 128), VM), out_first=((4, 2, 4, 8, 128), HB), out_weight_two=((min(planes, WINDOW), 4, groups, 128), HB)),
        up_scratch(planes, groups),
        9,
    )


def up_second(where, gathered, messages, down, first_down, first_up):
    planes, groups = gathered.shape[0], gathered.shape[1]
    return run(
        "up_second",
        lambda v: up_second_kernel(v, planes, groups),
        dict(**up_inputs(where, gathered, messages, down, first_down), in_weight_two=(first_up.out_weight_two, HB),
             in_first=(first_up.out_first, HB)),
        dict(result=((2, 4, 8, 384), VM)),
        dict(**up_scratch(planes, groups), matrix=pltpu.VMEM((512, 384), BF16)),
        8,
    ).result


def shifted(block, axis, by):
    count = lax.axis_size(axis)
    pairs = [(i, i + by) for i in range(count) if 0 <= i + by < count]
    return lax.ppermute(block, axis, pairs)


def gather_two(row):
    count_y, count_x = lax.axis_size("gy"), lax.axis_size("gx")
    width = row.shape[1]
    sent = jnp.broadcast_to(row[None], (count_x * count_y, 1, width))
    return lax.all_to_all(sent, ("gx", "gy"), 0, 0).reshape(count_x, count_y, width)


def beside(own):
    return jnp.concatenate(
        [
            shifted(own.back, "gx", 2),
            shifted(own.packed, "gx", 1),
            own.packed,
            shifted(own.packed, "gx", -1),
            shifted(own.front, "gx", -2),
        ]
    )


def surround(mid):
    return mid, shifted(mid, "gy", 1), shifted(mid, "gy", -1)


def exchange_one(down):
    return dict(
        from_y_low=shifted(down.send_y, "gy", 1),
        from_y_high=shifted(down.send_y, "gy", -1),
        from_low=shifted(down.send_up, "gx", 1),
        from_high=shifted(down.send_down, "gx", -1),
    )


def local(right_side, velocity_table, layer_index, absorb_level):
    where = jnp.stack([lax.axis_index("gx"), lax.axis_index("gy")]).astype(jnp.int32)
    packed = pack(velocity_table, right_side, layer_index, absorb_level)
    weight_two = gather_two(packed.inverse_two)
    down = down_first(*surround(beside(packed)))
    middle = up_first(where, gather_two(down.two), weight_two, exchange_one(down), down)
    rows = jnp.concatenate([beside(middle).reshape(EDGE, 8, 128), middle.edges])
    again = down_second(*surround(rows), down)
    return up_second(where, gather_two(again.two), exchange_one(again), again, down, middle)


def solution(mesh):
    placed = (P(None, "gx", "gy", None), P(), P("gx", "gy", None), P("gx", "gy", None))
    return jax.shard_map(
        local, mesh=mesh, in_specs=placed, out_specs=P(None, "gx", "gy", None), check_vma=False
    )
```

```python
import math
from types import SimpleNamespace

import jax
import jax.numpy as jnp
from jax import lax
from jax.experimental import pallas as pl
from jax.experimental.pallas import tpu as pltpu
from jax.sharding import PartitionSpec as P


NC = 8
WINDOW = 21
OMEGA = 0.6
BETA = 0.5
ABSORB = 0.25
KH_FACTOR = 2.0 * math.pi * 6.0 * 20.0

F32 = jnp.float32
BF16 = jnp.bfloat16
VM = pltpu.VMEM
SM = pltpu.SMEM
HB = pltpu.HBM
PARAMS = pltpu.CompilerParams(vmem_limit_bytes=32 * 1024 * 1024)


def run(kernel, inputs, outputs, scratch, copies):
    names = list(inputs) + list(outputs) + list(scratch) + ["sem"]
    result = pl.pallas_call(
        lambda *refs: kernel(SimpleNamespace(**dict(zip(names, refs)))),
        out_shape=tuple(HB(dims, F32) if space is HB else jax.ShapeDtypeStruct(dims, F32) for dims, space in outputs.values()),
        in_specs=[pl.BlockSpec(memory_space=space) for _, space in inputs.values()],
        out_specs=tuple(pl.BlockSpec(memory_space=space) for _, space in outputs.values()),
        scratch_shapes=[pltpu.VMEM(dims, F32) if isinstance(dims, tuple) else dims for dims in scratch.values()]
        + [pltpu.SemaphoreType.DMA((copies,))],
        compiler_params=PARAMS,
    )(*[pltpu.with_memory_space_constraint(array, HB) if space is HB else array for array, space in inputs.values()])
    return SimpleNamespace(**dict(zip(outputs, result)))


def sort_matrix(rows, columns, flip):
    first = lax.broadcasted_iota(jnp.int32, (rows, columns), 0)
    second = lax.broadcasted_iota(jnp.int32, (rows, columns), 1)
    if flip:
        first, second = second, first
    lane = second % 128
    hit = (first == 4 * lane + second // 128) & (lane < 96)
    return jnp.where(hit, 1.0, 0.0).astype(BF16)


def exact_dot(values, matrix):
    high = values.astype(BF16)
    rest = values - high.astype(F32)
    middle = rest.astype(BF16)
    low = (rest - middle.astype(F32)).astype(BF16)
    dot = lambda part: jnp.dot(part, matrix, preferred_element_type=F32)
    return (dot(low) + dot(middle)) + dot(high)


def scaled_inverse(real, imag, scale):
    diag_real = 6.0 * scale - real
    diag_imag = -imag
    factor = OMEGA / (diag_real * diag_real + diag_imag * diag_imag)
    factor = jnp.where(real > 0.0, factor, 0.0)
    return diag_real * factor, -diag_imag * factor


def product(a, b):
    return a[0] * b[0] - a[1] * b[1], a[0] * b[1] + a[1] * b[0]


def pair_rows(value, temp):
    temp[8:32, :] = value
    row = lax.broadcasted_iota(jnp.int32, (24, 128), 0)
    return value + jnp.where(row % 2 == 0, temp[9:33, :], temp[7:31, :])


def neighbour(ref, x, c, r, count, step, low=8, high=32):
    center = lambda s: ref[x, c, s, low:high, :]
    up = center(r + 1) if r < count - 1 else pltpu.roll(center(0), 127, 1)
    down = center(r - 1) if r > 0 else pltpu.roll(center(count - 1), 1, 1)
    total = ref[x - 1, c, r, low:high, :] + ref[x + 1, c, r, low:high, :]
    total = total + ref[x, c, r, low - step : high - step, :] + ref[x, c, r, low + step : high + step, :]
    return total + (up + down)


def sweep(old, new, weight, weight_at, source, source_at, low, high, count, step, scale):
    def body(x, _):
        for r in range(count):
            parts = []
            for c in range(2):
                total = neighbour(old, x, c, r, count, step)
                if scale != 1.0:
                    total = total * scale
                parts.append(source[x + source_at, c, r] + total)
            w = [weight[x + weight_at, c, r] for c in range(2)]
            moved = product(w, parts)
            for c in range(2):
                new[x, c, r, 8:32, :] = (1.0 - OMEGA) * old[x, c, r, 8:32, :] + moved[c]
        return 0

    lax.fori_loop(low, high, body, 0)


def clear(ref, count):
    def body(x, _):
        ref[x] = jnp.zeros(ref.shape[1:], F32)
        return 0

    lax.fori_loop(0, count, body, 0)


def clear_edges(ref, count, begin=0):
    zero = jnp.zeros((8, 128), F32)

    def body(x, _):
        for c in range(2):
            for r in range(ref.shape[2]):
                ref[x, c, r, 0:8, :] = zero
                ref[x, c, r, 32:40, :] = zero
        return 0

    lax.fori_loop(begin, count, body, 0)


def dense(parts):
    lane = lax.broadcasted_iota(jnp.int32, parts[0].shape, 1)
    result = []
    for n in range(3):
        head = parts[0] if n == 0 else pltpu.roll(parts[n], 128 - 32 * n, 1)
        result.append(jnp.where(lane < 96 - 32 * n, head, pltpu.roll(parts[n + 1], 96 - 32 * n, 1)))
    return result


def loose(parts, clean):
    lane = lax.broadcasted_iota(jnp.int32, parts[0].shape, 1)
    result = [parts[0]]
    for k in (1, 2):
        result.append(jnp.where(lane < 32 * k, pltpu.roll(parts[k - 1], 32 * k, 1), pltpu.roll(parts[k], 32 * k, 1)))
    result.append(pltpu.roll(parts[2], 96, 1))
    return [jnp.where(lane < 96, value, 0.0) for value in result] if clean else result


def put_dense(v, x, c, parts):
    for n, tile in enumerate(dense(parts)):
        v.packed[x, c, n] = tile
        depth = v.front.shape[0]
        if x < depth:
            v.front[x, c, n] = tile
        if x >= 4 - depth:
            v.back[x - 4 + depth, c, n] = tile


def pack_kernel(v):
    loads = [
        pltpu.make_async_copy(v.right_side, v.field, v.sem.at[0]),
        pltpu.make_async_copy(v.layer_index, v.layers, v.sem.at[1]),
        pltpu.make_async_copy(v.absorb_level, v.levels, v.sem.at[2]),
        pltpu.make_async_copy(v.speeds, v.table, v.sem.at[3]),
    ]
    for load in loads:
        load.start()
    matrix = sort_matrix(384, 512, False)
    for load in loads:
        load.wait()
    field = exact_dot(v.field[...].reshape(64, 384), matrix)
    both = jnp.concatenate([v.layers[...].reshape(32, 384), v.levels[...].reshape(32, 384)], axis=0)
    codes = jnp.dot(both.astype(F32).astype(BF16), matrix, preferred_element_type=F32)
    inside = lax.broadcasted_iota(jnp.int32, (32, 128), 1) < 96
    total = [jnp.zeros((32, 128), F32), jnp.zeros((32, 128), F32)]
    reals, imags = [], []
    for r in range(4):
        lanes = slice(r * 128, r * 128 + 128)
        layer = codes[0:32, lanes]
        velocity = jnp.full((32, 128), v.table[0], F32)
        for n in range(1, v.table.shape[0]):
            velocity = jnp.where(layer == float(n), v.table[n], velocity)
        ratio = KH_FACTOR / velocity
        real = jnp.where(inside, ratio * ratio, 0.0)
        imag = -real * (BETA + ABSORB * codes[32:64, lanes])
        total = [total[0] + real, total[1] + imag]
        reals.append(real)
        imags.append(imag)
    for x in range(4):
        rows = slice(x * 8, x * 8 + 8)
        for c in range(2):
            at = 32 * c + x * 8
            put_dense(v, x, c, [field[at : at + 8, r * 128 : r * 128 + 128] for r in range(4)])
        put_dense(v, x, 2, [reals[r][rows] for r in range(4)])
        put_dense(v, x, 3, [imags[r][rows] for r in range(4)])
    means = []
    for c in range(2):
        t = total[c]
        v.temp[c] = (t[0:8] + t[8:16]) + (t[16:24] + t[24:32])
        row = [v.temp[c, n : n + 1] for n in range(8)]
        means.append([((row[4 * k] + row[4 * k + 1]) + (row[4 * k + 2] + row[4 * k + 3])) * (1.0 / 64.0) for k in range(2)])
    w = [scaled_inverse(means[0][k], means[1][k], 0.0625) for k in range(2)]
    v.inverse_two[...] = jnp.concatenate(dense([w[k][c] for c in range(2) for k in range(2)]), axis=1)


def pack(table, right_side, layer_index, absorb_level):
    return run(
        pack_kernel,
        dict(speeds=(table, HB), right_side=(right_side, HB), layer_index=(layer_index, HB), absorb_level=(absorb_level, HB)),
        dict(packed=((4, 4, 3, 8, 128), VM), front=((2, 4, 3, 8, 128), VM), back=((2, 4, 3, 8, 128), VM),
             inverse_two=((1, 384), VM)),
        dict(field=right_side.shape, layers=pltpu.VMEM(layer_index.shape, jnp.int32),
             levels=pltpu.VMEM(absorb_level.shape, jnp.int32), table=pltpu.SMEM(table.shape, F32), temp=(2, 8, 128)),
        4,
    )


FINE = (16, 2, 4, 24, 128)
WIDE = (16, 2, 4, 40, 128)
PART = (8, 2, 4, 24, 128)
INNER = (12, 2, 4, 24, 128)
COARSE = (6, 2, 2, 24, 128)
COARSE_WIDE = (6, 2, 2, 40, 128)


def keep(v, number, source, target):
    copy = pltpu.make_async_copy(source, target, v.sem.at[number])
    copy.start()
    return copy


def squeeze_rows(target, n, source, k, c, tile, top):
    for s in range(2):
        target[n, s * 4 : s * 4 + 4, :] = source[k, c, s, pl.ds(top + 8 * tile, 4, 2), :]


def down_body(v, source, weight, diag, weight_one, diag_one, first_copy):
    def first(x, _):
        for r in range(4):
            e = product([weight[x, c, r] for c in range(2)], [source[x, c, r] for c in range(2)])
            for c in range(2):
                v.start[x, c, r, 8:32, :] = e[c]
        return 0

    lax.fori_loop(0, 16, first, 0)
    sweep(v.start, v.guess, weight, 0, source, 0, 1, 15, 4, 1, 1.0)
    copies = [keep(v, first_copy, v.guess.at[2:14, :, :, 8:32, :], v.out_guess)]

    def residual(k, _):
        for s in range(2):
            sums = [None, None]
            for half in range(2):
                x = 2 + 2 * k + half
                for r in (2 * s, 2 * s + 1):
                    e = [v.guess[x, c, r, 8:32, :] for c in range(2)]
                    moved = product([diag[x, c, r] for c in range(2)], e)
                    for c in range(2):
                        value = source[x, c, r] + neighbour(v.guess, x, c, r, 4, 1) - moved[c]
                        sums[c] = value if sums[c] is None else sums[c] + value
            g = [pair_rows(sums[c], v.temp.at[c]) * 0.125 for c in range(2)]
            e = product([weight_one[k, c, s] for c in range(2)], g)
            for c in range(2):
                v.source_one[k, c, s] = g[c]
                v.start_one[k, c, s, 8:32, :] = e[c]
        return 0

    lax.fori_loop(0, 6, residual, 0)
    copies.append(keep(v, first_copy + 1, v.source_one, v.out_source_one))
    sweep(v.start_one, v.guess_one, weight_one, 0, v.source_one, 0, 1, 5, 2, 2, 0.25)
    copies.append(keep(v, first_copy + 2, v.guess_one, v.out_guess_one))

    total = [None, None]
    for k in (2, 3):
        for s in range(2):
            e = [v.guess_one[k, c, s, 8:32, :] for c in range(2)]
            moved = product([diag_one[k, c, s] for c in range(2)], e)
            for c in range(2):
                value = v.source_one[k, c, s] + 0.25 * neighbour(v.guess_one, k, c, s, 2, 2) - moved[c]
                total[c] = value if total[c] is None else total[c] + value
    pieces = []
    for c in range(2):
        v.temp[c, 8:32, :] = total[c]
        for k in range(2):
            row = 16 + 4 * k
            pieces.append((v.temp[c, row : row + 1, :] + v.temp[c, row + 2 : row + 3, :]) * 0.125)
    for n, tile in enumerate(dense(pieces)):
        v.two[0:1, n * 128 : n * 128 + 128] = tile

    for c in range(2):
        for k in range(4):
            squeeze_rows(v.send_y, k * 2 + c, v.guess_one, k + 1, c, 1, 8)
        for tile in range(3):
            for k in range(2):
                n = (k * 3 + tile) * 2 + c
                squeeze_rows(v.send_up, n, v.guess_one, k + 1, c, tile, 8)
                squeeze_rows(v.send_down, n, v.guess_one, k + 3, c, tile, 8)
    return copies


def fill(v, target, at, count, x):
    for c in range(count):
        for tile, ref in enumerate((v.low, v.mid, v.high)):
            parts = loose([ref[x, at + c, n] for n in range(3)], at + c == 2)
            for r in range(4):
                target[x, c, r, 8 * tile : 8 * tile + 8, :] = parts[r]


def clear_down(v):
    clear_edges(v.start, 16)
    clear_edges(v.guess, 16)
    clear_edges(v.start_one, 6)
    clear_edges(v.guess_one, 6)


def down_first_kernel(v):
    clear_down(v)

    def filled(x, _):
        fill(v, v.source, 0, 2, x)
        fill(v, v.diag, 2, 2, x)
        for r in range(4):
            w = scaled_inverse(v.diag[x, 0, r], v.diag[x, 1, r], 1.0)
            for c in range(2):
                v.weight[x, c, r] = w[c]
        return 0

    lax.fori_loop(0, 16, filled, 0)
    copies = [keep(v, 0, v.source, v.out_source), keep(v, 1, v.weight, v.out_weight)]

    def coarse(k, _):
        for s in range(2):
            shift = []
            for c in range(2):
                total = None
                for half in range(2):
                    for r in (2 * s, 2 * s + 1):
                        value = v.diag[2 + 2 * k + half, c, r]
                        total = value if total is None else total + value
                shift.append(pair_rows(total, v.temp.at[c]) * 0.125)
            w = scaled_inverse(shift[0], shift[1], 0.25)
            d = (1.5 - shift[0], -shift[1])
            for c in range(2):
                v.weight_one[k, c, s] = w[c]
                v.diag_one[k, c, s] = d[c]
        return 0

    lax.fori_loop(0, 6, coarse, 0)

    def turn(x, _):
        for r in range(4):
            v.diag[x, 0, r] = 6.0 - v.diag[x, 0, r]
            v.diag[x, 1, r] = -v.diag[x, 1, r]
        return 0

    lax.fori_loop(0, 16, turn, 0)
    copies += [keep(v, 2, v.diag, v.out_diag), keep(v, 3, v.weight_one, v.out_weight_one),
               keep(v, 4, v.diag_one, v.out_diag_one)]
    copies += down_body(v, v.source, v.weight, v.diag, v.weight_one, v.diag_one, 5)
    for copy in copies:
        copy.wait()


def down_first(mid, low, high):
    return run(
        down_first_kernel,
        dict(mid=(mid, VM), low=(low, VM), high=(high, VM)),
        dict(out_source=(FINE, HB), out_weight=(FINE, HB), out_diag=(FINE, HB), out_weight_one=(COARSE, HB),
             out_diag_one=(COARSE, HB), out_guess=(INNER, HB), out_source_one=(COARSE, HB), out_guess_one=(COARSE_WIDE, HB),
             two=((1, 384), VM), send_y=((8, 8, 128), VM), send_up=((12, 8, 128), VM), send_down=((12, 8, 128), VM)),
        dict(source=FINE, weight=FINE, diag=FINE, weight_one=COARSE, diag_one=COARSE, start=WIDE, guess=WIDE,
             start_one=COARSE_WIDE, source_one=COARSE, guess_one=COARSE_WIDE, temp=(2, 40, 128)),
        8,
    )


EDGE = 18 * 2 * 3


def down_second_kernel(v):
    loads = [keep(v, 0, v.in_right, v.right), keep(v, 1, v.in_diag, v.diag), keep(v, 2, v.in_weight, v.weight),
             keep(v, 3, v.in_weight_one, v.weight_one), keep(v, 4, v.in_diag_one, v.diag_one)]
    clear_down(v)
    clear_edges(v.first, 18)

    def filled(x, _):
        for c in range(2):
            for tile, ref in enumerate((v.low, v.mid, v.high)):
                parts = loose([ref[(x * 2 + c) * 3 + n] for n in range(3)], True)
                for r in range(4):
                    v.first[x, c, r, 8 + 8 * tile : 16 + 8 * tile, :] = parts[r]
        return 0

    lax.fori_loop(0, 18, filled, 0)
    for x in range(4):
        for c in range(2):
            for r in range(4):
                row = slice(c * 4 + r, c * 4 + r + 1)
                v.first[x + 7, c, r, 7:8, :] = v.low[EDGE + x, row]
                v.first[x + 7, c, r, 32:33, :] = v.high[EDGE + 4 + x, row]
    for load in loads[0:2]:
        load.wait()

    def residual(x, _):
        for r in range(4):
            moved = product([v.diag[x, c, r] for c in range(2)], [v.first[x + 1, c, r, 8:32, :] for c in range(2)])
            for c in range(2):
                v.source[x, c, r] = v.right[x, c, r] + neighbour(v.first, x + 1, c, r, 4, 1) - moved[c]
        return 0

    lax.fori_loop(0, 16, residual, 0)
    for load in loads[2:5]:
        load.wait()
    copies = [keep(v, 8, v.source.at[4:12], v.out_source)]
    copies += down_body(v, v.source, v.weight, v.diag, v.weight_one, v.diag_one, 5)
    for copy in copies:
        copy.wait()


def down_second(mid, low, high, old):
    return run(
        down_second_kernel,
        dict(mid=(mid, VM), low=(low, VM), high=(high, VM), in_right=(old.out_source, HB), in_weight=(old.out_weight, HB),
             in_diag=(old.out_diag, HB), in_weight_one=(old.out_weight_one, HB), in_diag_one=(old.out_diag_one, HB)),
        dict(out_source=(PART, HB), out_guess=(INNER, HB), out_source_one=(COARSE, HB), out_guess_one=(COARSE_WIDE, HB),
             two=((1, 384), VM), send_y=((8, 8, 128), VM), send_up=((12, 8, 128), VM), send_down=((12, 8, 128), VM)),
        dict(source=FINE, weight=FINE, diag=FINE, weight_one=COARSE, diag_one=COARSE, start=WIDE, guess=WIDE,
             start_one=COARSE_WIDE, source_one=COARSE, guess_one=COARSE_WIDE, temp=(2, 40, 128),
             right=FINE, first=(18, 2, 4, 40, 128)),
        9,
    )


def over(low, count, block, body):
    def several(number, _):
        for n in range(block):
            body(low + number * block + n)
        return 0

    lax.fori_loop(0, count // block, several, 0)
    for n in range(count - count % block, count):
        body(low + n)


def unpack_two(packed, begin, target, window, clean):
    def body(x):
        parts = [packed[begin + x, :, n * 128 : n * 128 + 128] for n in range(3)]
        for k, part in enumerate(loose(parts, clean)):
            target[x, k] = part

    over(0, window, 7, body)


def solve_two(own, source, weight, ping, pong, window, groups):
    clear(ping, window + 8)
    clear(pong, window + 8)
    rows = slice(8, 8 + groups)

    def start(x):
        for k in range(2):
            e = product([weight[x, k], weight[x, 2 + k]], [source[x, k], source[x, 2 + k]])
            for c in range(2):
                ping[x + 4, c * 2 + k, rows, :] = e[c]

    over(0, window, 7, start)

    def step(old, new, left):
        def body(x):
            here = [old[x + 4, n, rows, :] for n in range(4)]
            for k in range(2):
                parts = []
                for c in range(2):
                    n, other = c * 2 + k, c * 2 + 1 - k
                    side = old[x + 4, other, 7 : 7 + groups, :] if k == 0 else old[x + 4, other, 9 : 9 + groups, :]
                    total = (old[x + 3, n, rows, :] + old[x + 5, n, rows, :]) + (here[other] + side)
                    total = total + (pltpu.roll(here[n], 1, 1) + pltpu.roll(here[n], 127, 1))
                    parts.append(source[x, n] + 0.0625 * total)
                moved = product([weight[x, k], weight[x, 2 + k]], parts)
                for c in range(2):
                    new[x + 4, c * 2 + k, rows, :] = (1.0 - OMEGA) * here[c * 2 + k] + moved[c]

        count = min(window, 2 * (3 + left) + 1)
        over(jnp.clip(own - 3 - left, 0, window - count), count, 4, body)

    pairs = (ping, pong)
    for number in range(NC - 1):
        step(pairs[number % 2], pairs[(number + 1) % 2], NC - 2 - number)
    return pairs[(NC - 1) % 2]


def spread_rows(target, top, x, c, tile, block):
    for s in range(2):
        for twice in range(2):
            target[x, c, s, pl.ds(top + 8 * tile + twice, 4, 2), :] = block[s * 4 : s * 4 + 4, :]


def add_two(answer, gx, gy, one, first, count):
    row = lax.broadcasted_iota(jnp.int32, (8, 128), 0)
    for j in range(count):
        x = gx + 4 + (first + j) // 2
        for c in range(2):
            for tile in range(3):
                spot = gy + 7 + tile
                low = jnp.broadcast_to(answer[x, c * 2, pl.ds(spot, 1), :], (8, 128))
                high = jnp.broadcast_to(answer[x, c * 2 + 1, pl.ds(spot, 1), :], (8, 128))
                value = jnp.where(row < 4, low, high)
                at = slice(8 + 8 * tile, 16 + 8 * tile)
                for s in range(2):
                    one[j, c, s, at, :] = one[j, c, s, at, :] + value


def up_kernel(v, planes, groups, second):
    count = 8
    loads = []
    if second:
        loads.append(keep(v, 7, v.in_weight_two, v.weight_two))
    own = v.in_source if second else v.in_source.at[4:12]
    loads += [keep(v, 0, own, v.source.at[4:12]), keep(v, 1, v.in_weight.at[4:12], v.weight.at[4:12]),
              keep(v, 2, v.in_guess, v.guess.at[2:14]), keep(v, 3, v.in_guess_one, v.guess_one),
              keep(v, 4, v.in_source_one, v.source_one), keep(v, 5, v.in_weight_one, v.weight_one)]
    if second:
        loads.append(keep(v, 6, v.in_first, v.first))
        v.matrix[...] = sort_matrix(512, 384, True)
    window = min(planes, WINDOW)
    begin = jnp.clip(v.where[0] - 10, 0, planes - window)
    unpack_two(v.gathered, begin, v.source_two, window, False)
    copies = []
    if second:
        loads.pop(0).wait()
    else:
        unpack_two(v.gathered_weight, begin, v.weight_two, window, True)
        copies.append(keep(v, 7, v.weight_two, v.out_weight_two))
    answer = solve_two(v.where[0] - begin, v.source_two, v.weight_two, v.ping, v.pong, window, groups)
    clear_edges(v.one, count)
    clear_edges(v.one_next, count)
    clear_edges(v.ea, 12, 4)
    clear_edges(v.eb, 11, 5)
    for load in loads:
        load.wait()

    for k in range(4):
        for c in range(2):
            for s in range(2):
                v.one[k + 2, c, s, 16:24, :] = v.guess_one[k + 1, c, s, 16:24, :]
            spread_rows(v.one, 8, k + 2, c, 0, v.from_y_low[k * 2 + c])
            spread_rows(v.one, 8, k + 2, c, 2, v.from_y_high[k * 2 + c])
    for c in range(2):
        for tile in range(3):
            for k in range(2):
                n = (k * 3 + tile) * 2 + c
                spread_rows(v.one, 8, k, c, tile, v.from_low[n])
                spread_rows(v.one, 8, 6 + k, c, tile, v.from_high[n])
    add_two(answer, v.where[0] - begin, v.where[1], v.one, -3, count)
    sweep(v.one, v.one_next, v.weight_one, -1, v.source_one, -1, 1, 7, 2, 2, 0.25)
    sweep(v.one_next, v.one, v.weight_one, -1, v.source_one, -1, 2, 6, 2, 2, 0.25)

    def correct(j, _):
        for half in range(2):
            x = 2 * j + half
            for r in range(4):
                for c in range(2):
                    v.ea[x, c, r, 8:32, :] = v.guess[x, c, r] + v.one[j, c, r // 2, 8:32, :]
        return 0

    lax.fori_loop(2, 6, correct, 0)
    sweep(v.ea, v.eb, v.weight, 0, v.source, 0, 5, 11, 4, 1, 1.0)
    sweep(v.eb, v.ea, v.weight, 0, v.source, 0, 6, 10, 4, 1, 1.0)
    return copies


def up_first_kernel(v, planes, groups):
    copies = up_kernel(v, planes, groups, False)
    for x in range(4):
        for c in range(2):
            for r in range(4):
                v.first[x, c, r] = v.ea[x + 6, c, r, 16:24, :]
                row = slice(c * 4 + r, c * 4 + r + 1)
                v.edges[x, row] = v.ea[x + 6, c, r, 15:16, :]
                v.edges[x + 4, row] = v.ea[x + 6, c, r, 24:25, :]
            put_dense(v, x, c, [v.ea[x + 6, c, r, 16:24, :] for r in range(4)])
    copies.append(keep(v, 8, v.first, v.out_first))
    for copy in copies:
        copy.wait()


def up_second_kernel(v, planes, groups):
    up_kernel(v, planes, groups, True)
    blocks = []
    for c in range(2):
        for x in range(4):
            blocks.append(
                jnp.concatenate([v.first[x, c, r] + v.ea[x + 6, c, r, 16:24, :] for r in range(4)], axis=1)
            )
    values = jnp.concatenate(blocks, axis=0)
    v.result[...] = exact_dot(values, v.matrix[...]).reshape(2, 4, 8, 384)


def up_scratch(planes, groups):
    level = (8, 2, 2, 40, 128)
    two = (min(planes, WINDOW) + 8, 4, 16 + groups, 128)
    source = (min(planes, WINDOW), 4, groups, 128)
    return dict(source=FINE, weight=FINE, guess=FINE, guess_one=COARSE_WIDE, source_one=COARSE, weight_one=COARSE,
                source_two=source, weight_two=source, ping=two, pong=two,
                one=level, one_next=level, ea=WIDE, eb=WIDE, first=(4, 2, 4, 8, 128))


def up_inputs(where, gathered, messages, down, first_down):
    return dict(where=(where, SM), gathered=(gathered, VM), **{name: (array, VM) for name, array in messages.items()},
                in_source=(down.out_source, HB), in_weight=(first_down.out_weight, HB), in_guess=(down.out_guess, HB),
                in_guess_one=(down.out_guess_one, HB), in_source_one=(down.out_source_one, HB),
                in_weight_one=(first_down.out_weight_one, HB))


def up_first(where, gathered, gathered_weight, messages, down):
    planes, groups = gathered.shape[0], gathered.shape[1]
    return run(
        lambda v: up_first_kernel(v, planes, groups),
        dict(**up_inputs(where, gathered, messages, down, down), gathered_weight=(gathered_weight, VM)),
        dict(packed=((4, 2, 3, 8, 128), VM), front=((3, 2, 3, 8, 128), VM), back=((3, 2, 3, 8, 128), VM),
             edges=((8, 8, 128), VM), out_first=((4, 2, 4, 8, 128), HB), out_weight_two=((min(planes, WINDOW), 4, groups, 128), HB)),
        up_scratch(planes, groups),
        9,
    )


def up_second(where, gathered, messages, down, first_down, first_up):
    planes, groups = gathered.shape[0], gathered.shape[1]
    return run(
        lambda v: up_second_kernel(v, planes, groups),
        dict(**up_inputs(where, gathered, messages, down, first_down), in_weight_two=(first_up.out_weight_two, HB),
             in_first=(first_up.out_first, HB)),
        dict(result=((2, 4, 8, 384), VM)),
        dict(**up_scratch(planes, groups), matrix=pltpu.VMEM((512, 384), BF16)),
        8,
    ).result


def shifted(block, axis, by):
    count = lax.axis_size(axis)
    pairs = [(i, i + by) for i in range(count) if 0 <= i + by < count]
    return lax.ppermute(block, axis, pairs)


def gather_two(row):
    count_y, count_x = lax.axis_size("gy"), lax.axis_size("gx")
    width = row.shape[1]
    sent = jnp.broadcast_to(row[None], (count_x * count_y, 1, width))
    return lax.all_to_all(sent, ("gx", "gy"), 0, 0).reshape(count_x, count_y, width)


def beside(own):
    after = shifted(own.front, "gx", -2)
    return jnp.concatenate(
        [
            shifted(own.back, "gx", 2),
            shifted(own.packed, "gx", 1),
            own.packed,
            shifted(own.packed, "gx", -1),
            after,
        ]
    )


def surround(mid):
    return mid, shifted(mid, "gy", 1), shifted(mid, "gy", -1)


def exchange_one(down):
    return dict(
        from_y_low=shifted(down.send_y, "gy", 1),
        from_y_high=shifted(down.send_y, "gy", -1),
        from_low=shifted(down.send_up, "gx", 1),
        from_high=shifted(down.send_down, "gx", -1),
    )


def local(right_side, velocity_table, layer_index, absorb_level):
    where = jnp.stack([lax.axis_index("gx"), lax.axis_index("gy")]).astype(jnp.int32)
    packed = pack(velocity_table, right_side, layer_index, absorb_level)
    weight_two = gather_two(packed.inverse_two)
    mid = beside(packed)
    down = down_first(*surround(mid))
    middle = up_first(where, gather_two(down.two), weight_two, exchange_one(down), down)
    rows = jnp.concatenate([beside(middle).reshape(EDGE, 8, 128), middle.edges])
    again = down_second(*surround(rows), down)
    return up_second(where, gather_two(again.two), exchange_one(again), again, down, middle)


def solution(mesh):
    placed = (P(None, "gx", "gy", None), P(), P("gx", "gy", None), P("gx", "gy", None))
    return jax.shard_map(
        local, mesh=mesh, in_specs=placed, out_specs=P(None, "gx", "gy", None), check_vma=False
    )
```

```python
import math
from types import SimpleNamespace

import jax
import jax.numpy as jnp
from jax import lax
from jax.experimental import pallas as pl
from jax.experimental.pallas import tpu as pltpu
from jax.sharding import PartitionSpec as P


NC = 8
WINDOW = 21
OMEGA = 0.6
BETA = 0.5
ABSORB = 0.25
KH_FACTOR = 2.0 * math.pi * 6.0 * 20.0

F32 = jnp.float32
BF16 = jnp.bfloat16
VM = pltpu.VMEM
SM = pltpu.SMEM
HB = pltpu.HBM
PARAMS = pltpu.CompilerParams(vmem_limit_bytes=32 * 1024 * 1024)


def run(name, kernel, inputs, outputs, scratch, copies):
    names = list(inputs) + list(outputs) + list(scratch) + ["sem"]
    result = pl.pallas_call(
        lambda *refs: kernel(SimpleNamespace(**dict(zip(names, refs)))),
        name=name,
        out_shape=tuple(HB(dims, F32) if space is HB else jax.ShapeDtypeStruct(dims, F32) for dims, space in outputs.values()),
        in_specs=[pl.BlockSpec(memory_space=space) for _, space in inputs.values()],
        out_specs=tuple(pl.BlockSpec(memory_space=space) for _, space in outputs.values()),
        scratch_shapes=[pltpu.VMEM(dims, F32) if isinstance(dims, tuple) else dims for dims in scratch.values()]
        + [pltpu.SemaphoreType.DMA((copies,))],
        compiler_params=PARAMS,
    )(*[pltpu.with_memory_space_constraint(array, HB) if space is HB else array for array, space in inputs.values()])
    return SimpleNamespace(**dict(zip(outputs, result)))


def sort_matrix(rows, columns, flip):
    first = lax.broadcasted_iota(jnp.int32, (rows, columns), 0)
    second = lax.broadcasted_iota(jnp.int32, (rows, columns), 1)
    if flip:
        first, second = second, first
    lane = second % 128
    hit = (first == 4 * lane + second // 128) & (lane < 96)
    return jnp.where(hit, 1.0, 0.0).astype(BF16)


def exact_dot(values, matrix):
    high = values.astype(BF16)
    rest = values - high.astype(F32)
    middle = rest.astype(BF16)
    low = (rest - middle.astype(F32)).astype(BF16)
    dot = lambda part: jnp.dot(part, matrix, preferred_element_type=F32)
    return (dot(low) + dot(middle)) + dot(high)


def scaled_inverse(real, imag, scale):
    diag_real = 6.0 * scale - real
    diag_imag = -imag
    factor = OMEGA / (diag_real * diag_real + diag_imag * diag_imag)
    factor = jnp.where(real > 0.0, factor, 0.0)
    return diag_real * factor, -diag_imag * factor


def product(a, b):
    return a[0] * b[0] - a[1] * b[1], a[0] * b[1] + a[1] * b[0]


def pair_rows(value, temp):
    temp[8:32, :] = value
    row = lax.broadcasted_iota(jnp.int32, (24, 128), 0)
    return value + jnp.where(row % 2 == 0, temp[9:33, :], temp[7:31, :])


def neighbour(ref, x, c, r, count, step, low=8, high=32):
    center = lambda s: ref[x, c, s, low:high, :]
    up = center(r + 1) if r < count - 1 else pltpu.roll(center(0), 127, 1)
    down = center(r - 1) if r > 0 else pltpu.roll(center(count - 1), 1, 1)
    total = ref[x - 1, c, r, low:high, :] + ref[x + 1, c, r, low:high, :]
    total = total + ref[x, c, r, low - step : high - step, :] + ref[x, c, r, low + step : high + step, :]
    return total + (up + down)


def sweep(old, new, weight, weight_at, source, source_at, low, high, count, step, scale, rows=(8, 32)):
    top, bottom = rows
    inner = slice(top - 8, bottom - 8)

    def body(x, _):
        for r in range(count):
            parts = []
            for c in range(2):
                total = neighbour(old, x, c, r, count, step, top, bottom)
                if scale != 1.0:
                    total = total * scale
                parts.append(source[x + source_at, c, r, inner, :] + total)
            w = [weight[x + weight_at, c, r, inner, :] for c in range(2)]
            moved = product(w, parts)
            for c in range(2):
                new[x, c, r, top:bottom, :] = (1.0 - OMEGA) * old[x, c, r, top:bottom, :] + moved[c]
        return 0

    lax.fori_loop(low, high, body, 0)


def clear(ref, count):
    def body(x, _):
        ref[x] = jnp.zeros(ref.shape[1:], F32)
        return 0

    lax.fori_loop(0, count, body, 0)


def clear_edges(ref, count, begin=0):
    zero = jnp.zeros((8, 128), F32)

    def body(x, _):
        for c in range(2):
            for r in range(ref.shape[2]):
                ref[x, c, r, 0:8, :] = zero
                ref[x, c, r, 32:40, :] = zero
        return 0

    lax.fori_loop(begin, count, body, 0)


def dense(parts):
    lane = lax.broadcasted_iota(jnp.int32, parts[0].shape, 1)
    result = []
    for n in range(3):
        head = parts[0] if n == 0 else pltpu.roll(parts[n], 128 - 32 * n, 1)
        result.append(jnp.where(lane < 96 - 32 * n, head, pltpu.roll(parts[n + 1], 96 - 32 * n, 1)))
    return result


def loose(parts, clean):
    lane = lax.broadcasted_iota(jnp.int32, parts[0].shape, 1)
    result = [parts[0]]
    for k in (1, 2):
        result.append(jnp.where(lane < 32 * k, pltpu.roll(parts[k - 1], 32 * k, 1), pltpu.roll(parts[k], 32 * k, 1)))
    result.append(pltpu.roll(parts[2], 96, 1))
    return [jnp.where(lane < 96, value, 0.0) for value in result] if clean else result


def put_dense(v, x, c, parts):
    for n, tile in enumerate(dense(parts)):
        v.packed[x, c, n] = tile
        depth = v.front.shape[0]
        if x < depth:
            v.front[x, c, n] = tile
        if x >= 4 - depth:
            v.back[x - 4 + depth, c, n] = tile


def pack_kernel(v):
    loads = [
        pltpu.make_async_copy(v.right_side, v.field, v.sem.at[0]),
        pltpu.make_async_copy(v.layer_index, v.layers, v.sem.at[1]),
        pltpu.make_async_copy(v.absorb_level, v.levels, v.sem.at[2]),
        pltpu.make_async_copy(v.speeds, v.table, v.sem.at[3]),
    ]
    for load in loads:
        load.start()
    matrix = sort_matrix(384, 512, False)
    for load in loads:
        load.wait()
    field = exact_dot(v.field[...].reshape(64, 384), matrix)
    both = jnp.concatenate([v.layers[...].reshape(32, 384), v.levels[...].reshape(32, 384)], axis=0)
    codes = jnp.dot(both.astype(F32).astype(BF16), matrix, preferred_element_type=F32)
    inside = lax.broadcasted_iota(jnp.int32, (32, 128), 1) < 96
    total = [jnp.zeros((32, 128), F32), jnp.zeros((32, 128), F32)]
    reals, imags = [], []
    for r in range(4):
        lanes = slice(r * 128, r * 128 + 128)
        layer = codes[0:32, lanes]
        velocity = jnp.full((32, 128), v.table[0], F32)
        for n in range(1, v.table.shape[0]):
            velocity = jnp.where(layer == float(n), v.table[n], velocity)
        ratio = KH_FACTOR / velocity
        real = jnp.where(inside, ratio * ratio, 0.0)
        imag = -real * (BETA + ABSORB * codes[32:64, lanes])
        total = [total[0] + real, total[1] + imag]
        reals.append(real)
        imags.append(imag)
    for x in range(4):
        rows = slice(x * 8, x * 8 + 8)
        for c in range(2):
            at = 32 * c + x * 8
            put_dense(v, x, c, [field[at : at + 8, r * 128 : r * 128 + 128] for r in range(4)])
        put_dense(v, x, 2, [reals[r][rows] for r in range(4)])
        put_dense(v, x, 3, [imags[r][rows] for r in range(4)])
    means = []
    for c in range(2):
        t = total[c]
        v.temp[c] = (t[0:8] + t[8:16]) + (t[16:24] + t[24:32])
        row = [v.temp[c, n : n + 1] for n in range(8)]
        means.append([((row[4 * k] + row[4 * k + 1]) + (row[4 * k + 2] + row[4 * k + 3])) * (1.0 / 64.0) for k in range(2)])
    w = [scaled_inverse(means[0][k], means[1][k], 0.0625) for k in range(2)]
    v.inverse_two[...] = jnp.concatenate(dense([w[k][c] for c in range(2) for k in range(2)]), axis=1)


def pack(table, right_side, layer_index, absorb_level):
    return run(
        "pack",
        pack_kernel,
        dict(speeds=(table, HB), right_side=(right_side, HB), layer_index=(layer_index, HB), absorb_level=(absorb_level, HB)),
        dict(packed=((4, 4, 3, 8, 128), VM), front=((2, 4, 3, 8, 128), VM), back=((2, 4, 3, 8, 128), VM),
             inverse_two=((1, 384), VM)),
        dict(field=right_side.shape, layers=pltpu.VMEM(layer_index.shape, jnp.int32),
             levels=pltpu.VMEM(absorb_level.shape, jnp.int32), table=pltpu.SMEM(table.shape, F32), temp=(2, 8, 128)),
        4,
    )


FINE = (16, 2, 4, 24, 128)
WIDE = (16, 2, 4, 40, 128)
PART = (8, 2, 4, 24, 128)
INNER = (12, 2, 4, 24, 128)
COARSE = (6, 2, 2, 24, 128)
COARSE_WIDE = (6, 2, 2, 40, 128)


def keep(v, number, source, target):
    copy = pltpu.make_async_copy(source, target, v.sem.at[number])
    copy.start()
    return copy


def squeeze_rows(target, n, source, k, c, tile, top):
    for s in range(2):
        target[n, s * 4 : s * 4 + 4, :] = source[k, c, s, pl.ds(top + 8 * tile, 4, 2), :]


def down_body(v, source, weight, diag, weight_one, diag_one, first_copy):
    sweep(v.start, v.guess, weight, 0, source, 0, 1, 15, 4, 1, 1.0)
    copies = [keep(v, first_copy, v.guess.at[2:14, :, :, 8:32, :], v.out_guess)]

    def residual(k, _):
        for s in range(2):
            sums = [None, None]
            for half in range(2):
                x = 2 + 2 * k + half
                for r in (2 * s, 2 * s + 1):
                    e = [v.guess[x, c, r, 8:32, :] for c in range(2)]
                    moved = product([diag[x, c, r] for c in range(2)], e)
                    for c in range(2):
                        value = source[x, c, r] + neighbour(v.guess, x, c, r, 4, 1) - moved[c]
                        sums[c] = value if sums[c] is None else sums[c] + value
            g = [pair_rows(sums[c], v.temp.at[c]) * 0.125 for c in range(2)]
            e = product([weight_one[k, c, s] for c in range(2)], g)
            for c in range(2):
                v.source_one[k, c, s] = g[c]
                v.start_one[k, c, s, 8:32, :] = e[c]
        return 0

    lax.fori_loop(0, 6, residual, 0)
    copies.append(keep(v, first_copy + 1, v.source_one, v.out_source_one))
    sweep(v.start_one, v.guess_one, weight_one, 0, v.source_one, 0, 1, 5, 2, 2, 0.25)
    copies.append(keep(v, first_copy + 2, v.guess_one, v.out_guess_one))

    total = [None, None]
    for k in (2, 3):
        for s in range(2):
            e = [v.guess_one[k, c, s, 8:32, :] for c in range(2)]
            moved = product([diag_one[k, c, s] for c in range(2)], e)
            for c in range(2):
                value = v.source_one[k, c, s] + 0.25 * neighbour(v.guess_one, k, c, s, 2, 2) - moved[c]
                total[c] = value if total[c] is None else total[c] + value
    pieces = []
    for c in range(2):
        v.temp[c, 8:32, :] = total[c]
        for k in range(2):
            row = 16 + 4 * k
            pieces.append((v.temp[c, row : row + 1, :] + v.temp[c, row + 2 : row + 3, :]) * 0.125)
    for n, tile in enumerate(dense(pieces)):
        v.two[0:1, n * 128 : n * 128 + 128] = tile

    for c in range(2):
        for k in range(4):
            squeeze_rows(v.send_y, k * 2 + c, v.guess_one, k + 1, c, 1, 8)
        for tile in range(3):
            for k in range(2):
                n = (k * 3 + tile) * 2 + c
                squeeze_rows(v.send_up, n, v.guess_one, k + 1, c, tile, 8)
                squeeze_rows(v.send_down, n, v.guess_one, k + 3, c, tile, 8)
    return copies


def fill(v, target, at, count, x):
    for c in range(count):
        for tile, ref in enumerate((v.low, v.mid, v.high)):
            parts = loose([ref[x, at + c, n] for n in range(3)], at + c == 2)
            for r in range(4):
                target[x, c, r, 8 * tile : 8 * tile + 8, :] = parts[r]


def begin_from(v, x, r, source, weight):
    e = product(weight, source)
    for c in range(2):
        v.start[x, c, r, 8:32, :] = e[c]


def clear_down(v):
    clear_edges(v.start, 16)
    clear_edges(v.guess, 16)
    clear_edges(v.start_one, 6)
    clear_edges(v.guess_one, 6)


def down_first_kernel(v):
    clear_down(v)

    def filled(x, _):
        fill(v, v.source, 0, 2, x)
        fill(v, v.diag, 2, 2, x)
        for r in range(4):
            w = scaled_inverse(v.diag[x, 0, r], v.diag[x, 1, r], 1.0)
            for c in range(2):
                v.weight[x, c, r] = w[c]
            begin_from(v, x, r, [v.source[x, c, r] for c in range(2)], w)
        return 0

    lax.fori_loop(0, 16, filled, 0)
    copies = [keep(v, 0, v.source, v.out_source), keep(v, 1, v.weight, v.out_weight)]

    def coarse(k, _):
        for s in range(2):
            shift = []
            for c in range(2):
                total = None
                for half in range(2):
                    for r in (2 * s, 2 * s + 1):
                        value = v.diag[2 + 2 * k + half, c, r]
                        total = value if total is None else total + value
                shift.append(pair_rows(total, v.temp.at[c]) * 0.125)
            w = scaled_inverse(shift[0], shift[1], 0.25)
            d = (1.5 - shift[0], -shift[1])
            for c in range(2):
                v.weight_one[k, c, s] = w[c]
                v.diag_one[k, c, s] = d[c]
        return 0

    lax.fori_loop(0, 6, coarse, 0)

    def turn(x, _):
        for r in range(4):
            v.diag[x, 0, r] = 6.0 - v.diag[x, 0, r]
            v.diag[x, 1, r] = -v.diag[x, 1, r]
        return 0

    lax.fori_loop(0, 16, turn, 0)
    copies += [keep(v, 2, v.diag, v.out_diag), keep(v, 3, v.weight_one, v.out_weight_one),
               keep(v, 4, v.diag_one, v.out_diag_one)]
    copies += down_body(v, v.source, v.weight, v.diag, v.weight_one, v.diag_one, 5)
    v.two[0:1, 384:768] = v.inverse_two[...]
    for copy in copies:
        copy.wait()


def down_first(mid, low, high, inverse_two):
    return run(
        "down_first",
        down_first_kernel,
        dict(mid=(mid, VM), low=(low, VM), high=(high, VM), inverse_two=(inverse_two, VM)),
        dict(out_source=(FINE, HB), out_weight=(FINE, HB), out_diag=(FINE, HB), out_weight_one=(COARSE, HB),
             out_diag_one=(COARSE, HB), out_guess=(INNER, HB), out_source_one=(COARSE, HB), out_guess_one=(COARSE_WIDE, HB),
             two=((1, 768), VM), send_y=((8, 8, 128), VM), send_up=((12, 8, 128), VM), send_down=((12, 8, 128), VM)),
        dict(source=FINE, weight=FINE, diag=FINE, weight_one=COARSE, diag_one=COARSE, start=WIDE, guess=WIDE,
             start_one=COARSE_WIDE, source_one=COARSE, guess_one=COARSE_WIDE, temp=(2, 40, 128)),
        8,
    )


EDGE = 18 * 2 * 3


def down_second_kernel(v):
    loads = [keep(v, 0, v.in_right, v.right), keep(v, 1, v.in_diag, v.diag), keep(v, 2, v.in_weight, v.weight),
             keep(v, 3, v.in_weight_one, v.weight_one), keep(v, 4, v.in_diag_one, v.diag_one)]
    clear_down(v)
    clear_edges(v.first, 18)

    def filled(x, _):
        for c in range(2):
            for tile, ref in enumerate((v.low, v.mid, v.high)):
                parts = loose([ref[(x * 2 + c) * 3 + n] for n in range(3)], True)
                for r in range(4):
                    v.first[x, c, r, 8 + 8 * tile : 16 + 8 * tile, :] = parts[r]
        return 0

    lax.fori_loop(0, 18, filled, 0)
    for x in range(4):
        for c in range(2):
            for r in range(4):
                row = slice(c * 4 + r, c * 4 + r + 1)
                v.first[x + 7, c, r, 7:8, :] = v.low[EDGE + x, row]
                v.first[x + 7, c, r, 32:33, :] = v.high[EDGE + 4 + x, row]
    for load in loads[0:3]:
        load.wait()

    def residual(x, _):
        for r in range(4):
            moved = product([v.diag[x, c, r] for c in range(2)], [v.first[x + 1, c, r, 8:32, :] for c in range(2)])
            value = [v.right[x, c, r] + neighbour(v.first, x + 1, c, r, 4, 1) - moved[c] for c in range(2)]
            for c in range(2):
                v.source[x, c, r] = value[c]
            begin_from(v, x, r, value, [v.weight[x, c, r] for c in range(2)])
        return 0

    lax.fori_loop(0, 16, residual, 0)
    copies = [keep(v, 8, v.source.at[4:12], v.out_source)]
    for load in loads[3:5]:
        load.wait()
    copies += down_body(v, v.source, v.weight, v.diag, v.weight_one, v.diag_one, 5)
    for copy in copies:
        copy.wait()


def down_second(mid, low, high, old):
    return run(
        "down_second",
        down_second_kernel,
        dict(mid=(mid, VM), low=(low, VM), high=(high, VM), in_right=(old.out_source, HB), in_weight=(old.out_weight, HB),
             in_diag=(old.out_diag, HB), in_weight_one=(old.out_weight_one, HB), in_diag_one=(old.out_diag_one, HB)),
        dict(out_source=(PART, HB), out_guess=(INNER, HB), out_source_one=(COARSE, HB), out_guess_one=(COARSE_WIDE, HB),
             two=((1, 384), VM), send_y=((8, 8, 128), VM), send_up=((12, 8, 128), VM), send_down=((12, 8, 128), VM)),
        dict(source=FINE, weight=FINE, diag=FINE, weight_one=COARSE, diag_one=COARSE, start=WIDE, guess=WIDE,
             start_one=COARSE_WIDE, source_one=COARSE, guess_one=COARSE_WIDE, temp=(2, 40, 128),
             right=FINE, first=(18, 2, 4, 40, 128)),
        9,
    )


def over(low, count, block, body):
    def several(number, _):
        for n in range(block):
            body(low + number * block + n)
        return 0

    lax.fori_loop(0, count // block, several, 0)
    for n in range(count - count % block, count):
        body(low + n)


def unpack_two(packed, first, begin, target, window, clean):
    def body(x):
        parts = [packed[begin + x, :, first + n * 128 : first + n * 128 + 128] for n in range(3)]
        for k, part in enumerate(loose(parts, clean)):
            target[x, k] = part

    over(0, window, 7, body)


def solve_two(own, source, weight, ping, pong, window, planes, groups):
    clear(ping, window + 8)
    clear(pong, window + 8)
    rows = slice(8, 8 + groups)

    def start(x):
        for k in range(2):
            e = product([weight[x, k], weight[x, 2 + k]], [source[x, k], source[x, 2 + k]])
            for c in range(2):
                ping[x + 4, c * 2 + k, rows, :] = e[c]

    over(0, window, 7, start)

    def step(old, new, left):
        def body(x):
            here = [old[x + 4, n, rows, :] for n in range(4)]
            for k in range(2):
                parts = []
                for c in range(2):
                    n, other = c * 2 + k, c * 2 + 1 - k
                    side = old[x + 4, other, 7 : 7 + groups, :] if k == 0 else old[x + 4, other, 9 : 9 + groups, :]
                    total = (old[x + 3, n, rows, :] + old[x + 5, n, rows, :]) + (here[other] + side)
                    total = total + (pltpu.roll(here[n], 1, 1) + pltpu.roll(here[n], 127, 1))
                    parts.append(source[x, n] + 0.0625 * total)
                moved = product([weight[x, k], weight[x, 2 + k]], parts)
                for c in range(2):
                    new[x + 4, c * 2 + k, rows, :] = (1.0 - OMEGA) * here[c * 2 + k] + moved[c]

        count = min(window, 2 * (3 + left) + 1)
        over(jnp.clip(own - 3 - left, 0, window - count), count, 4, body)

    pairs = (ping, pong)
    for number in range(NC - 1):
        step(pairs[number % 2], pairs[(number + 1) % 2], NC - 2 - number)
    return pairs[(NC - 1) % 2]


def spread_rows(target, top, x, c, tile, block):
    for s in range(2):
        for twice in range(2):
            target[x, c, s, pl.ds(top + 8 * tile + twice, 4, 2), :] = block[s * 4 : s * 4 + 4, :]


def add_two(answer, gx, gy, one, first, count):
    row = lax.broadcasted_iota(jnp.int32, (8, 128), 0)
    for j in range(count):
        x = gx + 4 + (first + j) // 2
        for c in range(2):
            for tile in range(3):
                spot = gy + 7 + tile
                low = jnp.broadcast_to(answer[x, c * 2, pl.ds(spot, 1), :], (8, 128))
                high = jnp.broadcast_to(answer[x, c * 2 + 1, pl.ds(spot, 1), :], (8, 128))
                value = jnp.where(row < 4, low, high)
                at = slice(8 + 8 * tile, 16 + 8 * tile)
                for s in range(2):
                    one[j, c, s, at, :] = one[j, c, s, at, :] + value


def up_kernel(v, planes, groups, second):
    count = 8
    loads = []
    if second:
        loads.append(keep(v, 7, v.in_weight_two, v.weight_two))
    own = v.in_source if second else v.in_source.at[4:12]
    loads += [keep(v, 0, own, v.source.at[4:12]), keep(v, 1, v.in_weight.at[4:12], v.weight.at[4:12]),
              keep(v, 2, v.in_guess, v.guess.at[2:14]), keep(v, 3, v.in_guess_one, v.guess_one),
              keep(v, 4, v.in_source_one, v.source_one), keep(v, 5, v.in_weight_one, v.weight_one)]
    if second:
        loads.append(keep(v, 6, v.in_first, v.first))
        v.matrix[...] = sort_matrix(512, 384, True)
    window = min(planes, WINDOW)
    begin = jnp.clip(v.where[0] - 10, 0, planes - window)
    unpack_two(v.gathered, 0, begin, v.source_two, window, False)
    copies = []
    if second:
        loads.pop(0).wait()
    else:
        unpack_two(v.gathered, 384, begin, v.weight_two, window, True)
        copies.append(keep(v, 7, v.weight_two, v.out_weight_two))
    answer = solve_two(v.where[0] - begin, v.source_two, v.weight_two, v.ping, v.pong, window, planes, groups)
    clear_edges(v.one, count)
    clear_edges(v.one_next, count)
    clear_edges(v.ea, 12, 4)
    clear_edges(v.eb, 11, 5)
    for load in loads:
        load.wait()

    for k in range(4):
        for c in range(2):
            for s in range(2):
                v.one[k + 2, c, s, 16:24, :] = v.guess_one[k + 1, c, s, 16:24, :]
            spread_rows(v.one, 8, k + 2, c, 0, v.from_y_low[k * 2 + c])
            spread_rows(v.one, 8, k + 2, c, 2, v.from_y_high[k * 2 + c])
    for c in range(2):
        for tile in range(3):
            for k in range(2):
                n = (k * 3 + tile) * 2 + c
                spread_rows(v.one, 8, k, c, tile, v.from_low[n])
                spread_rows(v.one, 8, 6 + k, c, tile, v.from_high[n])
    add_two(answer, v.where[0] - begin, v.where[1], v.one, -3, count)
    sweep(v.one, v.one_next, v.weight_one, -1, v.source_one, -1, 1, 7, 2, 2, 0.25)
    sweep(v.one_next, v.one, v.weight_one, -1, v.source_one, -1, 2, 6, 2, 2, 0.25)

    def correct(j, _):
        for half in range(2):
            x = 2 * j + half
            for r in range(4):
                for c in range(2):
                    v.ea[x, c, r, 8:32, :] = v.guess[x, c, r] + v.one[j, c, r // 2, 8:32, :]
        return 0

    lax.fori_loop(2, 6, correct, 0)
    sweep(v.ea, v.eb, v.weight, 0, v.source, 0, 5, 11, 4, 1, 1.0)
    sweep(v.eb, v.ea, v.weight, 0, v.source, 0, 6, 10, 4, 1, 1.0, (16, 24) if second else (8, 32))
    return copies


def up_first_kernel(v, planes, groups):
    copies = up_kernel(v, planes, groups, False)
    for x in range(4):
        for c in range(2):
            for r in range(4):
                v.first[x, c, r] = v.ea[x + 6, c, r, 16:24, :]
                row = slice(c * 4 + r, c * 4 + r + 1)
                v.edges[x, row] = v.ea[x + 6, c, r, 15:16, :]
                v.edges[x + 4, row] = v.ea[x + 6, c, r, 24:25, :]
            put_dense(v, x, c, [v.ea[x + 6, c, r, 16:24, :] for r in range(4)])
    copies.append(keep(v, 8, v.first, v.out_first))
    for copy in copies:
        copy.wait()


def up_second_kernel(v, planes, groups):
    up_kernel(v, planes, groups, True)
    blocks = []
    for c in range(2):
        for x in range(4):
            blocks.append(
                jnp.concatenate([v.first[x, c, r] + v.ea[x + 6, c, r, 16:24, :] for r in range(4)], axis=1)
            )
    values = jnp.concatenate(blocks, axis=0)
    v.result[...] = exact_dot(values, v.matrix[...]).reshape(2, 4, 8, 384)


def up_scratch(planes, groups):
    level = (8, 2, 2, 40, 128)
    two = (min(planes, WINDOW) + 8, 4, 16 + groups, 128)
    source = (min(planes, WINDOW), 4, groups, 128)
    return dict(source=FINE, weight=FINE, guess=FINE, guess_one=COARSE_WIDE, source_one=COARSE, weight_one=COARSE,
                source_two=source, weight_two=source, ping=two, pong=two,
                one=level, one_next=level, ea=WIDE, eb=WIDE, first=(4, 2, 4, 8, 128))


def up_inputs(where, gathered, messages, down, first_down):
    return dict(where=(where, SM), gathered=(gathered, VM), **{name: (array, VM) for name, array in messages.items()},
                in_source=(down.out_source, HB), in_weight=(first_down.out_weight, HB), in_guess=(down.out_guess, HB),
                in_guess_one=(down.out_guess_one, HB), in_source_one=(down.out_source_one, HB),
                in_weight_one=(first_down.out_weight_one, HB))


def up_first(where, gathered, messages, down):
    planes, groups = gathered.shape[0], gathered.shape[1]
    return run(
        "up_first",
        lambda v: up_first_kernel(v, planes, groups),
        up_inputs(where, gathered, messages, down, down),
        dict(packed=((4, 2, 3, 8, 128), VM), front=((3, 2, 3, 8, 128), VM), back=((3, 2, 3, 8, 128), VM),
             edges=((8, 8, 128), VM), out_first=((4, 2, 4, 8, 128), HB), out_weight_two=((min(planes, WINDOW), 4, groups, 128), HB)),
        up_scratch(planes, groups),
        9,
    )


def up_second(where, gathered, messages, down, first_down, first_up):
    planes, groups = gathered.shape[0], gathered.shape[1]
    return run(
        "up_second",
        lambda v: up_second_kernel(v, planes, groups),
        dict(**up_inputs(where, gathered, messages, down, first_down), in_weight_two=(first_up.out_weight_two, HB),
             in_first=(first_up.out_first, HB)),
        dict(result=((2, 4, 8, 384), VM)),
        dict(**up_scratch(planes, groups), matrix=pltpu.VMEM((512, 384), BF16)),
        8,
    ).result


def shifted(block, axis, by):
    count = lax.axis_size(axis)
    pairs = [(i, i + by) for i in range(count) if 0 <= i + by < count]
    return lax.ppermute(block, axis, pairs)


def gather_two(row):
    count_y, count_x = lax.axis_size("gy"), lax.axis_size("gx")
    width = row.shape[1]
    sent = jnp.broadcast_to(row[None], (count_x * count_y, 1, width))
    return lax.all_to_all(sent, ("gx", "gy"), 0, 0).reshape(count_x, count_y, width)


def beside(own):
    return jnp.concatenate(
        [
            shifted(own.back, "gx", 2),
            shifted(own.packed, "gx", 1),
            own.packed,
            shifted(own.packed, "gx", -1),
            shifted(own.front, "gx", -2),
        ]
    )


def surround(mid):
    return mid, shifted(mid, "gy", 1), shifted(mid, "gy", -1)


def exchange_one(down):
    return dict(
        from_y_low=shifted(down.send_y, "gy", 1),
        from_y_high=shifted(down.send_y, "gy", -1),
        from_low=shifted(down.send_up, "gx", 1),
        from_high=shifted(down.send_down, "gx", -1),
    )


def local(right_side, velocity_table, layer_index, absorb_level):
    where = jnp.stack([lax.axis_index("gx"), lax.axis_index("gy")]).astype(jnp.int32)
    packed = pack(velocity_table, right_side, layer_index, absorb_level)
    down = down_first(*surround(beside(packed)), packed.inverse_two)
    middle = up_first(where, gather_two(down.two), exchange_one(down), down)
    rows = jnp.concatenate([beside(middle).reshape(EDGE, 8, 128), middle.edges])
    again = down_second(*surround(rows), down)
    return up_second(where, gather_two(again.two), exchange_one(again), again, down, middle)


def solution(mesh):
    placed = (P(None, "gx", "gy", None), P(), P("gx", "gy", None), P("gx", "gy", None))
    return jax.shard_map(
        local, mesh=mesh, in_specs=placed, out_specs=P(None, "gx", "gy", None), check_vma=False
    )
```
